32 devices in a mesh: wide: 8 (over y, x, core), narrow: 4 (over z).
Axes of the slice: x: 2, y: 2, z: 4, core: 2. Of those that a mesh axis runs over, the one named last changes fastest.
Arguments:
- tokens: bfloat16 [32, 1536, 768], P(('wide', 'narrow')), may hold values from -6 to 6
- lengths: int32 [8, 4], P('wide'), may hold values from 1 to 1536, 4608 in all within a row
- qkv_weight: bfloat16 [768, 3, 768], P(None, None, 'narrow'), may hold values from -0.3125 to 0.3125
- qkv_bias: bfloat16 [3, 768], P(None, 'narrow'), may hold values from -3 to 3
- out_weight: bfloat16 [768, 768], P('narrow'), may hold values from -2.5 to 2.5
- out_bias: bfloat16 [768], replicated, may hold values from -2 to 2
- norm1_gain: bfloat16 [768], replicated, may hold values from 0.099609375 to 1.8984375
- norm1_shift: bfloat16 [768], replicated, may hold values from -2 to 2
- up_weight: bfloat16 [768, 3072], P(None, 'narrow'), may hold values from -0.21875 to 0.21875
- up_bias: bfloat16 [3072], P('narrow'), may hold values from -2 to 2
- down_weight: bfloat16 [3072, 768], P('narrow'), may hold values from -0.109375 to 0.109375
- down_bias: bfloat16 [768], replicated, may hold values from -2 to 2
- norm2_gain: bfloat16 [768], replicated, may hold values from 0.099609375 to 1.8984375
- norm2_shift: bfloat16 [768], replicated, may hold values from -2 to 2
- cotangent: bfloat16 [32, 1536, 768], P(('wide', 'narrow')), may hold values from -6 to 6
Outputs:
- output: bfloat16 [32, 1536, 768], P(('wide', 'narrow'))
- input_grad: float32 [32, 1536, 768], P(('wide', 'narrow'))
- grad_qkv_weight: float32 [768, 3, 768], P(None, None, 'narrow')
- grad_qkv_bias: float32 [3, 768], P(None, 'narrow')
- grad_out_weight: float32 [768, 768], P('narrow')
- grad_out_bias: float32 [768], replicated
- grad_norm1_gain: float32 [768], replicated
- grad_norm1_shift: float32 [768], replicated
- grad_up_weight: float32 [768, 3072], P(None, 'narrow')
- grad_up_bias: float32 [3072], P('narrow')
- grad_down_weight: float32 [3072, 768], P('narrow')
- grad_down_bias: float32 [768], replicated
- grad_norm2_gain: float32 [768], replicated
- grad_norm2_shift: float32 [768], replicated
The draws below stay inside these ranges and needn't reach their ends.
Inputs may be any that keep to these rules, and one draw needn't show every extreme that they name: The 4 lengths of each wide index sum to 4608; positions at or beyond a slot's length are keys that no query attends to.
All inputs are finite; a program needn't handle non-finite values.
Results may differ from the reference program's by a relative error of at most 0.018.
The reference program's roundings to bfloat16 on the way count: a program that leaves them out, or rounds other values in their place, can miss the bound.
Values may be sent and summed in bfloat16 or wider, within the bound.
No kernel may reach another device: no remote copies, remote signals or barrier semaphores. Data moves between devices by JAX's collectives and lax.ppermute only.
A program may use at most 256 MiB of HBM per device.

```python
import math
import jax
import jax.numpy as jnp
import numpy as np
from jax import lax

D = 768
HEADS = 12
HD = 64
FF = 3072
CAP = 1536
SLOTS = 4
BATCH = 32
N_WIDE = 8


def steps_of(rng, shape, split, low, high):
    gain = 1.0
    for axis_at, shards_of in split:
        heights = jax.random.uniform(jax.random.fold_in(jax.random.fold_in(rng, 6), axis_at), (shards_of,), jnp.float32, low / len(split), high / len(split))
        gain = gain * jnp.repeat(jnp.exp(heights), shape[axis_at] // shards_of).reshape((-1,) + (1,) * (len(shape) - 1 - axis_at))
    return gain


def split_up(count, total, limit, lean):
    portions = [(1 << 20) // math.isqrt(rank ** lean) + 1 for rank in range(2, count + 1)]
    surplus, given = total - limit - (count - 1), [1] * (count - 1)
    while surplus > 0:
        movable = [i for i in range(count - 1) if given[i] < limit]
        whole, budget = sum([portions[i] for i in movable]), surplus
        for i in movable:
            extra = min(limit - given[i], max(1, budget * portions[i] // whole), surplus)
            given[i] = given[i] + extra
            surplus = surplus - extra
    return np.array([limit] + given)


def ragged_sizes(own_key, amount, total, limit, slope):
    if amount == 2:
        one = jax.random.randint(own_key, (), max(1, total - limit), min(limit, total - 1) + 1)
        return jnp.stack([one, total - one])
    tallies = jnp.asarray(split_up(amount, total, limit, slope), jnp.int32)
    pairs = (amount - 1) // 2
    source_of, receiver = tallies[1:1 + 2 * pairs:2], tallies[2:2 + 2 * pairs:2]
    slack = jnp.minimum(source_of - 1, limit - receiver)
    shifted = jax.random.randint(jax.random.fold_in(own_key, 1), (pairs,), 0, 1 << 20) % (slack + 1)
    tallies = tallies.at[1:1 + 2 * pairs:2].set(source_of - shifted).at[2:2 + 2 * pairs:2].set(receiver + shifted)
    return tallies[jax.random.permutation(jax.random.fold_in(own_key, 2), amount)]


def bell_draw(key, extent, scale, limit, shards=(), held_as=jnp.bfloat16):
    values = scale * jax.random.normal(key, extent, jnp.float32)
    if shards:
        values = values * steps_of(key, extent, shards, -0.22, 0.18)
    return jnp.clip(values, -limit, limit).astype(held_as)


def setup_inputs(seed: int = 0) -> dict:
    key_list = jax.random.split(jax.random.key(seed), 16)
    tokens = bell_draw(key_list[0], (BATCH, CAP, D), 1.0, 6.0, ((0, 32),))
    lengths = jax.vmap(lambda own: ragged_sizes(own, SLOTS, SLOTS * CAP * 3 // 4, CAP, 2))(jax.random.split(key_list[1], N_WIDE)).reshape((N_WIDE, SLOTS)).astype(jnp.int32)
    qkv_weight = bell_draw(key_list[2], (D, 3, D), (D // 2) ** -0.5, 0.3125, ((2, 4),))
    qkv_bias = bell_draw(key_list[3], (3, D), 0.5, 3.0, ((1, 4),))
    out_weight = bell_draw(key_list[4], (D, D), (max(D // 128, 1)) ** -0.5, 2.5, ((0, 4),))
    out_bias = bell_draw(key_list[5], (D,), 0.3, 2.0)
    norm1_gain = jnp.clip(1.0 + 0.18 * jax.random.normal(key_list[6], (D,), jnp.float32), 0.099609375, 1.8984375).astype(jnp.bfloat16)
    norm1_shift = bell_draw(key_list[7], (D,), 0.3, 2.0)
    up_weight = bell_draw(key_list[8], (D, FF), D ** -0.5, 0.21875, ((1, 4),))
    up_bias = bell_draw(key_list[9], (FF,), 0.3, 2.0, ((0, 4),))
    down_weight = bell_draw(key_list[10], (FF, D), FF ** -0.5, 0.109375, ((0, 4),))
    down_bias = bell_draw(key_list[11], (D,), 0.3, 2.0)
    norm2_gain = jnp.clip(1.0 + 0.18 * jax.random.normal(key_list[12], (D,), jnp.float32), 0.099609375, 1.8984375).astype(jnp.bfloat16)
    norm2_shift = bell_draw(key_list[13], (D,), 0.3, 2.0)
    cotangent = bell_draw(key_list[14], (BATCH, CAP, D), 1.0, 6.0, ((0, 32),))
    return dict(tokens=tokens, lengths=lengths, qkv_weight=qkv_weight, qkv_bias=qkv_bias, out_weight=out_weight, out_bias=out_bias, norm1_gain=norm1_gain, norm1_shift=norm1_shift, up_weight=up_weight, up_bias=up_bias, down_weight=down_weight, down_bias=down_bias, norm2_gain=norm2_gain, norm2_shift=norm2_shift, cotangent=cotangent)


@jax.custom_vjp
def low(v):
    return lax.optimization_barrier(v.astype(jnp.bfloat16)).astype(jnp.float32)

@jax.custom_vjp
def low_back(v):
    return v

def low_keep(v):
    return (low(v), None)

def low_pass(kept, grad):
    return (grad,)

def back_keep(v):
    return (v, None)

def back_low(kept, grad):
    return (low(grad),)
low.defvjp(low_keep, low_pass)
low_back.defvjp(back_keep, back_low)
FULL_PRECISION = lax.Precision.HIGHEST
NORM_EPS = 1e-06
MASK_VALUE = -1000000000.0

def matmul(left, right):
    return jnp.dot(left, right, precision=FULL_PRECISION, preferred_element_type=jnp.float32)

def layer_norm(values, gain_vec, shift_vec):
    row_mean = lax.optimization_barrier(jnp.mean(values, axis=-1, keepdims=True))
    centred = values - row_mean
    inv_std = lax.rsqrt(lax.optimization_barrier(jnp.mean(centred * centred, axis=-1, keepdims=True)) + NORM_EPS)
    return centred * inv_std * gain_vec + shift_vec

def rotate(values, cosine, sine):
    half_dim = values.shape[-1] // 2
    first_half = values[..., :half_dim]
    second_half = values[..., half_dim:]
    return jnp.concatenate([first_half * cosine - second_half * sine, second_half * cosine + first_half * sine], axis=-1)

def rotary_tables(capacity, head_dim):
    positions = jnp.arange(capacity).astype(jnp.float32)
    frequencies = 10000.0 ** (-2.0 * jnp.arange(head_dim // 2).astype(jnp.float32) / head_dim)
    angles = positions[:, None] * frequencies[None, :]
    return (jnp.cos(angles)[:, None, :], jnp.sin(angles)[:, None, :])

def layer(params, slot_tokens, slot_length):
    qkv_weight, qkv_bias, out_weight, out_bias, norm1_gain, norm1_shift, up_weight, up_bias, down_weight, down_bias, norm2_gain, norm2_shift = params
    capacity = slot_tokens.shape[0]
    projected = low_back(jnp.einsum('cd,dje->cje', slot_tokens, qkv_weight, precision=FULL_PRECISION)) + qkv_bias
    cosine, sine = rotary_tables(capacity, HD)
    queries = low(rotate(projected[:, 0].reshape(capacity, HEADS, HD), cosine, sine))
    key_rows = low(rotate(projected[:, 1].reshape(capacity, HEADS, HD), cosine, sine))
    value_rows = low(projected[:, 2].reshape(capacity, HEADS, HD))
    scores = jnp.einsum('qhe,khe->hqk', queries, key_rows, precision=FULL_PRECISION) * HD ** (-0.5)
    live_keys = jnp.arange(capacity) < slot_length
    scores = low_back(jnp.where(live_keys[None, None, :], scores, MASK_VALUE))
    row_max = lax.optimization_barrier(jnp.max(scores, axis=-1, keepdims=True))
    exponentials = jnp.exp(scores - row_max)
    weights = low(exponentials / lax.optimization_barrier(jnp.sum(exponentials, axis=-1, keepdims=True)))
    context = jnp.einsum('hqk,khe->qhe', weights, value_rows, precision=FULL_PRECISION).reshape(capacity, D)
    context = low_back(low(context))
    attended = low_back(matmul(context, out_weight)) + out_bias
    hidden = layer_norm(slot_tokens + attended, norm1_gain, norm1_shift)
    upward = low_back(matmul(low(hidden), up_weight)) + up_bias
    active = low(jax.nn.gelu(upward, approximate=False))
    downward = low_back(matmul(active, down_weight)) + down_bias
    return layer_norm(hidden + downward, norm2_gain, norm2_shift)

def reference(tokens, lengths, qkv_weight, qkv_bias, out_weight, out_bias, norm1_gain, norm1_shift, up_weight, up_bias, down_weight, down_bias, norm2_gain, norm2_shift, cotangent):
    params = tuple((argument.astype(jnp.float32) for argument in (qkv_weight, qkv_bias, out_weight, out_bias, norm1_gain, norm1_shift, up_weight, up_bias, down_weight, down_bias, norm2_gain, norm2_shift)))
    slot_lengths = lengths.reshape(-1)

    def one_slot(totals, inputs):
        slot_tokens, slot_length, slot_cotangent = inputs

        def forward(layer_params, layer_input):
            return layer(layer_params, layer_input, slot_length)
        result, pullback = jax.vjp(forward, params, slot_tokens.astype(jnp.float32))
        param_grads, input_grad = pullback(slot_cotangent.astype(jnp.float32))
        totals = jax.tree.map(jnp.add, totals, param_grads)
        return (totals, (result.astype(jnp.bfloat16), input_grad))
    zero_grads = jax.tree.map(jnp.zeros_like, params)
    totals, (output, input_grad) = lax.scan(one_slot, zero_grads, (tokens, slot_lengths, cotangent))
    return (output, input_grad, totals[0], totals[1], totals[2], totals[3], totals[4], totals[5], totals[6], totals[7], totals[8], totals[9], totals[10], totals[11])
```

```python
import functools
import jax
import jax.numpy as jnp
from jax import lax
from jax.experimental import pallas as pl
from jax.experimental.pallas import tpu as pltpu
from jax.sharding import PartitionSpec as P

bf = jnp.bfloat16
f32 = jnp.float32
LOG2E = 1.4426950408889634
HEADS = 12
HD = 64


def dg(a, b, ca, cb):
    return lax.dot_general(a, b, (((ca,), (cb,)), ((), ())), preferred_element_type=f32)


def mean(x):
    return jnp.mean(x, axis=-1, keepdims=True)


def attn_fwd_kernel(len_ref,tok,w,b,cos,sin,qT,kT,vd,e,ctx,linv,Q2,KD,VA,S,flag,*,C,BQ,KC):
    iq=pl.program_id(1)
    length=len_ref[0,0]
    @pl.when(iq==0)
    def _():
        W=w[...].reshape(3*HD,w.shape[-1])
        p=dg(W,tok[...],1,1)+b[...].reshape(3*HD,1)
        c,s=cos[...],sin[...]
        def rot(x):
            u,v=x[:32],x[32:]
            return jnp.concatenate([u*c-v*s,v*c+u*s],axis=0)
        live=lax.broadcasted_iota(jnp.int32,(HD,C),1)<length
        q=rot(p[:HD]).astype(bf).astype(f32)
        k=jnp.where(live,rot(p[HD:2*HD]),0.0).astype(bf)
        v=jnp.where(live,p[2*HD:],0.0).astype(bf)
        qT[...]=(q*0.125).astype(bf)
        q=q*(0.125*LOG2E)
        hi=q.astype(bf)
        Q2[:HD,:]=hi
        Q2[HD:,:]=(q-hi.astype(f32)).astype(bf)
        kT[...]=k
        KD[...]=jnp.concatenate([k,k],axis=0).T
        vd[...]=jnp.concatenate([v,v],axis=0).T
        VA[:HD,:]=v
        VA[HD:,:]=jnp.where(live[:16],1.0,0.0).astype(bf)
        kf=k.astype(f32)
        qn=jnp.max(jnp.sum(q*q,axis=0,keepdims=True))
        kn=jnp.max(jnp.sum(kf*kf,axis=0,keepdims=True))
        flag[0]=(qn*kn<=1e4).astype(jnp.int32)
    cols=pl.ds(pl.multiple_of(iq*BQ,BQ),BQ)
    nk=C//KC
    def finish(o):
        inv=1.0/o[HD:HD+1]
        linv[...]=inv
        ctx[...]=(o[:HD]*inv).astype(bf)
    @pl.when(flag[0]==1)
    def _():
        qq=Q2[:,cols]
        for j in range(nk):
            r=slice(j*KC,(j+1)*KC)
            e[r,:]=jnp.exp2(dg(KD[r,:],qq,1,0)).astype(bf)
        finish(dg(VA[...],e[...],1,0))
    @pl.when(flag[0]==0)
    def _():
        qq=Q2[:,cols]
        keys=lax.broadcasted_iota(jnp.int32,(C,BQ),0)
        S[...]=jnp.where(keys<length,dg(KD[...],qq,1,0),-1e30)
        m=jnp.max(S[...],axis=0,keepdims=True)
        e[...]=jnp.exp2(S[...]-m).astype(bf)
        finish(dg(VA[...],e[...],1,0))
def attn_fwd(length,tok,w,b,cos,sin,*,BQ=None,KC=128):
    C,D=tok.shape; N,_,G=w.shape[:3]; H=N*G; BQ=BQ or C
    full=lambda h,i:(0,0)
    per=lambda h,i:(h,0,0)
    blk=lambda h,i:(h,0,i)
    grp=lambda h,i:(h//G,0,h%G,0,0)
    return pl.pallas_call(functools.partial(attn_fwd_kernel,C=C,BQ=BQ,KC=KC),
      grid=(H,C//BQ),
      in_specs=[pl.BlockSpec(memory_space=pltpu.SMEM),pl.BlockSpec((C,D),full),
        pl.BlockSpec((None,3,None,HD,D),grp),pl.BlockSpec((None,3,None,HD,1),grp),
        pl.BlockSpec((32,C),full),pl.BlockSpec((32,C),full)],
      out_specs=[pl.BlockSpec((None,HD,C),per),pl.BlockSpec((None,HD,C),per),pl.BlockSpec((None,C,128),per),
        pl.BlockSpec((None,C,BQ),blk),pl.BlockSpec((None,HD,BQ),blk),pl.BlockSpec((None,1,BQ),blk)],
      out_shape=[jax.ShapeDtypeStruct((H,HD,C),bf),jax.ShapeDtypeStruct((H,HD,C),bf),jax.ShapeDtypeStruct((H,C,128),bf),
        jax.ShapeDtypeStruct((H,C,C),bf),jax.ShapeDtypeStruct((H,HD,C),bf),jax.ShapeDtypeStruct((H,1,C),f32)],
      scratch_shapes=[pltpu.VMEM((128,C),bf),pltpu.VMEM((C,128),bf),pltpu.VMEM((80,C),bf),pltpu.VMEM((C,BQ),f32),pltpu.SMEM((1,),jnp.int32)],
      compiler_params=pltpu.CompilerParams(vmem_limit_bytes=60<<20),
      name="attn_fwd")(length,tok,w,b,cos,sin)


def ffn_kernel(tok,cot,ctxT,ow,up,dn,vec,ub,out,act,gu,hl_o,gl_o,g1_o,gol_o,dOT,sm,ubg,G,*,R):
    i=pl.program_id(0)
    @pl.when(i==0)
    def _():
        sm[...]=jnp.zeros_like(sm); ubg[...]=jnp.zeros_like(ubg)
    ob,g1,s1,db,g2,s2=[vec[k:k+1,:] for k in range(6)]
    D=tok.shape[1]; J=up.shape[0]
    def csum(k,x): sm[k:k+1,:]+=jnp.sum(x,axis=0,keepdims=True)
    W=ow[...]
    pre=tok[...].astype(f32)+dg(ctxT[...].reshape(D,R).T,W,1,0)+ob
    cen=pre-mean(pre)
    r1=lax.rsqrt(mean(cen*cen)+1e-6)
    n1=cen*r1
    hid=n1*g1+s1
    hl=hid.astype(bf)
    hl_o[...]=hl
    acc=hid+db
    F=up.shape[2]
    for j in range(J):
        u=dg(hl,up[j],1,0)+ub[j:j+1,:]
        phi=0.5*lax.erf(u*0.7071067811865476)+0.5
        a=(u*phi).astype(bf)
        act[:,j*F:(j+1)*F]=a
        G[:,j*F:(j+1)*F]=phi+u*(jnp.exp2(u*u*-0.7213475204444817)*0.3989422804014327)
        acc=acc+dg(a,dn[j],1,0)
    cen=acc-mean(acc)
    r2=lax.rsqrt(mean(cen*cen)+1e-6)
    n2=cen*r2
    out[...]=(n2*g2+s2).astype(bf)
    c=cot[...].astype(f32)
    csum(0,c*n2); csum(1,c)
    sg=c*g2
    gt=r2*(sg-mean(sg)-n2*mean(sg*n2))
    csum(2,gt)
    gl=gt.astype(bf)
    gl_o[...]=gl
    dh=gt
    for j in range(J):
        g=dg(gl,dn[j],1,1)*G[:,j*F:(j+1)*F]
        ubg[j:j+1,:]+=jnp.sum(g,axis=0,keepdims=True)
        gb=g.astype(bf)
        gu[:,j*F:(j+1)*F]=gb
        dh=dh+dg(gb,up[j],1,1)
    csum(3,dh*n1); csum(4,dh)
    sg=dh*g1
    go=r1*(sg-mean(sg)-n1*mean(sg*n1))
    csum(5,go)
    g1_o[...]=go
    gol=go.astype(bf)
    gol_o[...]=gol
    dOT[...]=dg(W,gol,1,1).astype(bf).reshape(dOT.shape)
def ffn(tok,cot,ctxT,ow,up,dn,vec,ub,*,R=512):
    C,D=tok.shape; J,_,F=up.shape; H,HD,_=ctxT.shape
    row=lambda w: pl.BlockSpec((R,w),lambda i:(i,0))
    fix=lambda a: pl.BlockSpec(a.shape,lambda i:(0,)*a.ndim,pipeline_mode=pl.Buffered(1))
    hb=pl.BlockSpec((H,HD,R),lambda i:(0,0,i))
    acc=lambda s: pl.BlockSpec(s,lambda i:(0,0))
    S=jax.ShapeDtypeStruct
    return pl.pallas_call(functools.partial(ffn_kernel,R=R),grid=(C//R,),
      in_specs=[row(D),row(D),hb,fix(ow),fix(up),fix(dn),fix(vec),fix(ub)],
      out_specs=[row(D),row(J*F),row(J*F),row(D),row(D),row(D),row(D),hb,acc((8,D)),acc((J,F))],
      out_shape=[S((C,D),bf),S((C,J*F),bf),S((C,J*F),bf),S((C,D),bf),S((C,D),bf),S((C,D),f32),S((C,D),bf),S((H,HD,C),bf),S((8,D),f32),S((J,F),f32)],
      scratch_shapes=[pltpu.VMEM((R,J*F),f32)],
      compiler_params=pltpu.CompilerParams(vmem_limit_bytes=63<<20),name="ffn")(tok,cot,ctxT,ow,up,dn,vec,ub)


def attn_bwd_kernel(len_ref,e,vd,dOT,ctxT,linv,qT,kT,cos,sin,gp,gb,D2,DI,DS,DST,ET,*,C,KC,var):
    length=len_ref[0,0]
    do=dOT[...].astype(f32)
    inv=linv[...]
    DI[...]=jnp.sum(do*ctxT[...].astype(f32),axis=0,keepdims=True)*inv
    do=do*inv
    hi=do.astype(bf)
    D2[:HD,:]=hi
    D2[HD:,:]=(do-hi.astype(f32)).astype(bf)
    nk=C//KC
    dk=[];dv=[];dq=None
    for j in range(nk):
        r=slice(j*KC,(j+1)*KC)
        dp=dg(vd[r,:],D2[...],1,0)
        ej=e[r,:]
        ds=(ej.astype(f32)*(dp-DI[...])).astype(bf)
        if var==1:
            DS[r,:]=ds
            DST[:,r]=ds.T
            ET[:,r]=ej.T
        else:
            dk.append(dg(qT[...],ds.T,1,0))
            dv.append(dg(D2[:HD,:],ej.T,1,0))
            q_=dg(kT[:,r],ds,1,0)
            dq=q_ if dq is None else dq+q_
    if var==1:
        dq=dg(kT[...],DS[...],1,0)
        dk=dg(qT[...],DST[...],1,0)
        dv=dg(D2[:HD,:],ET[...],1,0)
    else:
        dk=jnp.concatenate(dk,axis=1); dv=jnp.concatenate(dv,axis=1)
    live=lax.broadcasted_iota(jnp.int32,(HD,C),1)<length
    c,s=cos[...],sin[...]
    def unrot(x):
        u,w=x[:32],x[32:]
        return jnp.concatenate([u*c+w*s,w*c-u*s],axis=0)
    def put(k,x):
        gp[k]=x.astype(bf)
        gb[k]=jnp.sum(x,axis=1,keepdims=True)
    put(0,unrot(dq*0.125))
    put(1,unrot(jnp.where(live,dk,0.0)))
    put(2,jnp.where(live,dv,0.0))
def attn_bwd(length,e,vd,dOT,ctxT,linv,qT,kT,cos,sin,*,KC=256,var=1,G=3):
    H,C,_=e.shape
    per=lambda h:(h,0,0)
    hb=pl.BlockSpec((None,HD,C),per)
    tab=pl.BlockSpec((32,C),lambda h:(0,0))
    grp=lambda h:(h//G,0,h%G,0,0)
    return pl.pallas_call(functools.partial(attn_bwd_kernel,C=C,KC=KC,var=var),grid=(H,),
      in_specs=[pl.BlockSpec(memory_space=pltpu.SMEM),pl.BlockSpec((None,C,C),per),pl.BlockSpec((None,C,128),per),hb,hb,pl.BlockSpec((None,1,C),per),hb,hb,tab,tab],
      out_specs=[pl.BlockSpec((None,3,None,HD,C),grp),pl.BlockSpec((None,3,None,HD,1),grp)],
      out_shape=[jax.ShapeDtypeStruct((H//G,3,G,HD,C),bf),jax.ShapeDtypeStruct((H//G,3,G,HD,1),f32)],
      scratch_shapes=[pltpu.VMEM((128,C),bf),pltpu.VMEM((1,C),f32)]+[pltpu.VMEM((C,C),bf)]*3,
      compiler_params=pltpu.CompilerParams(vmem_limit_bytes=63<<20),name="attn_bwd")(length,e,vd,dOT,ctxT,linv,qT,kT,cos,sin)


def rotary_tables(capacity):
    positions = jnp.arange(capacity).astype(f32)
    frequencies = 10000.0 ** (-2.0 * jnp.arange(HD // 2).astype(f32) / HD)
    angles = frequencies[:, None] * positions[None, :]
    return jnp.cos(angles), jnp.sin(angles)


def gather_all(local):
    wide, narrow = lax.axis_size("wide"), lax.axis_size("narrow")
    rows = local.shape[0] // wide
    piece = lax.dynamic_slice_in_dim(local, lax.axis_index("wide") * rows, rows, 0)
    full = lax.all_gather(piece, ("narrow", "wide"), axis=0, tiled=True)
    return full.reshape((narrow,) + local.shape)


def reduce_all(full):
    part = lax.psum_scatter(full.astype(bf), "wide", scatter_dimension=1, tiled=True)
    part = lax.psum_scatter(part, "narrow", scatter_dimension=0, tiled=True)
    return lax.all_gather(part[0], "wide", axis=0, tiled=True).astype(f32)


def shards(
    tokens, lengths, qkv_weight, qkv_bias, out_weight, out_bias, norm1_gain, norm1_shift,
    up_weight, up_bias, down_weight, down_bias, norm2_gain, norm2_shift, cotangent,
):
    narrow = lax.axis_size("narrow")
    me = lax.axis_index("narrow")
    tok, cot = tokens[0], cotangent[0]
    capacity, width = tok.shape
    heads_here = HEADS // narrow
    length = lax.dynamic_slice(lengths, (0, me), (1, 1))
    cos, sin = rotary_tables(capacity)
    qkv_t = qkv_weight.transpose(1, 2, 0).reshape(3 * heads_here * HD, width)
    wq = gather_all(qkv_t).reshape(narrow, 3, heads_here, HD, width)
    ow = gather_all(out_weight).reshape(HEADS * HD, width)
    up = gather_all(up_weight)
    dn = gather_all(down_weight)
    biases = lax.all_gather(jnp.concatenate([qkv_bias.reshape(-1), up_bias]), "narrow").astype(f32)
    n_qkv = qkv_bias.size
    bq = biases[:, :n_qkv].reshape(narrow, 3, heads_here, HD, 1)
    ub = biases[:, n_qkv:]
    vec = jnp.stack([out_bias, norm1_gain, norm1_shift, down_bias, norm2_gain, norm2_shift]).astype(f32)
    q_t, k_t, v_d, e, ctx_t, linv = attn_fwd(length, tok, wq, bq, cos, sin)
    out, act, gu, hid, g2, g1, g1_low, do_t, small, ub_grad = ffn(tok, cot, ctx_t, ow, up, dn, vec, ub)
    hidden = act.shape[1] // narrow
    dn_grad = dg(act, g2, 0, 0).reshape(narrow, hidden, width)
    up_grad = jnp.stack([dg(hid, gu[:, j * hidden:(j + 1) * hidden], 0, 0) for j in range(narrow)])
    ow_grad = dg(ctx_t.reshape(HEADS * HD, capacity), g1_low, 1, 0).reshape(narrow, heads_here * HD, width)
    gp, gb = attn_bwd(length, e, v_d, do_t, ctx_t, linv, q_t, k_t, cos, sin, G=heads_here)
    gp = gp.reshape(-1, capacity)
    qkv_grad = dg(gp, tok, 1, 0).reshape((narrow,) + qkv_t.shape)
    input_grad = dg(gp, wq.reshape(-1, width), 0, 0) + g1
    packed = jnp.concatenate([small[:6].reshape(-1), ub_grad.reshape(-1), gb.reshape(-1)])
    packed = lax.psum(packed, ("wide", "narrow"))
    small = packed[:6 * width].reshape(6, width)
    ub_grad = lax.dynamic_index_in_dim(packed[6 * width:6 * width + ub_grad.size].reshape(narrow, -1), me, 0, False)
    gb = lax.dynamic_index_in_dim(packed[6 * width + narrow * hidden:].reshape(narrow, 3, -1), me, 0, False)
    dn_grad, up_grad, ow_grad, qkv_grad = [reduce_all(x) for x in (dn_grad, up_grad, ow_grad, qkv_grad)]
    qkv_grad = qkv_grad.reshape(3, heads_here * HD, width).transpose(2, 0, 1)
    return (
        out[None], input_grad[None], qkv_grad, gb, ow_grad, small[5], small[3], small[4],
        up_grad, ub_grad, dn_grad, small[2], small[0], small[1],
    )


def solution(mesh):
    rows = P(("wide", "narrow"), None, None)
    weights = (P(None, None, "narrow"), P(None, "narrow"), P("narrow", None), P(), P(), P(),
               P(None, "narrow"), P("narrow"), P("narrow", None), P(), P(), P())
    return jax.shard_map(
        shards, mesh=mesh, in_specs=(rows, P("wide", None)) + weights + (rows,),
        out_specs=(rows, rows) + weights, check_vma=False,
    )
```

```python
import functools

import jax
import jax.numpy as jnp
from jax import lax
from jax.experimental import pallas as pl
from jax.experimental.pallas import tpu as pltpu
from jax.sharding import PartitionSpec as P

bf = jnp.bfloat16
f32 = jnp.float32
LOG2E = 1.4426950408889634
HEADS = 12
HD = 64
SPLIT = 8
EXTRA = 8
MIB = 1 << 20


def dg(a, b, ca, cb):
    return lax.dot_general(a, b, (((ca,), (cb,)), ((), ())), preferred_element_type=f32)


def mean(x):
    return jnp.mean(x, axis=-1, keepdims=True)


def shape(s, d):
    return jax.ShapeDtypeStruct(s, d)


SMEM = pl.BlockSpec(memory_space=pltpu.SMEM)
ANY = pl.BlockSpec(memory_space=pl.ANY)


def params(mib):
    return pltpu.CompilerParams(vmem_limit_bytes=mib * MIB)


def cost(flops, nbytes):
    return pl.CostEstimate(flops=1, bytes_accessed=1, transcendentals=0)


def put_piece(meta, src, g, lanes, place, dst, sem):
    rel, half, whole = place
    rows = src.shape[1]
    at = 0 if rel is None else (meta[0, 1] ^ rel) * whole + half
    return pltpu.make_async_copy(src.at[g, :, lanes], dst.at[pl.ds(pl.multiple_of(at, 16), rows), :], sem)


def attn_fwd_kernel(meta, *refs, C, KC, G, layout, own):
    pieces, refs = refs[:len(layout)], refs[len(layout):]
    x, b, cos, sin, q_t, k_t, v_d, e, ctx, linv, w_t, *rest = refs
    if own:
        x_t, Q2, KD, VA, S, W, flag, sem = rest
    else:
        x_t, (Q2, KD, VA, S, W, flag, sem) = x, rest
    h = pl.program_id(0)
    length = meta[0, 0]
    groups = pieces[0].shape[0]

    def copies(g):
        return [put_piece(meta, pieces[t], g, slice(None), layout[t], W.at[g], sem.at[g, t]) for t in range(len(pieces))]

    @pl.when(h == 0)
    def _():
        for g in range(groups):
            for c in copies(g):
                c.start()
        if own:
            x_t[...] = x[...].T

    for g in range(groups):
        @pl.when(h == g * G)
        def _(g=g):
            for c in copies(g):
                c.wait()
            w_t[...] = W[g].T

    at = lax.rem(h, G)
    w = jnp.concatenate([w_t[pl.ds(pl.multiple_of((p * G + at) * HD, HD), HD), :] for p in range(3)], axis=0)
    p = dg(w, x_t[...], 1, 0) + b[...].reshape(3 * HD, 1)
    c, s = cos[...], sin[...]

    def rot(v):
        u, z = v[:HD // 2], v[HD // 2:]
        return jnp.concatenate([u * c - z * s, z * c + u * s], axis=0)

    live = lax.broadcasted_iota(jnp.int32, (HD, C), 1) < length
    q = rot(p[:HD]).astype(bf).astype(f32)
    k = jnp.where(live, rot(p[HD:2 * HD]), 0.0).astype(bf)
    v = jnp.where(live, p[2 * HD:], 0.0).astype(bf)
    q_t[...] = (q * 0.125).astype(bf)
    q = q * (0.125 * LOG2E)
    hi = q.astype(bf)
    Q2[:HD, :] = hi
    Q2[HD:, :] = (q - hi.astype(f32)).astype(bf)
    k_t[...] = k
    KD[...] = jnp.concatenate([k, k], axis=0).T
    v_d[...] = jnp.concatenate([v, v], axis=0).T
    VA[:HD, :] = v
    VA[HD:, :] = jnp.where(live[:16], 1.0, 0.0).astype(bf)
    kf = k.astype(f32)
    qn = jnp.max(jnp.sum(q * q, axis=0, keepdims=True))
    kn = jnp.max(jnp.sum(kf * kf, axis=0, keepdims=True))
    flag[0] = (qn * kn <= 1e4).astype(jnp.int32)

    @pl.when(flag[0] == 1)
    def _():
        for j in range(C // KC):
            r = slice(j * KC, (j + 1) * KC)
            e[r, :] = jnp.exp2(dg(KD[r, :], Q2[...], 1, 0)).astype(bf)

    @pl.when(flag[0] == 0)
    def _():
        BQ = S.shape[1]

        def block(i, carry):
            cols = pl.ds(pl.multiple_of(i * BQ, BQ), BQ)
            keys = lax.broadcasted_iota(jnp.int32, (C, BQ), 0)
            S[...] = jnp.where(keys < length, dg(KD[...], Q2[:, cols], 1, 0), -1e30)
            m = jnp.max(S[...], axis=0, keepdims=True)
            e[:, cols] = jnp.exp2(S[...] - m).astype(bf)
            return carry

        lax.fori_loop(0, C // BQ, block, 0)

    o = dg(VA[...], e[...], 1, 0)
    inv = 1.0 / o[HD:HD + 1]
    linv[...] = inv
    ctx[...] = (o[:HD] * inv).astype(bf)


def attn_fwd(meta, pieces, layout, x, b, cos, sin, own):
    groups, _, D = pieces[0].shape
    C = x.shape[0] if own else x.shape[1]
    G = b.shape[2]
    H = groups * G
    per = lambda h: (h, 0, 0)
    fix = lambda a: pl.BlockSpec(a.shape, lambda h: (0,) * a.ndim, pipeline_mode=pl.Buffered(1))
    hb = pl.BlockSpec((None, HD, C), per)
    out_specs = [hb, hb, pl.BlockSpec((None, C, 2 * HD), per), pl.BlockSpec((None, C, C), per), hb,
                 pl.BlockSpec((None, 1, C), per), pl.BlockSpec((None, D, D), lambda h: (h // G, 0, 0))]
    out_shape = [shape((H, HD, C), bf), shape((H, HD, C), bf), shape((H, C, 2 * HD), bf), shape((H, C, C), bf),
                 shape((H, HD, C), bf), shape((H, 1, C), f32), shape((groups, D, D), bf)]
    if own:
        out_specs.append(pl.BlockSpec((D, C), lambda h: (0, 0)))
        out_shape.append(shape((D, C), bf))
    return pl.pallas_call(
        functools.partial(attn_fwd_kernel, C=C, KC=min(128, C), G=G, layout=layout, own=own), grid=(H,),
        in_specs=[SMEM] + [ANY] * len(pieces) + [fix(x), pl.BlockSpec((None, 3, None, HD, 1), lambda h: (h // G, 0, h % G, 0, 0)), fix(cos), fix(sin)],
        out_specs=out_specs, out_shape=out_shape,
        scratch_shapes=[pltpu.VMEM((2 * HD, C), bf), pltpu.VMEM((C, 2 * HD), bf), pltpu.VMEM((HD + 16, C), bf),
                        pltpu.VMEM((C, C // 3 if C % 384 == 0 else C), f32), pltpu.VMEM((groups, D, D), bf), pltpu.SMEM((1,), jnp.int32),
                        pltpu.SemaphoreType.DMA((groups, len(pieces)))],
        compiler_params=params(60), cost_estimate=cost(H * (4 * C * C * 256 + 2 * C * D * 3 * HD), H * C * C * 2 + 8 * MIB),
        name="attn_fwd_own" if own else "attn_fwd",
    )(meta, *pieces, x, b, cos, sin)


def ffn_kernel(meta, u_own, d_own, *refs, R, layout):
    pieces, refs = refs[:len(layout)], refs[len(layout):]
    tok, cot, *refs = refs
    J = pieces[0].shape[0] + 1
    ctxs, ows, refs = refs[:2], refs[2:4], refs[4:]
    (vec, ub, out, act, gu, hid_t, gl_t, g1_o, gol_t, do_t, small, ubg, G, U, Dn, sem) = refs
    i = pl.program_id(0)
    groups = J - 1

    def copies():
        cs = [pltpu.make_async_copy(u_own, U.at[0], sem.at[0, 0, 0]), pltpu.make_async_copy(d_own, Dn.at[0], sem.at[1, 0, 0])]
        for g in range(groups):
            for t, (piece, (parts, place)) in enumerate(zip(pieces, layout)):
                for k, s in enumerate(parts):
                    lanes = slice(k * U.shape[2], (k + 1) * U.shape[2])
                    cs.append(put_piece(meta, piece, g, lanes, place, (U, Dn)[s].at[g + 1], sem.at[s, g + 1, t]))
        return cs

    @pl.when(i == 0)
    def _():
        for c in copies():
            c.start()
        small[...] = jnp.zeros_like(small)
        ubg[...] = jnp.zeros_like(ubg)
        for c in copies():
            c.wait()

    ob, g1, s1, db, g2, s2 = [vec[k:k + 1, :] for k in range(6)]
    D = tok.shape[1]
    F = U.shape[2]

    def csum(k, x):
        small[k:k + 1, :] += jnp.sum(x, axis=0, keepdims=True)

    ow = jnp.concatenate([w[g] for w in ows for g in range(w.shape[0])], axis=0)
    ctx = jnp.concatenate([c[...].reshape(-1, R) for c in ctxs], axis=0)
    pre = tok[...].astype(f32) + dg(ctx.T, ow, 1, 0) + ob
    cen = pre - mean(pre)
    r1 = lax.rsqrt(mean(cen * cen) + 1e-6)
    n1 = cen * r1
    hid = n1 * g1 + s1
    hl = hid.astype(bf)
    hid_t[...] = hl.T
    acc = hid + db
    for j in range(J):
        u = dg(hl, U[j], 1, 0) + ub[j:j + 1, :]
        phi = 0.5 * lax.erf(u * 0.7071067811865476) + 0.5
        a = (u * phi).astype(bf)
        act[:, j * F:(j + 1) * F] = a
        G[:, j * F:(j + 1) * F] = phi + u * (jnp.exp2(u * u * -0.7213475204444817) * 0.3989422804014327)
        acc = acc + dg(a, Dn[j], 1, 0)
    cen = acc - mean(acc)
    r2 = lax.rsqrt(mean(cen * cen) + 1e-6)
    n2 = cen * r2
    out[...] = (n2 * g2 + s2).astype(bf)
    c = cot[...].astype(f32)
    csum(0, c * n2)
    csum(1, c)
    sg = c * g2
    gt = r2 * (sg - mean(sg) - n2 * mean(sg * n2))
    csum(2, gt)
    gl = gt.astype(bf)
    gl_t[...] = gl.T
    dh = gt
    for j in range(J):
        g = dg(gl, Dn[j], 1, 1) * G[:, j * F:(j + 1) * F]
        ubg[j:j + 1, :] += jnp.sum(g, axis=0, keepdims=True)
        gb = g.astype(bf)
        gu[:, j * F:(j + 1) * F] = gb
        dh = dh + dg(gb, U[j], 1, 1)
    csum(3, dh * n1)
    csum(4, dh)
    sg = dh * g1
    go = r1 * (sg - mean(sg) - n1 * mean(sg * n1))
    csum(5, go)
    g1_o[...] = go
    gol = go.astype(bf)
    gol_t[...] = gol.T
    do_t[...] = dg(ow, gol, 1, 1).astype(bf).reshape(do_t.shape)


def ffn(meta, u_own, d_own, pieces, layout, tok, cot, ctxs, wts, vec, ub, R=512):
    C, D = tok.shape
    J, F = ub.shape
    H = HEADS
    row = lambda w: pl.BlockSpec((R, w), lambda i: (i, 0))
    col = pl.BlockSpec((D, R), lambda i: (0, i))
    fix = lambda a: pl.BlockSpec(a.shape, lambda i: (0,) * a.ndim, pipeline_mode=pl.Buffered(1))
    hb = lambda n: pl.BlockSpec((n, HD, R), lambda i: (0, 0, i))
    acc = lambda s: pl.BlockSpec(s, lambda i: (0, 0))
    share = H // J * HD
    at = 3
    owb = lambda w: pl.BlockSpec((w.shape[0], share, D), lambda i: (0, at, 0), pipeline_mode=pl.Buffered(1))
    return pl.pallas_call(
        functools.partial(ffn_kernel, R=R, layout=layout), grid=(C // R,),
        in_specs=[SMEM, ANY, ANY] + [ANY] * len(pieces) + [row(D), row(D)] + [hb(c.shape[0]) for c in ctxs] + [owb(w) for w in wts] + [fix(vec), fix(ub)],
        out_specs=[row(D), row(J * F), row(J * F), col, col, row(D), col, hb(H), acc((8, D)), acc((J, F))],
        out_shape=[shape((C, D), bf), shape((C, J * F), bf), shape((C, J * F), bf), shape((D, C), bf), shape((D, C), bf), shape((C, D), f32),
                   shape((D, C), bf), shape((H, HD, C), bf), shape((8, D), f32), shape((J, F), f32)],
        scratch_shapes=[pltpu.VMEM((R, J * F), f32), pltpu.VMEM((J, D, F), bf), pltpu.VMEM((J, F, D), bf),
                        pltpu.SemaphoreType.DMA((2, J, len(pieces)))],
        compiler_params=params(60), cost_estimate=cost(2 * C * D * (2 * D + 4 * J * F), 60 * MIB), name="ffn",
    )(meta, u_own, d_own, *pieces, tok, cot, *ctxs, *wts, vec, ub)


def attn_bwd_kernel(meta, e, v_d, do_t, ctx, linv, q_t, k_t, cos, sin, gp, gb, D2, DI, DS, DST, ET, *, C, KC):
    length = meta[0, 0]
    g = do_t[...].astype(f32)
    inv = linv[...]
    DI[...] = jnp.sum(g * ctx[...].astype(f32), axis=0, keepdims=True) * inv
    g = g * inv
    hi = g.astype(bf)
    D2[:HD, :] = hi
    D2[HD:, :] = (g - hi.astype(f32)).astype(bf)
    for j in range(C // KC):
        r = slice(j * KC, (j + 1) * KC)
        dp = dg(v_d[r, :], D2[...], 1, 0)
        ej = e[r, :]
        ds = (ej.astype(f32) * (dp - DI[...])).astype(bf)
        DS[r, :] = ds
        DST[:, r] = ds.T
        ET[:, r] = ej.T
    dq = dg(k_t[...], DS[...], 1, 0)
    dk = dg(q_t[...], DST[...], 1, 0)
    dv = dg(D2[:HD, :], ET[...], 1, 0)
    live = lax.broadcasted_iota(jnp.int32, (HD, C), 1) < length
    c, s = cos[...], sin[...]

    def unrot(x):
        u, w = x[:HD // 2], x[HD // 2:]
        return jnp.concatenate([u * c + w * s, w * c - u * s], axis=0)

    def put(k, x):
        gp[k] = x.astype(bf)
        total = jnp.sum(x, axis=1, keepdims=True)
        gb[k:k + 1, :] = jnp.broadcast_to(total, (HD, 2 * HD)).T[:1]

    put(0, unrot(dq * 0.125))
    put(1, unrot(jnp.where(live, dk, 0.0)))
    put(2, jnp.where(live, dv, 0.0))


def attn_bwd(meta, saved, do_t, cos, sin, G, first, shift, H):
    e, v_d, ctx, linv, q_t, k_t = saved
    C = e.shape[1]
    sp = lambda s: pl.BlockSpec((None,) + s, lambda h: (h + first, 0, 0))
    tab = pl.BlockSpec((HD // 2, C), lambda h: (0, 0))
    return pl.pallas_call(
        functools.partial(attn_bwd_kernel, C=C, KC=min(256, C)), grid=(H,),
        in_specs=[SMEM, sp((C, C)), sp((C, 2 * HD)), pl.BlockSpec((None, HD, C), lambda h: (h + first + shift, 0, 0)), sp((HD, C)), sp((1, C)),
                  sp((HD, C)), sp((HD, C)), tab, tab],
        out_specs=[pl.BlockSpec((None, 3, None, HD, C), lambda h: (h // G, 0, h % G, 0, 0)), pl.BlockSpec((None, 3, HD), lambda h: (h, 0, 0))],
        out_shape=[shape((H // G, 3, G, HD, C), bf), shape((H, 3, HD), f32)],
        scratch_shapes=[pltpu.VMEM((2 * HD, C), bf), pltpu.VMEM((1, C), f32)] + [pltpu.VMEM((C, C), bf)] * 3,
        compiler_params=params(60), cost_estimate=cost(H * 8 * C * C * 256, H * C * C * 2 + 16 * MIB), name="attn_bwd",
    )(meta, e, v_d, do_t, ctx, linv, q_t, k_t, cos, sin)


NEAR = (0, 2, 4, 6)
SWAP = (0, 4, 2, 6)


def lay(meta, S, theirs, mine, rows, lanes, order):
    for i, rel in enumerate(order):
        for ref, low in ((mine, 0), (theirs, 1)):
            ref[i // 2, i % 2, 0, rows, lanes] = S[meta[0, 1] ^ (rel | low)].astype(bf)


def wgrad_d_kernel(meta, gl_t, act, vecs, theirs, mine, S):
    rows = S.shape[1]
    S[...] = dg(gl_t[...], act[...], 1, 0).reshape(S.shape)
    lay(meta, S, theirs, mine, slice(0, rows), slice(None), SWAP)
    for i, rel in enumerate(SWAP):
        for ref, low in ((mine, 0), (theirs, 1)):
            line = vecs[pl.ds(meta[0, 1] ^ (rel | low), 1), :]
            ref[i // 2, i % 2, 0, rows:, :] = jnp.broadcast_to(line, (EXTRA, line.shape[1])).astype(bf)


def wgrad_u_kernel(meta, hid_t, gu, gol_t, *refs):
    c0, c1, theirs, mine, S, SO = refs
    F = gu.shape[1]
    S[...] = dg(hid_t[...], gu[...], 1, 0).reshape(S.shape)
    lay(meta, S, theirs, mine, slice(None), slice(0, F), NEAR)

    def out(ctx):
        SO[...] = dg(gol_t[...], ctx[...].reshape(-1, ctx.shape[-1]), 1, 1).reshape(SO.shape)

    pl.when(pl.program_id(0) == 0)(lambda: out(c0))
    pl.when(pl.program_id(0) > 0)(lambda: out(c1))
    lay(meta, SO, theirs, mine, slice(None), slice(F, F + SO.shape[2]), NEAR)


def wgrad_q_kernel(meta, tok_t, gp, gb, theirs, mine, S):
    rows = S.shape[1]
    S[...] = dg(tok_t[...], gp[...], 1, 1).reshape(S.shape)
    lay(meta, S, theirs, mine, slice(0, rows), slice(None), SWAP)
    line = jnp.broadcast_to(gb[...], (EXTRA, gb.shape[1])).astype(bf)
    for i in range(4):
        for ref in (mine, theirs):
            ref[i // 2, i % 2, 0, rows:, :] = line


def wgrad(kernel, meta, args, specs, J, rows, lanes, scratch, name, flops):
    spec = pl.BlockSpec((2, 2, 1, rows, lanes), lambda j: (0, 0, j, 0, 0))
    return pl.pallas_call(
        kernel, grid=(J,), in_specs=[SMEM] + specs, out_specs=[spec] * 2, out_shape=[shape((2, 2, J, rows, lanes), bf)] * 2,
        scratch_shapes=[pltpu.VMEM(s, f32) for s in scratch],
        compiler_params=params(60), cost_estimate=cost(flops, 20 * MIB), name=name,
    )(meta, *args)


def final_du_kernel(meta, x, y, down, up, ow, small, S, SO):
    rows = S.shape[1]
    F = up.shape[1]
    for low, ref in enumerate((x, y)):
        for t, rel in enumerate(NEAR):
            at = meta[0, 1] ^ (rel | low)
            S[at] = ref[t, :rows, :F].astype(f32)
            small[pl.ds(at, 1), :] = ref[t, rows:rows + 1, :F].astype(f32)
            up[pl.ds(pl.multiple_of(at * rows, rows), rows), :] = ref[t, :rows, F:2 * F].astype(f32)
            SO[at] = ref[t, :rows, 2 * F:].astype(f32)
    down[...] = S[...].reshape(down.shape).T
    ow[...] = SO[...].reshape(-1, SO.shape[2]).T


def final_q_kernel(meta, x, y, qkv, gb):
    rows = x.shape[1] - EXTRA
    for low, ref in enumerate((x, y)):
        for t, rel in enumerate(NEAR):
            at = meta[0, 1] ^ (rel | low)
            qkv[pl.ds(pl.multiple_of(at * rows, rows), rows), :] = ref[t, :rows, :].astype(f32)
    gb[...] = x[0, rows:rows + 1, :].astype(f32)


def final(kernel, meta, xs, outs, scratch, name):
    return pl.pallas_call(
        kernel, in_specs=[SMEM] + [pl.BlockSpec(memory_space=pltpu.VMEM)] * 2,
        out_shape=[shape(s, f32) for s in outs], scratch_shapes=[pltpu.VMEM(s, f32) for s in scratch],
        compiler_params=params(60), cost_estimate=cost(0, 8 * MIB), name=name,
    )(meta, *xs)


def input_grad_kernel(*refs, N, n):
    gps, (w0, w1, g1, out) = refs[:n], refs[n:]
    acc = g1[...]
    j = 0
    for gp in gps:
        for i in range(gp.shape[0]):
            w = w0[0, :N, :] if j == 0 else w1[j - 1, :N, :]
            acc = acc + dg(gp[i], w, 0, 0)
            j += 1
    out[...] = acc


def input_grad(gps, w0, w1, g1, R=512):
    _, N, C = gps[0].shape
    D = g1.shape[1]
    fix = lambda a: pl.BlockSpec(a.shape, lambda i: (0,) * a.ndim, pipeline_mode=pl.Buffered(1))
    return pl.pallas_call(
        functools.partial(input_grad_kernel, N=N, n=len(gps)), grid=(C // R,),
        in_specs=[pl.BlockSpec((g.shape[0], N, R), lambda i: (0, 0, i)) for g in gps] + [fix(w0), fix(w1), pl.BlockSpec((R, D), lambda i: (i, 0))],
        out_specs=pl.BlockSpec((R, D), lambda i: (i, 0)), out_shape=shape((C, D), f32),
        compiler_params=params(60), cost_estimate=cost(2 * C * D * D * 3, 24 * MIB), name="input_grad",
    )(*gps, w0, w1, g1)


def fetch(x, s):
    n = lax.axis_size("narrow")
    return lax.ppermute(x, "narrow", [((i + s) % n, i) for i in range(n)])


def give(x, s):
    n = lax.axis_size("narrow")
    return lax.ppermute(x, "narrow", [(i, (i + s) % n) for i in range(n)])


def flip(x, bit):
    return lax.ppermute(x, "wide", [(i, i ^ bit) for i in range(lax.axis_size("wide"))])


def gather(x):
    x = jnp.stack([x] + [flip(x, rel) for rel in NEAR[1:]])
    return x, flip(x, 1)


def total(terms):
    x = terms[0].astype(f32)
    for y in terms[1:]:
        x = x + y.astype(f32)
    return x.astype(bf)


def rest(x):
    bit = SPLIT
    while bit < lax.axis_size("wide"):
        x = add(x, flip(x, bit))
        bit *= 2
    return x


def tie(xs, deps):
    return lax.optimization_barrier((xs, deps))[0]


def add(a, b):
    return (a.astype(f32) + b.astype(f32)).astype(bf)


def rotary_tables(capacity):
    positions = jnp.arange(capacity).astype(f32)
    frequencies = 10000.0 ** (-2.0 * jnp.arange(HD // 2).astype(f32) / HD)
    angles = frequencies[:, None] * positions[None, :]
    return jnp.cos(angles), jnp.sin(angles)


def shards(
    tokens, lengths, qkv_weight, qkv_bias, out_weight, out_bias, norm1_gain, norm1_shift,
    up_weight, up_bias, down_weight, down_bias, norm2_gain, norm2_shift, cotangent,
):
    J = lax.axis_size("narrow")
    tok, cot = tokens[0], cotangent[0]
    C, D = tok.shape
    G = HEADS // J
    N = 3 * G * HD
    F = up_weight.shape[1]
    rows = D // SPLIT
    low = jnp.bitwise_and(lax.axis_index("wide"), SPLIT - 1).astype(jnp.int32)
    length = lax.dynamic_slice(lengths, (0, lax.axis_index("narrow")), (1, 1))
    meta = jnp.concatenate([length, low.reshape(1, 1)], axis=1)
    cos, sin = rotary_tables(C)

    qo = jnp.concatenate([qkv_weight.reshape(D, N), out_weight.T], axis=1)
    bias = jnp.concatenate([qkv_bias.reshape(-1), up_bias])
    bias = jnp.pad(bias, (0, 2 * D - bias.size)).reshape(2, D)
    cut = lambda x: lax.dynamic_slice_in_dim(x, low * rows, rows, 0)
    q_piece = jnp.concatenate([cut(qo), jnp.pad(bias, ((0, EXTRA - 2), (0, 0)))], axis=0)
    got = [fetch(q_piece, s) for s in range(1, J)]
    vec = jnp.stack([out_bias, norm1_gain, norm1_shift, down_bias, norm2_gain, norm2_shift]).astype(f32)
    b_own = qkv_bias.astype(f32).reshape(1, 3, G, HD, 1)
    ud_piece = jnp.concatenate([cut(up_weight), cut(down_weight)], axis=1)
    ud_got = [fetch(tie(ud_piece, q_piece), 1)]
    q0, k0, v0, e0, c0, l0, wt0, tok_t = attn_fwd(meta, [qo[None]], ((None, 0, 0),), tok, b_own, cos, sin, True)
    got, ud_got, tok_t = lax.optimization_barrier((got, ud_got, tok_t))
    biases = jnp.stack([bias] + [x[rows:rows + 2] for x in got]).reshape(J, 2 * D).astype(f32)
    bq, ub = biases[1:, :N].reshape(J - 1, 3, G, HD, 1), biases[:, N:N + F]
    q = jnp.stack([x[:rows] for x in got])
    q_x, q_y = flip(q, 2), flip(q, 4)
    ud_2 = fetch(tie(ud_piece, got), 2)
    h = rows // 2
    q_x, q_y, ud_2 = lax.optimization_barrier((q_x, q_y, ud_2))
    q_d = [flip(q_y[:, :h], 2), flip(q_x[:, h:], 4)]
    q_far = [flip(x, 1) for x in (q, q_x, q_y)]
    ud_3 = fetch(tie(ud_piece, q_x), 3)
    q_d, ud_3 = lax.optimization_barrier((q_d, ud_3))
    q_far = q_far + [flip(x, 1) for x in q_d]
    q_pieces = [q, q_x, q_y] + q_d + q_far
    q_places = tuple((rel | low, half, rows) for low in (0, 1) for rel, half in ((0, 0), (2, 0), (4, 0), (6, 0), (6, h)))
    ud = jnp.stack(ud_got + [ud_2, ud_3])
    ud_near = [flip(ud, rel) for rel in NEAR[1:]]
    ud_far = [flip(ud, 1)]
    tok_t = tie(tok_t, ud)
    q1, k1, v1, e1, c1, l1, wt1 = attn_fwd(meta, q_pieces, q_places, tok_t, bq, cos, sin, False)
    ud_near, ud_far, c1 = lax.optimization_barrier((ud_near, ud_far, c1))
    ud_pieces = [ud] + ud_near + ud_far + [flip(x, 1) for x in ud_near]
    ud_places = [(rel | low, 0, rows) for low in (0, 1) for rel in NEAR]
    ud_layout = tuple(((0, 1), place) for place in ud_places)
    out, act, gu, hid_t, gl_t, g1, gol_t, do_t, small, ubg = ffn(
        meta, up_weight, down_weight, ud_pieces, ud_layout, tok, cot, (c0, c1), (wt0, wt1), vec, ub)

    whole = lambda a: pl.BlockSpec(a.shape, lambda j: (0,) * a.ndim, pipeline_mode=pl.Buffered(1))
    vecs = jnp.concatenate([jnp.broadcast_to(small[None, :6], (J, 6, D)), ubg[:, None], jnp.zeros((J, 1, D), f32)], axis=1)
    u_t, u_m = wgrad(
        wgrad_u_kernel, meta, (hid_t, gu, gol_t, c0, c1),
        [whole(hid_t), pl.BlockSpec((C, F), lambda j: (0, j)), whole(gol_t), pl.BlockSpec((G, HD, C), lambda j: (0, 0, 0)),
         pl.BlockSpec((G, HD, C), lambda j: (jnp.maximum(j - 1, 0), 0, 0))],
        J, rows, F + G * HD, [(SPLIT, rows, F), (SPLIT, rows, G * HD)], "wgrad_u", 2 * C * D * (J * F + D))
    u_1 = flip(u_t, 1)
    gl_t = tie(gl_t, u_t)
    d_t, d_m = wgrad(
        wgrad_d_kernel, meta, (gl_t, act, vecs),
        [whole(gl_t), pl.BlockSpec((C, F), lambda j: (0, j)), pl.BlockSpec((None, 8, D), lambda j: (j, 0, 0))],
        J, rows + EXTRA, F, [(SPLIT, rows, F)], "wgrad_d", 2 * C * D * J * F)

    def grad_q(gp, gb):
        n = gp.shape[0]
        return wgrad(
            wgrad_q_kernel, meta, (tok_t, gp, gb),
            [whole(tok_t), pl.BlockSpec((None, N, C), lambda j: (j, 0, 0)), pl.BlockSpec((None, 1, N), lambda j: (j, 0, 0))],
            n, rows + EXTRA, N, [(SPLIT, rows, N)], "wgrad_q", 2 * C * D * n * N)

    def backward(group, count, do_t):
        saved, shift = ((e0, v0, c0, l0, q0, k0), 0) if group == 0 else ((e1, v1, c1, l1, q1, k1), G)
        gp, gb = attn_bwd(meta, saved, do_t, cos, sin, G, group * G - shift, shift, count * G)
        return gp.reshape(count, N, C), gb.reshape(count, G, 3, HD).transpose(0, 2, 1, 3).reshape(count, 1, N)

    def halves(mine, got):
        return add(mine[0], got[0]), add(mine[1], got[1])

    u_1, u_m, d_t = lax.optimization_barrier((u_1, u_m, d_t))
    d_1 = flip(d_t, 1)
    u_k, u_s = halves(u_m, u_1)
    u_2 = flip(u_s, 4)
    do_t = tie(do_t, u_s)
    d_1, d_m, do_t = lax.optimization_barrier((d_1, d_m, do_t))
    d_k, d_s = halves(d_m, d_1)
    d_2 = flip(d_s, 2)
    do_t = tie(do_t, d_s)
    gpa, gba = backward(1, 2, do_t)
    u_2, d_2, gpa, do_t = lax.optimization_barrier((u_2, d_2, gpa, do_t))
    u_k, u_s = halves(u_k, u_2)
    u_3 = flip(u_s, 2)
    d_k, d_s = halves(d_k, d_2)
    d_3 = flip(d_s, 4)
    gpa_ = tie(gpa, (u_s, d_s))
    qa_t, qa_m = grad_q(gpa_, gba)
    qa_1 = flip(qa_t, 1)
    do_t = tie(do_t, qa_t)
    gpb, gbb = backward(0, 1, do_t)
    u_3, d_3, qa_1, gpb, do_t = lax.optimization_barrier((u_3, d_3, qa_1, gpb, do_t))
    du_s = [jnp.concatenate([add(d_k[j], d_3[j]), jnp.pad(add(u_k[j], u_3[j]), ((0, EXTRA), (0, 0)))], axis=1) for j in range(J)]
    du_3 = [give(du_s[s], s) for s in (1, 3)]
    qa_k, qa_s = halves(qa_m, qa_1)
    qa_2 = flip(qa_s, 2)
    do_t = tie(do_t, (du_s, qa_s))
    gpc, gbc = backward(3, 1, do_t)
    du_3, qa_2, gpb, gpc = lax.optimization_barrier((du_3, qa_2, gpb, gpc))
    du_3.append(give(tie(du_s[2], gpc), 2))
    qa_k, qa_s = halves(qa_k, qa_2)
    qa_3 = flip(qa_s, 4)
    gbc_ = jnp.stack([gpb[0], gpc[0]])
    gbc_ = tie(gbc_, (qa_s, qa_k))
    qb_t, qb_m = grad_q(gbc_, jnp.concatenate([gbb, gbc], axis=0))
    qb_1 = flip(qb_t, 1)
    qa_3, du_3, qb_m, qb_1 = lax.optimization_barrier((qa_3, du_3, qb_m, qb_1))
    qa_s = [add(qa_k[j], qa_3[j]) for j in range(2)]
    q_3 = [give(qa_s[0], 1), give(qa_s[1], 2)]
    du = rest(total([du_s[0]] + du_3))
    du_4 = [flip(du, rel) for rel in NEAR[1:]]
    qb_k, qb_s = halves(qb_m, qb_1)
    qb_2 = flip(qb_s, 2)
    g1 = tie(g1, (qb_k, qb_s, du, qa_s))
    x_grad = input_grad([gpb, gpa, gpc], wt0, wt1, g1)
    qb_2, qb_k, du_4, q_3 = tie((qb_2, qb_k, du_4, q_3), x_grad)
    qb_k, qb_s = halves(qb_k, qb_2)
    qb_3 = flip(qb_s, 4)
    du = jnp.stack([du] + du_4)
    du_5 = flip(du, 1)
    qb_3, du_5 = lax.optimization_barrier((qb_3, du_5))
    q_3 = [add(qb_k[0], qb_3[0])] + q_3 + [give(add(qb_k[1], qb_3[1]), J - 1)]
    q_sum = gather(rest(total(q_3)))
    down_g, up_g, ow_g, small = final(
        final_du_kernel, meta, (du, du_5), [(F, D), (D, F), (G * HD, D), (8, D)], [(SPLIT, rows, F), (SPLIT, rows, G * HD)], "final_du")
    qkv_g, gb = final(final_q_kernel, meta, q_sum, [(D, N), (1, N)], [], "final_q")
    return (
        out[None], x_grad[None], qkv_g.reshape(D, 3, G * HD), gb.reshape(3, G * HD), ow_g, small[5], small[3], small[4],
        up_g, small[6], down_g, small[2], small[0], small[1],
    )


def solution(mesh):
    rows = P(("wide", "narrow"), None, None)
    weights = (P(None, None, "narrow"), P(None, "narrow"), P("narrow", None), P(), P(), P(),
               P(None, "narrow"), P("narrow"), P("narrow", None), P(), P(), P())
    return jax.shard_map(
        shards, mesh=mesh, in_specs=(rows, P("wide", None)) + weights + (rows,),
        out_specs=(rows, rows) + weights, check_vma=False,
    )
```

```python
import functools

import jax
import jax.numpy as jnp
from jax import lax
from jax.experimental import pallas as pl
from jax.experimental.pallas import tpu as pltpu
from jax.sharding import PartitionSpec as P

bf = jnp.bfloat16
f32 = jnp.float32
LOG2E = 1.4426950408889634
HEADS = 12
HD = 64
SPLIT = 8
EXTRA = 8
MIB = 1 << 20


def dg(a, b, ca, cb):
    return lax.dot_general(a, b, (((ca,), (cb,)), ((), ())), preferred_element_type=f32)


def mean(x):
    return jnp.mean(x, axis=-1, keepdims=True)


def shape(s, d):
    return jax.ShapeDtypeStruct(s, d)


SMEM = pl.BlockSpec(memory_space=pltpu.SMEM)
ANY = pl.BlockSpec(memory_space=pl.ANY)


def length_of(lengths):
    return lengths[0, lax.axis_index("narrow")]


def low_bits():
    return jnp.bitwise_and(lax.axis_index("wide"), SPLIT - 1)


def params(mib):
    return pltpu.CompilerParams(vmem_limit_bytes=mib * MIB)


def cost(flops, nbytes):
    return pl.CostEstimate(flops=1, bytes_accessed=1, transcendentals=0)


def put_piece(meta, src, g, lanes, place, dst, sem):
    rel, half, whole = place
    rows = src.shape[1]
    at = 0 if rel is None else (low_bits() ^ rel) * whole + half
    return pltpu.make_async_copy(src.at[g, :, lanes], dst.at[pl.ds(pl.multiple_of(at, 16), rows), :], sem)


def attn_fwd_kernel(meta, *refs, C, KC, G, layout, own):
    pieces, refs = refs[:len(layout)], refs[len(layout):]
    x, b, cos, sin, q_t, k_t, v_d, e, ctx, linv, w_t, *rest = refs
    if own:
        x_t, Q2, KD, VA, S, W, flag, sem = rest
    else:
        x_t, (Q2, KD, VA, S, W, flag, sem) = x, rest
    s = pl.program_id(0)
    last = pl.num_programs(0) - 1
    length = length_of(meta)
    now, then = lax.rem(s, 2), 1 - lax.rem(s, 2)

    if own:
        @pl.when(s == 0)
        def _():
            x_t[...] = x[...].T
            n = pieces[0].shape[0]
            w_t[:n, :] = pieces[0][...]
            w_t[n:, :] = pieces[1][...]
    else:
        groups = pieces[0].shape[0]

        def copies(g):
            return [put_piece(meta, pieces[t], g, slice(None), layout[t], W.at[g], sem.at[g, t]) for t in range(len(pieces))]

        @pl.when(s == 0)
        def _():
            for g in range(groups):
                for c in copies(g):
                    c.start()

        for g in range(groups):
            @pl.when(s == g * G)
            def _(g=g):
                for c in copies(g):
                    c.wait()
                w_t[...] = W[g].T

    def project():
        at = lax.rem(s, G)
        w = jnp.concatenate([w_t[pl.ds(pl.multiple_of((p * G + at) * HD, HD), HD), :] for p in range(3)], axis=0)
        p = dg(w, x_t[...], 1, 0) + b[...].reshape(3 * HD, 1)
        c, d = cos[...], sin[...]

        def rot(v):
            u, z = v[:HD // 2], v[HD // 2:]
            return jnp.concatenate([u * c - z * d, z * c + u * d], axis=0)

        live = lax.broadcasted_iota(jnp.int32, (HD, C), 1) < length
        q = rot(p[:HD]).astype(bf).astype(f32)
        k = jnp.where(live, rot(p[HD:2 * HD]), 0.0).astype(bf)
        v = jnp.where(live, p[2 * HD:], 0.0).astype(bf)
        q_t[...] = (q * 0.125).astype(bf)
        q = q * (0.125 * LOG2E)
        hi = q.astype(bf)
        Q2[now, :HD, :] = hi
        Q2[now, HD:, :] = (q - hi.astype(f32)).astype(bf)
        k_t[...] = k
        KD[now] = jnp.concatenate([k, k], axis=0).T
        v_d[...] = jnp.concatenate([v, v], axis=0).T
        VA[now, :HD, :] = v
        VA[now, HD:, :] = jnp.where(live[:16], 1.0, 0.0).astype(bf)
        kf = k.astype(f32)
        qn = jnp.max(jnp.sum(q * q, axis=0, keepdims=True))
        kn = jnp.max(jnp.sum(kf * kf, axis=0, keepdims=True))
        flag[now] = (qn * kn <= 1e4).astype(jnp.int32)

    def attend():
        o = dg(VA[then], e[...], 1, 0)
        inv = 1.0 / o[HD:HD + 1]
        linv[...] = inv
        ctx[...] = (o[:HD] * inv).astype(bf)

    def plain():
        for j in range(C // KC):
            r = slice(j * KC, (j + 1) * KC)
            e[r, :] = jnp.exp2(dg(KD[then, r, :], Q2[then], 1, 0)).astype(bf)
        attend()

    def shifted():
        BQ = S.shape[1]

        def block(i, carry):
            cols = pl.ds(pl.multiple_of(i * BQ, BQ), BQ)
            keys = lax.broadcasted_iota(jnp.int32, (C, BQ), 0)
            S[...] = jnp.where(keys < length, dg(KD[then], Q2[then, :, cols], 1, 0), -1e30)
            m = jnp.max(S[...], axis=0, keepdims=True)
            e[:, cols] = jnp.exp2(S[...] - m).astype(bf)
            return carry

        lax.fori_loop(0, C // BQ, block, 0)
        attend()

    fits = flag[then] == 1

    @pl.when(s == 0)
    def _():
        project()

    @pl.when((s > 0) & (s < last) & fits)
    def _():
        plain()
        project()

    @pl.when((s == last) & fits)
    def _():
        plain()

    @pl.when((s > 0) & jnp.logical_not(fits))
    def _():
        shifted()

    @pl.when((s > 0) & (s < last) & jnp.logical_not(fits))
    def _():
        project()


def attn_fwd(meta, pieces, layout, x, b, cos, sin, own):
    groups, _, D = pieces[0].shape if not own else (1,) + pieces[0].shape
    C = x.shape[0] if own else x.shape[1]
    G = b.shape[2]
    H = groups * G
    cur = lambda s: jnp.minimum(s, H - 1)
    at = lambda s: (cur(s), 0, 0)
    was = lambda s: (jnp.maximum(s - 1, 0), 0, 0)
    fix = lambda a: pl.BlockSpec(a.shape, lambda s: (0,) * a.ndim, pipeline_mode=pl.Buffered(1))
    hb = lambda i: pl.BlockSpec((None, HD, C), i)
    out_specs = [hb(at), hb(at), pl.BlockSpec((None, C, 2 * HD), at), pl.BlockSpec((None, C, C), was), hb(was),
                 pl.BlockSpec((None, 1, C), was), pl.BlockSpec((None, D, D), lambda s: (cur(s) // G, 0, 0))]
    out_shape = [shape((H, HD, C), bf), shape((H, HD, C), bf), shape((H, C, 2 * HD), bf), shape((H, C, C), bf),
                 shape((H, HD, C), bf), shape((H, 1, C), f32), shape((groups, D, D), bf)]
    if own:
        out_specs.append(pl.BlockSpec((D, C), lambda s: (0, 0)))
        out_shape.append(shape((D, C), bf))
    return pl.pallas_call(
        functools.partial(attn_fwd_kernel, C=C, KC=min(128, C), G=G, layout=layout, own=own), grid=(H + 1,),
        in_specs=[SMEM] + ([fix(p) for p in pieces] if own else [ANY] * len(pieces))
        + [fix(x), pl.BlockSpec((None, 3, None, HD, 1), lambda s: (cur(s) // G, 0, cur(s) % G, 0, 0)), fix(cos), fix(sin)],
        out_specs=out_specs, out_shape=out_shape,
        scratch_shapes=[pltpu.VMEM((2, 2 * HD, C), bf), pltpu.VMEM((2, C, 2 * HD), bf), pltpu.VMEM((2, HD + 16, C), bf),
                        pltpu.VMEM((C, C // 3 if C % 384 == 0 else C), f32), pltpu.VMEM((8, 128) if own else (groups, D, D), bf),
                        pltpu.SMEM((2,), jnp.int32), pltpu.SemaphoreType.DMA((groups, len(pieces)))],
        compiler_params=params(60), cost_estimate=cost(H * (4 * C * C * 256 + 2 * C * D * 3 * HD), H * C * C * 2 + 8 * MIB),
        name="attn_fwd_own" if own else "attn_fwd",
    )(meta, *pieces, x, b, cos, sin)


def ffn_kernel(meta, u_own, d_own, *refs, R, layout):
    pieces, refs = refs[:len(layout)], refs[len(layout):]
    tok, cot, *refs = refs
    J = pieces[0].shape[0] + 1
    ctxs, ows, refs = refs[:2], refs[2:4], refs[4:]
    (vec, ub, out, act, gu, hid_t, gl_t, g1_o, gol_t, do_t, small, ubg, G, U, Dn, sem) = refs
    i = pl.program_id(0)
    groups = J - 1

    def copies():
        cs = [pltpu.make_async_copy(u_own, U.at[0], sem.at[0, 0, 0]), pltpu.make_async_copy(d_own, Dn.at[0], sem.at[1, 0, 0])]
        for g in range(groups):
            for t, (piece, (parts, place)) in enumerate(zip(pieces, layout)):
                for k, s in enumerate(parts):
                    lanes = slice(k * U.shape[2], (k + 1) * U.shape[2])
                    cs.append(put_piece(meta, piece, g, lanes, place, (U, Dn)[s].at[g + 1], sem.at[s, g + 1, t]))
        return cs

    @pl.when(i == 0)
    def _():
        for c in copies():
            c.start()
        small[...] = jnp.zeros_like(small)
        ubg[...] = jnp.zeros_like(ubg)

    ob, g1, s1, db, g2, s2 = [vec[k:k + 1, :] for k in range(6)]
    D = tok.shape[1]
    F = U.shape[2]

    def csum(k, x):
        small[k:k + 1, :] += jnp.sum(x, axis=0, keepdims=True)

    ow = jnp.concatenate([w[g] for w in ows for g in range(w.shape[0])], axis=0)
    ctx = jnp.concatenate([c[...].reshape(-1, R) for c in ctxs], axis=0)
    pre = tok[...].astype(f32) + dg(ctx.T, ow, 1, 0) + ob
    cen = pre - mean(pre)
    r1 = lax.rsqrt(mean(cen * cen) + 1e-6)
    n1 = cen * r1
    hid = n1 * g1 + s1
    hl = hid.astype(bf)
    hid_t[...] = hl.T
    acc = hid + db

    @pl.when(i == 0)
    def _():
        for c in copies():
            c.wait()

    for j in range(J):
        u = dg(hl, U[j], 1, 0) + ub[j:j + 1, :]
        phi = 0.5 * lax.erf(u * 0.7071067811865476) + 0.5
        a = (u * phi).astype(bf)
        act[:, j * F:(j + 1) * F] = a
        G[:, j * F:(j + 1) * F] = phi + u * (jnp.exp2(u * u * -0.7213475204444817) * 0.3989422804014327)
        acc = acc + dg(a, Dn[j], 1, 0)
    cen = acc - mean(acc)
    r2 = lax.rsqrt(mean(cen * cen) + 1e-6)
    n2 = cen * r2
    out[...] = (n2 * g2 + s2).astype(bf)
    c = cot[...].astype(f32)
    csum(0, c * n2)
    csum(1, c)
    sg = c * g2
    gt = r2 * (sg - mean(sg) - n2 * mean(sg * n2))
    csum(2, gt)
    gl = gt.astype(bf)
    gl_t[...] = gl.T
    dh = gt
    for j in range(J):
        g = dg(gl, Dn[j], 1, 1) * G[:, j * F:(j + 1) * F]
        ubg[j:j + 1, :] += jnp.sum(g, axis=0, keepdims=True)
        gb = g.astype(bf)
        gu[:, j * F:(j + 1) * F] = gb
        dh = dh + dg(gb, U[j], 1, 1)
    csum(3, dh * n1)
    csum(4, dh)
    sg = dh * g1
    go = r1 * (sg - mean(sg) - n1 * mean(sg * n1))
    csum(5, go)
    g1_o[...] = go
    gol = go.astype(bf)
    gol_t[...] = gol.T
    do_t[...] = dg(ow, gol, 1, 1).astype(bf).reshape(do_t.shape)


def ffn(meta, u_own, d_own, pieces, layout, tok, cot, ctxs, wts, vec, ub, R=512):
    C, D = tok.shape
    J, F = ub.shape
    H = HEADS
    row = lambda w: pl.BlockSpec((R, w), lambda i: (i, 0))
    col = pl.BlockSpec((D, R), lambda i: (0, i))
    fix = lambda a: pl.BlockSpec(a.shape, lambda i: (0,) * a.ndim, pipeline_mode=pl.Buffered(1))
    hb = lambda n: pl.BlockSpec((n, HD, R), lambda i: (0, 0, i))
    acc = lambda s: pl.BlockSpec(s, lambda i: (0, 0))
    share = H // J * HD
    at = 3
    owb = lambda w: pl.BlockSpec((w.shape[0], share, D), lambda i: (0, at, 0), pipeline_mode=pl.Buffered(1))
    return pl.pallas_call(
        functools.partial(ffn_kernel, R=R, layout=layout), grid=(C // R,),
        in_specs=[SMEM, ANY, ANY] + [ANY] * len(pieces) + [row(D), row(D)] + [hb(c.shape[0]) for c in ctxs] + [owb(w) for w in wts] + [fix(vec), fix(ub)],
        out_specs=[row(D), row(J * F), row(J * F), col, col, row(D), col, hb(H), acc((8, D)), acc((J, F))],
        out_shape=[shape((C, D), bf), shape((C, J * F), bf), shape((C, J * F), bf), shape((D, C), bf), shape((D, C), bf), shape((C, D), f32),
                   shape((D, C), bf), shape((H, HD, C), bf), shape((8, D), f32), shape((J, F), f32)],
        scratch_shapes=[pltpu.VMEM((R, J * F), f32), pltpu.VMEM((J, D, F), bf), pltpu.VMEM((J, F, D), bf),
                        pltpu.SemaphoreType.DMA((2, J, len(pieces)))],
        compiler_params=params(60), cost_estimate=cost(2 * C * D * (2 * D + 4 * J * F), 60 * MIB), name="ffn",
    )(meta, u_own, d_own, *pieces, tok, cot, *ctxs, *wts, vec, ub)


def attn_bwd_kernel(meta, e, v_d, do_t, ctx, linv, q_t, k_t, cos, sin, gp, gb, D2, DI, DS, DST, ET, *, C, KC):
    length = length_of(meta)
    g = do_t[...].astype(f32)
    inv = linv[...]
    DI[...] = jnp.sum(g * ctx[...].astype(f32), axis=0, keepdims=True) * inv
    g = g * inv
    hi = g.astype(bf)
    D2[:HD, :] = hi
    D2[HD:, :] = (g - hi.astype(f32)).astype(bf)
    for j in range(C // KC):
        r = slice(j * KC, (j + 1) * KC)
        dp = dg(v_d[r, :], D2[...], 1, 0)
        ej = e[r, :]
        ds = (ej.astype(f32) * (dp - DI[...])).astype(bf)
        DS[r, :] = ds
        DST[:, r] = ds.T
        ET[:, r] = ej.T
    dq = dg(k_t[...], DS[...], 1, 0)
    dk = dg(q_t[...], DST[...], 1, 0)
    dv = dg(D2[:HD, :], ET[...], 1, 0)
    live = lax.broadcasted_iota(jnp.int32, (HD, C), 1) < length
    c, s = cos[...], sin[...]

    def unrot(x):
        u, w = x[:HD // 2], x[HD // 2:]
        return jnp.concatenate([u * c + w * s, w * c - u * s], axis=0)

    def put(k, x):
        gp[k] = x.astype(bf)
        total = jnp.sum(x, axis=1, keepdims=True)
        gb[k:k + 1, :] = jnp.broadcast_to(total, (HD, 2 * HD)).T[:1]

    put(0, unrot(dq * 0.125))
    put(1, unrot(jnp.where(live, dk, 0.0)))
    put(2, jnp.where(live, dv, 0.0))


def attn_bwd(meta, saved, do_t, cos, sin, G, first, shift, H):
    e, v_d, ctx, linv, q_t, k_t = saved
    C = e.shape[1]
    sp = lambda s: pl.BlockSpec((None,) + s, lambda h: (h + first, 0, 0))
    tab = pl.BlockSpec((HD // 2, C), lambda h: (0, 0))
    return pl.pallas_call(
        functools.partial(attn_bwd_kernel, C=C, KC=min(256, C)), grid=(H,),
        in_specs=[SMEM, sp((C, C)), sp((C, 2 * HD)), pl.BlockSpec((None, HD, C), lambda h: (h + first + shift, 0, 0)), sp((HD, C)), sp((1, C)),
                  sp((HD, C)), sp((HD, C)), tab, tab],
        out_specs=[pl.BlockSpec((None, 3, None, HD, C), lambda h: (h // G, 0, h % G, 0, 0)), pl.BlockSpec((None, 3, HD), lambda h: (h, 0, 0))],
        out_shape=[shape((H // G, 3, G, HD, C), bf), shape((H, 3, HD), f32)],
        scratch_shapes=[pltpu.VMEM((2 * HD, C), bf), pltpu.VMEM((1, C), f32)] + [pltpu.VMEM((C, C), bf)] * 3,
        compiler_params=params(60), cost_estimate=cost(H * 8 * C * C * 256, H * C * C * 2 + 16 * MIB), name="attn_bwd",
    )(meta, e, v_d, do_t, ctx, linv, q_t, k_t, cos, sin)


NEAR = (0, 2, 4, 6)
SWAP = (0, 4, 2, 6)


def lay(meta, S, theirs, mine, rows, lanes, order):
    for i, rel in enumerate(order):
        for ref, low in ((mine, 0), (theirs, 1)):
            ref[i // 2, i % 2, 0, rows, lanes] = S[low_bits() ^ (rel | low)].astype(bf)


def wgrad_d_kernel(meta, gl_t, act, vecs, theirs, mine, S):
    rows = S.shape[1]
    S[...] = dg(gl_t[...], act[...], 1, 0).reshape(S.shape)
    lay(meta, S, theirs, mine, slice(0, rows), slice(None), SWAP)
    for i, rel in enumerate(SWAP):
        for ref, low in ((mine, 0), (theirs, 1)):
            line = vecs[pl.ds(low_bits() ^ (rel | low), 1), :]
            ref[i // 2, i % 2, 0, rows:, :] = jnp.broadcast_to(line, (EXTRA, line.shape[1])).astype(bf)


def wgrad_u_kernel(meta, hid_t, gu, gol_t, *refs):
    c0, c1, theirs, mine, S, SO = refs
    F = gu.shape[1]
    S[...] = dg(hid_t[...], gu[...], 1, 0).reshape(S.shape)
    lay(meta, S, theirs, mine, slice(None), slice(0, F), NEAR)

    def out(ctx):
        SO[...] = dg(gol_t[...], ctx[...].reshape(-1, ctx.shape[-1]), 1, 1).reshape(SO.shape)

    pl.when(pl.program_id(0) == 0)(lambda: out(c0))
    pl.when(pl.program_id(0) > 0)(lambda: out(c1))
    lay(meta, SO, theirs, mine, slice(None), slice(F, F + SO.shape[2]), NEAR)


def wgrad_q_kernel(meta, tok_t, *refs):
    gps, (gb, theirs, mine, S) = refs[:-4], refs[-4:]
    rows = S.shape[1]
    if len(gps) == 1:
        S[...] = dg(tok_t[...], gps[0][...], 1, 1).reshape(S.shape)
    for j, gp in enumerate(gps if len(gps) > 1 else ()):
        @pl.when(pl.program_id(0) == j)
        def _(gp=gp):
            S[...] = dg(tok_t[...], gp[...], 1, 1).reshape(S.shape)

    lay(meta, S, theirs, mine, slice(0, rows), slice(None), SWAP)
    line = jnp.broadcast_to(gb[...], (EXTRA, gb.shape[1])).astype(bf)
    for i in range(4):
        for ref in (mine, theirs):
            ref[i // 2, i % 2, 0, rows:, :] = line


def wgrad(kernel, meta, args, specs, J, rows, lanes, scratch, name, flops):
    spec = pl.BlockSpec((2, 2, 1, rows, lanes), lambda j: (0, 0, j, 0, 0))
    return pl.pallas_call(
        kernel, grid=(J,), in_specs=[SMEM] + specs, out_specs=[spec] * 2, out_shape=[shape((2, 2, J, rows, lanes), bf)] * 2,
        scratch_shapes=[pltpu.VMEM(s, f32) for s in scratch],
        compiler_params=params(28), cost_estimate=cost(flops, 20 * MIB), name=name,
    )(meta, *[pltpu.with_memory_space_constraint(x, pltpu.HBM) for x in args])


def final_du_kernel(meta, x, y, down, up, ow, small, S, SO):
    rows = S.shape[1]
    F = up.shape[1]
    for low, ref in enumerate((x, y)):
        for t, rel in enumerate(NEAR):
            at = low_bits() ^ (rel | low)
            S[at] = ref[t, :rows, :F].astype(f32)
            small[pl.ds(at, 1), :] = ref[t, rows:rows + 1, :F].astype(f32)
            up[pl.ds(pl.multiple_of(at * rows, rows), rows), :] = ref[t, :rows, F:2 * F].astype(f32)
            SO[at] = ref[t, :rows, 2 * F:].astype(f32)
    down[...] = S[...].reshape(down.shape).T
    ow[...] = SO[...].reshape(-1, SO.shape[2]).T


def final_q_kernel(meta, x, y, qkv, gb, S):
    rows = x.shape[1] - EXTRA
    for low, ref in enumerate((x, y)):
        for t, rel in enumerate(NEAR):
            S[low_bits() ^ (rel | low)] = ref[t, :rows, :].astype(f32)
    qkv[...] = S[...].reshape(-1, S.shape[2]).T
    gb[...] = x[0, rows:rows + 1, :].astype(f32)


def final(kernel, meta, xs, outs, scratch, name):
    return pl.pallas_call(
        kernel, in_specs=[SMEM] + [pl.BlockSpec(memory_space=pltpu.VMEM)] * 2,
        out_shape=[shape(s, f32) for s in outs], scratch_shapes=[pltpu.VMEM(s, f32) for s in scratch],
        compiler_params=params(60), cost_estimate=cost(0, 8 * MIB), name=name,
    )(meta, *xs)


def input_grad_kernel(*refs, N, n):
    gps, (w0, w1, g1, *_, out) = refs[:n], refs[n:]
    acc = g1[...]
    j = 0
    for gp in gps:
        for i in range(gp.shape[0]):
            w = w0[0, :N, :] if j == 0 else w1[j - 1, :N, :]
            acc = acc + dg(gp[i], w, 0, 0)
            j += 1
    out[...] = acc


def input_grad(gps, w0, w1, g1, first, count, before=None, R=512):
    _, N, C = gps[0].shape
    D = g1.shape[1]
    fix = lambda a: pl.BlockSpec(a.shape, lambda i: (0,) * a.ndim, pipeline_mode=pl.Buffered(1))
    row = pl.BlockSpec((R, D), lambda i: (i + first, 0))
    more = [] if before is None else [before]
    return pl.pallas_call(
        functools.partial(input_grad_kernel, N=N, n=len(gps)), grid=(count,),
        in_specs=[pl.BlockSpec((g.shape[0], N, R), lambda i: (0, 0, i + first)) for g in gps] + [fix(w0), fix(w1), row] + [ANY] * len(more),
        out_specs=row, out_shape=shape((C, D), f32), input_output_aliases={len(gps) + 3: 0} if more else {},
        compiler_params=params(28), cost_estimate=cost(2 * C * D * D * 3, 24 * MIB), name="input_grad",
    )(*gps, w0, w1, g1, *more)


def fetch(x, s):
    n = lax.axis_size("narrow")
    return lax.ppermute(x, "narrow", [((i + s) % n, i) for i in range(n)])


def give(x, s):
    n = lax.axis_size("narrow")
    return lax.ppermute(x, "narrow", [(i, (i + s) % n) for i in range(n)])


def flip(x, bit):
    return lax.ppermute(x, "wide", [(i, i ^ bit) for i in range(lax.axis_size("wide"))])


def total(terms):
    x = terms[0].astype(f32)
    for y in terms[1:]:
        x = x + y.astype(f32)
    return x.astype(bf)


def rest(x):
    bit = SPLIT
    while bit < lax.axis_size("wide"):
        x = add(x, flip(x, bit))
        bit *= 2
    return x


def tie(xs, deps):
    return lax.optimization_barrier((xs, deps))[0]


def add(a, b):
    return (a.astype(f32) + b.astype(f32)).astype(bf)


def rotary_tables(capacity):
    positions = jnp.arange(capacity).astype(f32)
    frequencies = 10000.0 ** (-2.0 * jnp.arange(HD // 2).astype(f32) / HD)
    angles = frequencies[:, None] * positions[None, :]
    return jnp.cos(angles), jnp.sin(angles)


def shards(
    tokens, lengths, qkv_weight, qkv_bias, out_weight, out_bias, norm1_gain, norm1_shift,
    up_weight, up_bias, down_weight, down_bias, norm2_gain, norm2_shift, cotangent,
):
    J = lax.axis_size("narrow")
    tok, cot = tokens[0], cotangent[0]
    C, D = tok.shape
    G = HEADS // J
    N = 3 * G * HD
    F = up_weight.shape[1]
    rows = D // SPLIT
    low = jnp.bitwise_and(lax.axis_index("wide"), SPLIT - 1).astype(jnp.int32)
    meta = lengths
    cos, sin = rotary_tables(C)

    qkv_t = qkv_weight.transpose(1, 2, 0).reshape(N, D)
    qo = jnp.concatenate([qkv_weight.reshape(D, N), out_weight.T], axis=1)
    bias = jnp.concatenate([qkv_bias.reshape(-1), up_bias])
    bias = jnp.pad(bias, (0, 2 * D - bias.size)).reshape(2, D)
    cut = lambda x: lax.dynamic_slice_in_dim(x, low * rows, rows, 0)
    q_piece = jnp.concatenate([cut(qo), jnp.pad(bias, ((0, EXTRA - 2), (0, 0)))], axis=0)
    got = [fetch(q_piece, s) for s in range(1, J)]
    vec = jnp.stack([out_bias, norm1_gain, norm1_shift, down_bias, norm2_gain, norm2_shift]).astype(f32)
    b_own = qkv_bias.astype(f32).reshape(1, 3, G, HD, 1)
    ud_piece = jnp.concatenate([cut(up_weight), cut(down_weight)], axis=1)
    ud_got = [fetch(tie(ud_piece, q_piece), 1)]
    q0, k0, v0, e0, c0, l0, wt0, tok_t = attn_fwd(meta, [qkv_t, out_weight], (0, 1), tok, b_own, cos, sin, True)
    got, ud_got, tok_t = lax.optimization_barrier((got, ud_got, tok_t))
    biases = jnp.stack([bias] + [x[rows:rows + 2] for x in got]).reshape(J, 2 * D).astype(f32)
    bq, ub = biases[1:, :N].reshape(J - 1, 3, G, HD, 1), biases[:, N:N + F]
    q = jnp.stack([x[:rows] for x in got])
    q_x, q_y = flip(q, 2), flip(q, 4)
    ud_2 = fetch(tie(ud_piece, got), 2)
    h = rows // 2
    q_x, q_y, ud_2, bq, ub, vec = lax.optimization_barrier((q_x, q_y, ud_2, bq, ub, vec))
    q_d = [flip(q_y[:, :h], 2), flip(q_x[:, h:], 4)]
    q_far = [flip(x, 1) for x in (q, q_x, q_y)]
    ud_3 = fetch(tie(ud_piece, q_x), 3)
    q_d, ud_3 = lax.optimization_barrier((q_d, ud_3))
    q_far = q_far + [flip(x, 1) for x in q_d]
    q_places = tuple((rel | low, half, rows) for low in (0, 1) for rel, half in ((0, 0), (2, 0), (4, 0), (6, 0), (6, h)))
    q_far, ud_3 = lax.optimization_barrier((q_far, ud_3))
    ud = jnp.stack(ud_got + [ud_2, ud_3])
    q_pieces = [q, q_x, q_y] + q_d + q_far
    ud_near = [flip(ud, rel) for rel in NEAR[1:]]
    ud_far = [flip(ud, 1)]
    tok_t = tie(tok_t, ud)
    q1, k1, v1, e1, c1, l1, wt1 = attn_fwd(meta, q_pieces, q_places, tok_t, bq, cos, sin, False)
    ud_near, ud_far, c1 = lax.optimization_barrier((ud_near, ud_far, c1))
    ud_pieces = [ud] + ud_near + ud_far + [flip(x, 1) for x in ud_near]
    ud_places = [(rel | low, 0, rows) for low in (0, 1) for rel in NEAR]
    ud_layout = tuple(((0, 1), place) for place in ud_places)
    out, act, gu, hid_t, gl_t, g1, gol_t, do_t, small, ubg = ffn(
        meta, up_weight, down_weight, ud_pieces, ud_layout, tok, cot, (c0, c1), (wt0, wt1), vec, ub)

    whole = lambda a: pl.BlockSpec(a.shape, lambda j: (0,) * a.ndim, pipeline_mode=pl.Buffered(1))
    vecs = jnp.concatenate([jnp.broadcast_to(small[None, :6], (J, 6, D)), ubg[:, None], jnp.zeros((J, 1, D), f32)], axis=1)
    u_t, u_m = wgrad(
        wgrad_u_kernel, meta, (hid_t, gu, gol_t, c0, c1),
        [whole(hid_t), pl.BlockSpec((C, F), lambda j: (0, j)), whole(gol_t), pl.BlockSpec((G, HD, C), lambda j: (0, 0, 0)),
         pl.BlockSpec((G, HD, C), lambda j: (jnp.maximum(j - 1, 0), 0, 0))],
        J, rows, F + G * HD, [(SPLIT, rows, F), (SPLIT, rows, G * HD)], "wgrad_u", 2 * C * D * (J * F + D))
    u_1 = flip(u_t, 1)
    gl_t = tie(gl_t, u_t)
    d_t, d_m = wgrad(
        wgrad_d_kernel, meta, (gl_t, act, vecs),
        [whole(gl_t), pl.BlockSpec((C, F), lambda j: (0, j)), pl.BlockSpec((None, 8, D), lambda j: (j, 0, 0))],
        J, rows + EXTRA, F, [(SPLIT, rows, F)], "wgrad_d", 2 * C * D * J * F)

    def grad_q(gps, gb):
        n = gb.shape[0]
        one = pl.BlockSpec((None, N, C), lambda j: (j, 0, 0)) if len(gps) == 1 else pl.BlockSpec((None, N, C), lambda j: (0, 0, 0))
        return wgrad(
            wgrad_q_kernel, meta, (tok_t, *gps, gb), [whole(tok_t)] + [one] * len(gps) + [pl.BlockSpec((None, 1, N), lambda j: (j, 0, 0))],
            n, rows + EXTRA, N, [(SPLIT, rows, N)], "wgrad_q", 2 * C * D * n * N)

    def backward(group, count, do_t):
        saved, shift = ((e0, v0, c0, l0, q0, k0), 0) if group == 0 else ((e1, v1, c1, l1, q1, k1), G)
        gp, gb = attn_bwd(meta, saved, do_t, cos, sin, G, group * G - shift, shift, count * G)
        return gp.reshape(count, N, C), gb.reshape(count, G, 3, HD).transpose(0, 2, 1, 3).reshape(count, 1, N)

    def halves(mine, got):
        return add(mine[0], got[0]), add(mine[1], got[1])

    u_1, u_m, d_t = lax.optimization_barrier((u_1, u_m, d_t))
    d_1 = flip(d_t, 1)
    u_k, u_s = halves(u_m, u_1)
    u_2 = flip(u_s, 4)
    do_t = tie(do_t, u_s)
    d_1, d_m, do_t = lax.optimization_barrier((d_1, d_m, do_t))
    d_k, d_s = halves(d_m, d_1)
    d_2 = flip(d_s, 2)
    do_t = tie(do_t, d_s)
    gpa, gba = backward(1, 2, do_t)
    u_2, d_2, gpa, do_t = lax.optimization_barrier((u_2, d_2, gpa, do_t))
    u_k, u_s = halves(u_k, u_2)
    u_3 = flip(u_s, 2)
    d_k, d_s = halves(d_k, d_2)
    d_3 = flip(d_s, 4)
    gpa_ = tie(gpa, (u_s, d_s))
    qa_t, qa_m = grad_q((gpa_,), gba)
    qa_1 = flip(qa_t, 1)
    do_t = tie(do_t, qa_t)
    gpb, gbb = backward(0, 1, do_t)
    u_3, d_3, qa_1, gpb, do_t = lax.optimization_barrier((u_3, d_3, qa_1, gpb, do_t))
    du_s = [jnp.concatenate([add(d_k[j], d_3[j]), jnp.pad(add(u_k[j], u_3[j]), ((0, EXTRA), (0, 0)))], axis=1) for j in range(J)]
    du_3 = [give(du_s[s], s) for s in (1, 3)]
    qa_k, qa_s = halves(qa_m, qa_1)
    qa_2 = flip(qa_s, 2)
    do_t = tie(do_t, (du_s, qa_s))
    gpc, gbc = backward(3, 1, do_t)
    du_3, qa_2, gpb, gpc = lax.optimization_barrier((du_3, qa_2, gpb, gpc))
    qa_k, qa_s = halves(qa_k, qa_2)
    qa_3 = flip(qa_s, 4)
    gpc_ = tie(gpc, (qa_s, qa_k))
    du_2 = give(tie(du_s[2], qa_s), 2)
    qb_t, qb_m = grad_q((gpb, gpc_), jnp.concatenate([gbb, gbc], axis=0))
    qb_1 = flip(qb_t, 1)
    qa_3, du_2, qb_t, qb_m = lax.optimization_barrier((qa_3, du_2, qb_t, qb_m))
    du = rest(total([du_s[0], du_2] + du_3))
    du_x, du_y = flip(du, 2), flip(du, 4)
    qa_s = [add(qa_k[j], qa_3[j]) for j in range(2)]
    q_3 = [give(qa_s[0], 1), give(qa_s[1], 2)]
    g1 = tie(g1, (qb_t, qa_s, du))
    x_grad = input_grad([gpb, gpa, gpc], wt0, wt1, g1, 0, 1)
    qb_1, qb_m, q_3, x_grad = lax.optimization_barrier((qb_1, qb_m, q_3, x_grad))
    qb_s = [add(qb_m[i // 2, i % 2], qb_1[i // 2, i % 2]) for i in range(4)]
    qb_2 = [flip(qb_s[i], SWAP[i]) for i in (1, 2, 3)]
    g1, x_grad = tie((g1, x_grad), qb_s)
    x_grad = input_grad([gpb, gpa, gpc], wt0, wt1, g1, 1, C // 512 - 1, x_grad)
    qb_2, du_x, du_y, x_grad = lax.optimization_barrier((qb_2, du_x, du_y, x_grad))
    cut_at = du.shape[0] // 16 * 8
    du_d = [flip(du_y[:cut_at], 2), flip(du_x[cut_at:], 4)]
    qb = total([qb_s[0]] + qb_2)
    q_3.append(give(qb[1], J - 1))
    q_3, du_d = lax.optimization_barrier((q_3, du_d))
    q = rest(total([qb[0]] + q_3))
    q_4 = [flip(q, rel) for rel in NEAR[1:]]
    du = jnp.stack([du, du_x, du_y, jnp.concatenate(du_d, axis=0)])
    du_5 = flip(du, 1)
    q_4, du_5 = lax.optimization_barrier((q_4, du_5))
    q = jnp.stack([q] + q_4)
    q_5 = flip(q, 1)
    du = tie(du, q)
    down_g, up_g, ow_g, small = final(
        final_du_kernel, meta, (du, du_5), [(F, D), (D, F), (G * HD, D), (8, D)], [(SPLIT, rows, F), (SPLIT, rows, G * HD)], "final_du")
    q_5, down_g = lax.optimization_barrier((q_5, down_g))
    qkv_g, gb = final(final_q_kernel, meta, (q, q_5), [(N, D), (1, N)], [(SPLIT, rows, N)], "final_q")
    return (
        out[None], x_grad[None], qkv_g.reshape(3, G * HD, D).transpose(2, 0, 1), gb.reshape(3, G * HD), ow_g, small[5], small[3], small[4],
        up_g, small[6], down_g, small[2], small[0], small[1],
    )


def solution(mesh):
    rows = P(("wide", "narrow"), None, None)
    weights = (P(None, None, "narrow"), P(None, "narrow"), P("narrow", None), P(), P(), P(),
               P(None, "narrow"), P("narrow"), P("narrow", None), P(), P(), P())
    return jax.shard_map(
        shards, mesh=mesh, in_specs=(rows, P("wide", None)) + weights + (rows,),
        out_specs=(rows, rows) + weights, check_vma=False,
    )
```

```python
import functools

import jax
import jax.numpy as jnp
from jax import lax
from jax.experimental import pallas as pl
from jax.experimental.pallas import tpu as pltpu
from jax.sharding import PartitionSpec as P

bf = jnp.bfloat16
f32 = jnp.float32
LOG2E = 1.4426950408889634
HEADS = 12
HD = 64
SPLIT = 8
EXTRA = 8
MIB = 1 << 20


def dg(a, b, ca, cb):
    return lax.dot_general(a, b, (((ca,), (cb,)), ((), ())), preferred_element_type=f32)


def mean(x):
    return jnp.mean(x, axis=-1, keepdims=True)


def shape(s, d):
    return jax.ShapeDtypeStruct(s, d)


SMEM = pl.BlockSpec(memory_space=pltpu.SMEM)
ANY = pl.BlockSpec(memory_space=pl.ANY)


def length_of(lengths):
    return lengths[0, lax.axis_index("narrow")]


def low_bits():
    return jnp.bitwise_and(lax.axis_index("wide"), SPLIT - 1)


def params(mib):
    return pltpu.CompilerParams(vmem_limit_bytes=mib * MIB)


def cost(flops, nbytes):
    return pl.CostEstimate(flops=1, bytes_accessed=1, transcendentals=0)


def put_piece(meta, src, g, lanes, place, dst, sem):
    rel, half, whole = place
    rows = src.shape[1]
    at = 0 if rel is None else (low_bits() ^ rel) * whole + half
    return pltpu.make_async_copy(src.at[g, :, lanes], dst.at[pl.ds(pl.multiple_of(at, 16), rows), :], sem)


def attn_fwd_kernel(meta, *refs, C, KC, G, layout, own):
    pieces, refs = refs[:len(layout)], refs[len(layout):]
    x, b, cos, sin, q_t, k_t, v_d, e, ctx, linv, w_t, *rest = refs
    if own:
        x_t, Q2, KD, VA, S, W, flag, sem = rest
    else:
        x_t, (Q2, KD, VA, S, W, flag, sem) = x, rest
    h = pl.program_id(0)
    length = length_of(meta)

    if own:
        @pl.when(h == 0)
        def _():
            x_t[...] = x[...].T
            n = pieces[0].shape[0]
            w_t[:n, :] = pieces[0][...]
            w_t[n:, :] = pieces[1][...]
    else:
        groups = pieces[0].shape[0]

        def copies(g):
            return [put_piece(meta, pieces[t], g, slice(None), layout[t], W.at[g], sem.at[g, t]) for t in range(len(pieces))]

        @pl.when(h == 0)
        def _():
            for g in range(groups):
                for c in copies(g):
                    c.start()

        @pl.when(lax.rem(h, G) == 0)
        def _():
            g = lax.div(h, G)
            for c in copies(g):
                c.wait()
            w_t[...] = W[g].T

    at = lax.rem(h, G)
    w = jnp.concatenate([w_t[pl.ds(pl.multiple_of((p * G + at) * HD, HD), HD), :] for p in range(3)], axis=0)
    bias = [jnp.broadcast_to(b[i:i + 1, :], (2 * HD, HD)).T[:, :1] for i in range(3)]
    p = dg(w, x_t[...], 1, 0) + jnp.concatenate(bias, axis=0)
    c, d = cos[...], sin[...]

    def rot(v):
        u, z = v[:HD // 2], v[HD // 2:]
        return jnp.concatenate([u * c - z * d, z * c + u * d], axis=0)

    live = lax.broadcasted_iota(jnp.int32, (HD, C), 1) < length
    q = rot(p[:HD]).astype(bf).astype(f32)
    k = jnp.where(live, rot(p[HD:2 * HD]), 0.0).astype(bf)
    v = jnp.where(live, p[2 * HD:], 0.0).astype(bf)
    q_t[...] = (q * 0.125).astype(bf)
    q = q * (0.125 * LOG2E)
    hi = q.astype(bf)
    Q2[:HD, :] = hi
    Q2[HD:, :] = (q - hi.astype(f32)).astype(bf)
    k_t[...] = k
    KD[...] = jnp.concatenate([k, k], axis=0).T
    v_d[...] = jnp.concatenate([v, v], axis=0).T
    VA[:HD, :] = v
    VA[HD:, :] = jnp.where(live[:16], 1.0, 0.0).astype(bf)
    kf = k.astype(f32)
    qn = jnp.max(jnp.sum(q * q, axis=0, keepdims=True))
    kn = jnp.max(jnp.sum(kf * kf, axis=0, keepdims=True))
    flag[0] = (qn * kn <= 1e4).astype(jnp.int32)

    @pl.when(flag[0] == 1)
    def _():
        for j in range(C // KC):
            r = slice(j * KC, (j + 1) * KC)
            e[r, :] = jnp.exp2(dg(KD[r, :], Q2[...], 1, 0)).astype(bf)

    @pl.when(flag[0] == 0)
    def _():
        BQ = S.shape[1]

        def block(i, carry):
            cols = pl.ds(pl.multiple_of(i * BQ, BQ), BQ)

            def score(j, m):
                r = pl.ds(pl.multiple_of(j * KC, KC), KC)
                keys = lax.broadcasted_iota(jnp.int32, (KC, BQ), 0) + j * KC
                x = jnp.where(keys < length, dg(KD[r, :], Q2[:, cols], 1, 0), -1e30)
                S[r, :] = x
                return jnp.maximum(m, jnp.max(x, axis=0, keepdims=True))

            m = lax.fori_loop(0, C // KC, score, jnp.full((1, BQ), -1e30, f32))

            def power(j, carry):
                r = pl.ds(pl.multiple_of(j * KC, KC), KC)
                e[r, cols] = jnp.exp2(S[r, :] - m).astype(bf)
                return carry

            return lax.fori_loop(0, C // KC, power, carry)

        lax.fori_loop(0, C // BQ, block, 0)

    o = dg(VA[...], e[...], 1, 0)
    inv = 1.0 / o[HD:HD + 1]
    linv[...] = inv
    ctx[...] = (o[:HD] * inv).astype(bf)


def attn_fwd(meta, pieces, layout, x, b, cos, sin, own):
    groups, _, D = pieces[0].shape if not own else (1,) + pieces[0].shape
    C = x.shape[0] if own else x.shape[1]
    G = b.shape[1]
    H = groups * G
    at = lambda h: (h, 0, 0)
    fix = lambda a: pl.BlockSpec(a.shape, lambda h: (0,) * a.ndim, pipeline_mode=pl.Buffered(1))
    hb = pl.BlockSpec((None, HD, C), at)
    out_specs = [hb, hb, pl.BlockSpec((None, C, 2 * HD), at), pl.BlockSpec((None, C, C), at), hb,
                 pl.BlockSpec((None, 1, C), at), pl.BlockSpec((None, D, D), lambda h: (h // G, 0, 0))]
    out_shape = [shape((H, HD, C), bf), shape((H, HD, C), bf), shape((H, C, 2 * HD), bf), shape((H, C, C), bf),
                 shape((H, HD, C), bf), shape((H, 1, C), f32), shape((groups, D, D), bf)]
    if own:
        out_specs.append(pl.BlockSpec((D, C), lambda h: (0, 0)))
        out_shape.append(shape((D, C), bf))
    return pl.pallas_call(
        functools.partial(attn_fwd_kernel, C=C, KC=min(128, C), G=G, layout=layout, own=own), grid=(H,),
        in_specs=[SMEM] + ([fix(p) for p in pieces] if own else [ANY] * len(pieces))
        + [fix(x), pl.BlockSpec((None, None, 3, HD), lambda h: (h // G, h % G, 0, 0)), fix(cos), fix(sin)],
        out_specs=out_specs, out_shape=out_shape,
        scratch_shapes=[pltpu.VMEM((2 * HD, C), bf), pltpu.VMEM((C, 2 * HD), bf), pltpu.VMEM((HD + 16, C), bf),
                        pltpu.VMEM((C, C // 3 if C % 384 == 0 else C), f32), pltpu.VMEM((8, 128) if own else (groups, D, D), bf),
                        pltpu.SMEM((1,), jnp.int32), pltpu.SemaphoreType.DMA((groups, len(pieces)))],
        compiler_params=params(60), cost_estimate=cost(H * (4 * C * C * 256 + 2 * C * D * 3 * HD), H * C * C * 2 + 8 * MIB),
        name="attn_fwd_own" if own else "attn_fwd",
    )(meta, *pieces, x, b, cos, sin)


def ffn_kernel(meta, u_own, d_own, *refs, R, layout):
    pieces, refs = refs[:len(layout)], refs[len(layout):]
    tok, cot, *refs = refs
    J = pieces[0].shape[0] + 1
    ctxs, ows, refs = refs[:2], refs[2:4], refs[4:]
    (vec, ub, out, act, gu, hid_t, gl_t, g1_o, gol_t, do_t, small, ubg, G, U, Dn, sem) = refs
    i = pl.program_id(0)
    groups = J - 1

    def copies():
        cs = [pltpu.make_async_copy(u_own, U.at[0], sem.at[0, 0, 0]), pltpu.make_async_copy(d_own, Dn.at[0], sem.at[1, 0, 0])]
        for g in range(groups):
            for t, (piece, (parts, place)) in enumerate(zip(pieces, layout)):
                for k, s in enumerate(parts):
                    lanes = slice(k * U.shape[2], (k + 1) * U.shape[2])
                    cs.append(put_piece(meta, piece, g, lanes, place, (U, Dn)[s].at[g + 1], sem.at[s, g + 1, t]))
        return cs

    @pl.when(i == 0)
    def _():
        for c in copies():
            c.start()
        small[...] = jnp.zeros_like(small)
        ubg[...] = jnp.zeros_like(ubg)

    ob, g1, s1, db, g2, s2 = [vec[k:k + 1, :] for k in range(6)]
    D = tok.shape[1]
    F = U.shape[2]

    def csum(k, x):
        small[k:k + 1, :] += jnp.sum(x, axis=0, keepdims=True)

    ow = jnp.concatenate([w[g] for w in ows for g in range(w.shape[0])], axis=0)
    ctx = jnp.concatenate([c[...].reshape(-1, R) for c in ctxs], axis=0)
    pre = tok[...].astype(f32) + dg(ctx.T, ow, 1, 0) + ob
    cen = pre - mean(pre)
    r1 = lax.rsqrt(mean(cen * cen) + 1e-6)
    n1 = cen * r1
    hid = n1 * g1 + s1
    hl = hid.astype(bf)
    hid_t[...] = hl.T
    acc = hid + db

    @pl.when(i == 0)
    def _():
        for c in copies():
            c.wait()

    for j in range(J):
        u = dg(hl, U[j], 1, 0) + ub[j:j + 1, :]
        phi = 0.5 * lax.erf(u * 0.7071067811865476) + 0.5
        a = (u * phi).astype(bf)
        act[:, j * F:(j + 1) * F] = a
        G[:, j * F:(j + 1) * F] = phi + u * (jnp.exp2(u * u * -0.7213475204444817) * 0.3989422804014327)
        acc = acc + dg(a, Dn[j], 1, 0)
    cen = acc - mean(acc)
    r2 = lax.rsqrt(mean(cen * cen) + 1e-6)
    n2 = cen * r2
    out[...] = (n2 * g2 + s2).astype(bf)
    c = cot[...].astype(f32)
    csum(0, c * n2)
    csum(1, c)
    sg = c * g2
    gt = r2 * (sg - mean(sg) - n2 * mean(sg * n2))
    csum(2, gt)
    gl = gt.astype(bf)
    gl_t[...] = gl.T
    dh = gt
    for j in range(J):
        g = dg(gl, Dn[j], 1, 1) * G[:, j * F:(j + 1) * F]
        ubg[j:j + 1, :] += jnp.sum(g, axis=0, keepdims=True)
        gb = g.astype(bf)
        gu[:, j * F:(j + 1) * F] = gb
        dh = dh + dg(gb, U[j], 1, 1)
    csum(3, dh * n1)
    csum(4, dh)
    sg = dh * g1
    go = r1 * (sg - mean(sg) - n1 * mean(sg * n1))
    csum(5, go)
    g1_o[...] = go
    gol = go.astype(bf)
    gol_t[...] = gol.T
    do_t[...] = dg(ow, gol, 1, 1).astype(bf).reshape(do_t.shape)


def ffn(meta, u_own, d_own, pieces, layout, tok, cot, ctxs, wts, vec, ub, R=512):
    C, D = tok.shape
    J, F = ub.shape
    H = HEADS
    row = lambda w: pl.BlockSpec((R, w), lambda i: (i, 0))
    col = pl.BlockSpec((D, R), lambda i: (0, i))
    fix = lambda a: pl.BlockSpec(a.shape, lambda i: (0,) * a.ndim, pipeline_mode=pl.Buffered(1))
    hb = lambda n: pl.BlockSpec((n, HD, R), lambda i: (0, 0, i))
    acc = lambda s: pl.BlockSpec(s, lambda i: (0, 0))
    share = H // J * HD
    at = 3
    owb = lambda w: pl.BlockSpec((w.shape[0], share, D), lambda i: (0, at, 0), pipeline_mode=pl.Buffered(1))
    return pl.pallas_call(
        functools.partial(ffn_kernel, R=R, layout=layout), grid=(C // R,),
        in_specs=[SMEM, ANY, ANY] + [ANY] * len(pieces) + [row(D), row(D)] + [hb(c.shape[0]) for c in ctxs] + [owb(w) for w in wts] + [fix(vec), fix(ub)],
        out_specs=[row(D), row(J * F), row(J * F), col, col, row(D), col, hb(H), acc((8, D)), acc((J, F))],
        out_shape=[shape((C, D), bf), shape((C, J * F), bf), shape((C, J * F), bf), shape((D, C), bf), shape((D, C), bf), shape((C, D), f32),
                   shape((D, C), bf), shape((H, HD, C), bf), shape((8, D), f32), shape((J, F), f32)],
        scratch_shapes=[pltpu.VMEM((R, J * F), f32), pltpu.VMEM((J, D, F), bf), pltpu.VMEM((J, F, D), bf),
                        pltpu.SemaphoreType.DMA((2, J, len(pieces)))],
        compiler_params=params(60), cost_estimate=cost(2 * C * D * (2 * D + 4 * J * F), 60 * MIB), name="ffn",
    )(meta, u_own, d_own, *pieces, tok, cot, *ctxs, *wts, vec, ub)


def attn_bwd_kernel(meta, e, v_d, do_t, ctx, linv, q_t, k_t, cos, sin, gp, gb, D2, DI, DS, DST, ET, *, C, KC):
    length = length_of(meta)
    g = do_t[...].astype(f32)
    inv = linv[...]
    DI[...] = jnp.sum(g * ctx[...].astype(f32), axis=0, keepdims=True) * inv
    g = g * inv
    hi = g.astype(bf)
    D2[:HD, :] = hi
    D2[HD:, :] = (g - hi.astype(f32)).astype(bf)
    for j in range(C // KC):
        r = slice(j * KC, (j + 1) * KC)
        dp = dg(v_d[r, :], D2[...], 1, 0)
        ej = e[r, :]
        ds = (ej.astype(f32) * (dp - DI[...])).astype(bf)
        DS[r, :] = ds
        DST[:, r] = ds.T
        ET[:, r] = ej.T
    dq = dg(k_t[...], DS[...], 1, 0)
    dk = dg(q_t[...], DST[...], 1, 0)
    dv = dg(D2[:HD, :], ET[...], 1, 0)
    live = lax.broadcasted_iota(jnp.int32, (HD, C), 1) < length
    c, s = cos[...], sin[...]

    def unrot(x):
        u, w = x[:HD // 2], x[HD // 2:]
        return jnp.concatenate([u * c + w * s, w * c - u * s], axis=0)

    def put(k, x):
        gp[k] = x.astype(bf)
        total = jnp.sum(x, axis=1, keepdims=True)
        gb[k:k + 1, :] = jnp.broadcast_to(total, (HD, 2 * HD)).T[:1]

    put(0, unrot(dq * 0.125))
    put(1, unrot(jnp.where(live, dk, 0.0)))
    put(2, jnp.where(live, dv, 0.0))


def attn_bwd(meta, saved, do_t, cos, sin, G, first, shift, H):
    e, v_d, ctx, linv, q_t, k_t = saved
    C = e.shape[1]
    sp = lambda s: pl.BlockSpec((None,) + s, lambda h: (h + first, 0, 0))
    tab = pl.BlockSpec((HD // 2, C), lambda h: (0, 0))
    return pl.pallas_call(
        functools.partial(attn_bwd_kernel, C=C, KC=min(256, C)), grid=(H,),
        in_specs=[SMEM, sp((C, C)), sp((C, 2 * HD)), pl.BlockSpec((None, HD, C), lambda h: (h + first + shift, 0, 0)), sp((HD, C)), sp((1, C)),
                  sp((HD, C)), sp((HD, C)), tab, tab],
        out_specs=[pl.BlockSpec((None, 3, None, HD, C), lambda h: (h // G, 0, h % G, 0, 0)), pl.BlockSpec((None, 3, HD), lambda h: (h, 0, 0))],
        out_shape=[shape((H // G, 3, G, HD, C), bf), shape((H, 3, HD), f32)],
        scratch_shapes=[pltpu.VMEM((2 * HD, C), bf), pltpu.VMEM((1, C), f32)] + [pltpu.VMEM((C, C), bf)] * 3,
        compiler_params=params(60), cost_estimate=cost(H * 8 * C * C * 256, H * C * C * 2 + 16 * MIB), name="attn_bwd",
    )(meta, e, v_d, do_t, ctx, linv, q_t, k_t, cos, sin)


NEAR = (0, 2, 4, 6)
SWAP = (0, 4, 2, 6)


def lay(meta, S, theirs, mine, rows, lanes, order):
    for i, rel in enumerate(order):
        for ref, low in ((mine, 0), (theirs, 1)):
            ref[i // 2, i % 2, 0, rows, lanes] = S[low_bits() ^ (rel | low)].astype(bf)


def wgrad_d_kernel(meta, gl_t, act, vecs, theirs, mine, S):
    rows = S.shape[1]
    S[...] = dg(gl_t[...], act[...], 1, 0).reshape(S.shape)
    lay(meta, S, theirs, mine, slice(0, rows), slice(None), SWAP)
    for i, rel in enumerate(SWAP):
        for ref, low in ((mine, 0), (theirs, 1)):
            line = vecs[pl.ds(low_bits() ^ (rel | low), 1), :]
            ref[i // 2, i % 2, 0, rows:, :] = jnp.broadcast_to(line, (EXTRA, line.shape[1])).astype(bf)


def wgrad_u_kernel(meta, hid_t, gu, gol_t, *refs):
    c0, c1, theirs, mine, S, SO = refs
    F = gu.shape[1]
    S[...] = dg(hid_t[...], gu[...], 1, 0).reshape(S.shape)
    lay(meta, S, theirs, mine, slice(None), slice(0, F), NEAR)

    def out(ctx):
        SO[...] = dg(gol_t[...], ctx[...].reshape(-1, ctx.shape[-1]), 1, 1).reshape(SO.shape)

    pl.when(pl.program_id(0) == 0)(lambda: out(c0))
    pl.when(pl.program_id(0) > 0)(lambda: out(c1))
    lay(meta, SO, theirs, mine, slice(None), slice(F, F + SO.shape[2]), NEAR)


def wgrad_q_kernel(meta, tok_t, *refs):
    gps, (gb, theirs, mine, S) = refs[:-4], refs[-4:]
    rows = S.shape[1]
    if len(gps) == 1:
        S[...] = dg(tok_t[...], gps[0][...], 1, 1).reshape(S.shape)
    for j, gp in enumerate(gps if len(gps) > 1 else ()):
        @pl.when(pl.program_id(0) == j)
        def _(gp=gp):
            S[...] = dg(tok_t[...], gp[...], 1, 1).reshape(S.shape)

    lay(meta, S, theirs, mine, slice(0, rows), slice(None), SWAP)
    line = jnp.broadcast_to(gb[...], (EXTRA, gb.shape[1])).astype(bf)
    for i in range(4):
        for ref in (mine, theirs):
            ref[i // 2, i % 2, 0, rows:, :] = line


def wgrad(kernel, meta, args, specs, J, rows, lanes, scratch, name, flops):
    spec = pl.BlockSpec((2, 2, 1, rows, lanes), lambda j: (0, 0, j, 0, 0))
    return pl.pallas_call(
        kernel, grid=(J,), in_specs=[SMEM] + specs, out_specs=[spec] * 2, out_shape=[shape((2, 2, J, rows, lanes), bf)] * 2,
        scratch_shapes=[pltpu.VMEM(s, f32) for s in scratch],
        compiler_params=params(28), cost_estimate=cost(flops, 20 * MIB), name=name,
    )(meta, *[pltpu.with_memory_space_constraint(x, pltpu.HBM) for x in args])


def final_du_kernel(meta, x, y, down, up, ow, small, S, SO):
    rows = S.shape[1]
    F = up.shape[1]
    for low, ref in enumerate((x, y)):
        for t, rel in enumerate(NEAR):
            at = low_bits() ^ (rel | low)
            S[at] = ref[t, :rows, :F].astype(f32)
            small[pl.ds(at, 1), :] = ref[t, rows:rows + 1, :F].astype(f32)
            up[pl.ds(pl.multiple_of(at * rows, rows), rows), :] = ref[t, :rows, F:2 * F].astype(f32)
            SO[at] = ref[t, :rows, 2 * F:].astype(f32)
    down[...] = S[...].reshape(down.shape).T
    ow[...] = SO[...].reshape(-1, SO.shape[2]).T


def final_q_kernel(meta, x, y, qkv, gb, S):
    rows = x.shape[1] - EXTRA
    for low, ref in enumerate((x, y)):
        for t, rel in enumerate(NEAR):
            S[low_bits() ^ (rel | low)] = ref[t, :rows, :].astype(f32)
    qkv[...] = S[...].reshape(-1, S.shape[2]).T
    gb[...] = x[0, rows:rows + 1, :].astype(f32)


def final(kernel, meta, xs, outs, scratch, name):
    return pl.pallas_call(
        kernel, in_specs=[SMEM] + [pl.BlockSpec(memory_space=pltpu.VMEM)] * 2,
        out_shape=[shape(s, f32) for s in outs], scratch_shapes=[pltpu.VMEM(s, f32) for s in scratch],
        compiler_params=params(60), cost_estimate=cost(0, 8 * MIB), name=name,
    )(meta, *xs)


def input_grad_kernel(*refs, N, n):
    gps, (w0, w1, g1, *_, out) = refs[:n], refs[n:]
    acc = g1[...]
    j = 0
    for gp in gps:
        for i in range(gp.shape[0]):
            w = w0[0, :N, :] if j == 0 else w1[j - 1, :N, :]
            acc = acc + dg(gp[i], w, 0, 0)
            j += 1
    out[...] = acc


def input_grad(gps, w0, w1, g1, first, count, before=None, R=256):
    _, N, C = gps[0].shape
    D = g1.shape[1]
    fix = lambda a: pl.BlockSpec(a.shape, lambda i: (0,) * a.ndim, pipeline_mode=pl.Buffered(1))
    row = pl.BlockSpec((R, D), lambda i: (i + first, 0))
    more = [] if before is None else [before]
    return pl.pallas_call(
        functools.partial(input_grad_kernel, N=N, n=len(gps)), grid=(count,),
        in_specs=[pl.BlockSpec((g.shape[0], N, R), lambda i: (0, 0, i + first)) for g in gps] + [fix(w0), fix(w1), row] + [ANY] * len(more),
        out_specs=row, out_shape=shape((C, D), f32), input_output_aliases={len(gps) + 3: 0} if more else {},
        compiler_params=params(28), cost_estimate=cost(2 * C * D * D * 3, 24 * MIB), name="input_grad",
    )(*gps, w0, w1, g1, *more)


def fetch(x, s):
    n = lax.axis_size("narrow")
    return lax.ppermute(x, "narrow", [((i + s) % n, i) for i in range(n)])


def give(x, s):
    n = lax.axis_size("narrow")
    return lax.ppermute(x, "narrow", [(i, (i + s) % n) for i in range(n)])


def flip(x, bit):
    return lax.ppermute(x, "wide", [(i, i ^ bit) for i in range(lax.axis_size("wide"))])


def total(terms):
    x = terms[0].astype(f32)
    for y in terms[1:]:
        x = x + y.astype(f32)
    return x.astype(bf)


def rest(x):
    bit = SPLIT
    while bit < lax.axis_size("wide"):
        x = add(x, flip(x, bit))
        bit *= 2
    return x


def tie(xs, deps):
    return lax.optimization_barrier((xs, deps))[0]


def add(a, b):
    return (a.astype(f32) + b.astype(f32)).astype(bf)


def rotary_tables(capacity):
    positions = jnp.arange(capacity).astype(f32)
    frequencies = 10000.0 ** (-2.0 * jnp.arange(HD // 2).astype(f32) / HD)
    angles = frequencies[:, None] * positions[None, :]
    return jnp.cos(angles), jnp.sin(angles)


def shards(
    tokens, lengths, qkv_weight, qkv_bias, out_weight, out_bias, norm1_gain, norm1_shift,
    up_weight, up_bias, down_weight, down_bias, norm2_gain, norm2_shift, cotangent,
):
    J = lax.axis_size("narrow")
    tok, cot = tokens[0], cotangent[0]
    C, D = tok.shape
    G = HEADS // J
    N = 3 * G * HD
    F = up_weight.shape[1]
    rows = D // SPLIT
    low = jnp.bitwise_and(lax.axis_index("wide"), SPLIT - 1).astype(jnp.int32)
    meta = lengths
    cos, sin = rotary_tables(C)

    qkv_t = qkv_weight.transpose(1, 2, 0).reshape(N, D)
    qo = jnp.concatenate([qkv_weight.reshape(D, N), out_weight.T], axis=1)
    bias = jnp.concatenate([qkv_bias.reshape(-1), up_bias])
    bias = jnp.pad(bias, (0, 2 * D - bias.size)).reshape(2, D)
    cut = lambda x: lax.dynamic_slice_in_dim(x, low * rows, rows, 0)
    q_piece = jnp.concatenate([cut(qo), jnp.pad(bias, ((0, EXTRA - 2), (0, 0)))], axis=0)
    got = [fetch(q_piece, s) for s in range(1, J)]
    vec = jnp.stack([out_bias, norm1_gain, norm1_shift, down_bias, norm2_gain, norm2_shift]).astype(f32)
    b_own = qkv_bias.astype(f32).reshape(1, 3, G, HD).transpose(0, 2, 1, 3)
    ud_piece = jnp.concatenate([cut(up_weight), cut(down_weight)], axis=1)
    ud_got = [fetch(tie(ud_piece, q_piece), 1)]
    q0, k0, v0, e0, c0, l0, wt0, tok_t = attn_fwd(meta, [qkv_t, out_weight], (0, 1), tok, b_own, cos, sin, True)
    got, ud_got, tok_t = lax.optimization_barrier((got, ud_got, tok_t))
    biases = jnp.stack([bias] + [x[rows:rows + 2] for x in got]).reshape(J, 2 * D).astype(f32)
    bq, ub = biases[1:, :N].reshape(J - 1, 3, G, HD).transpose(0, 2, 1, 3), biases[:, N:N + F]
    q = jnp.stack([x[:rows] for x in got])
    q_near = [flip(q, rel) for rel in NEAR[1:]]
    ud_2, ud_3 = [fetch(tie(ud_piece, got), n) for n in (2, 3)]
    q_near, ud_2, ud_3, bq, ub, vec = lax.optimization_barrier((q_near, ud_2, ud_3, bq, ub, vec))
    q_near = [q] + q_near
    q_far = [flip(x, 1) for x in q_near]
    q_places = tuple((rel | low, 0, rows) for low in (0, 1) for rel in NEAR)
    q_far, ud_2, ud_3 = lax.optimization_barrier((q_far, ud_2, ud_3))
    ud = jnp.stack(ud_got + [ud_2, ud_3])
    q_pieces = q_near + q_far
    ud_near = [flip(ud, rel) for rel in NEAR[1:]]
    ud_far = [flip(ud, 1)]
    tok_t = tie(tok_t, ud)
    q1, k1, v1, e1, c1, l1, wt1 = attn_fwd(meta, q_pieces, q_places, tok_t, bq, cos, sin, False)
    ud_near, ud_far, c1 = lax.optimization_barrier((ud_near, ud_far, c1))
    ud_pieces = [ud] + ud_near + ud_far + [flip(x, 1) for x in ud_near]
    ud_places = [(rel | low, 0, rows) for low in (0, 1) for rel in NEAR]
    ud_layout = tuple(((0, 1), place) for place in ud_places)
    out, act, gu, hid_t, gl_t, g1, gol_t, do_t, small, ubg = ffn(
        meta, up_weight, down_weight, ud_pieces, ud_layout, tok, cot, (c0, c1), (wt0, wt1), vec, ub)

    whole = lambda a: pl.BlockSpec(a.shape, lambda j: (0,) * a.ndim, pipeline_mode=pl.Buffered(1))
    vecs = jnp.concatenate([jnp.broadcast_to(small[None, :6], (J, 6, D)), ubg[:, None], jnp.zeros((J, 1, D), f32)], axis=1)
    u_t, u_m = wgrad(
        wgrad_u_kernel, meta, (hid_t, gu, gol_t, c0, c1),
        [whole(hid_t), pl.BlockSpec((C, F), lambda j: (0, j)), whole(gol_t), pl.BlockSpec((G, HD, C), lambda j: (0, 0, 0)),
         pl.BlockSpec((G, HD, C), lambda j: (jnp.maximum(j - 1, 0), 0, 0))],
        J, rows, F + G * HD, [(SPLIT, rows, F), (SPLIT, rows, G * HD)], "wgrad_u", 2 * C * D * (J * F + D))
    u_1 = flip(u_t, 1)
    gl_t = tie(gl_t, u_t)
    d_t, d_m = wgrad(
        wgrad_d_kernel, meta, (gl_t, act, vecs),
        [whole(gl_t), pl.BlockSpec((C, F), lambda j: (0, j)), pl.BlockSpec((None, 8, D), lambda j: (j, 0, 0))],
        J, rows + EXTRA, F, [(SPLIT, rows, F)], "wgrad_d", 2 * C * D * J * F)

    def grad_q(gps, gb):
        n = gb.shape[0]
        one = pl.BlockSpec((None, N, C), lambda j: (j, 0, 0)) if len(gps) == 1 else pl.BlockSpec((None, N, C), lambda j: (0, 0, 0))
        return wgrad(
            wgrad_q_kernel, meta, (tok_t, *gps, gb), [whole(tok_t)] + [one] * len(gps) + [pl.BlockSpec((None, 1, N), lambda j: (j, 0, 0))],
            n, rows + EXTRA, N, [(SPLIT, rows, N)], "wgrad_q", 2 * C * D * n * N)

    def backward(group, count, do_t):
        saved, shift = ((e0, v0, c0, l0, q0, k0), 0) if group == 0 else ((e1, v1, c1, l1, q1, k1), G)
        gp, gb = attn_bwd(meta, saved, do_t, cos, sin, G, group * G - shift, shift, count * G)
        return gp.reshape(count, N, C), gb.reshape(count, G, 3, HD).transpose(0, 2, 1, 3).reshape(count, 1, N)

    def first(terms):
        return total([t[1] for t in terms]), [t[0] for t in terms]

    u_1, u_m, d_t = lax.optimization_barrier((u_1, u_m, d_t))
    d_1 = flip(d_t, 1)
    u_s, u_k = first([u_m, u_1])
    u_2 = flip(u_s, 4)
    do_t = tie(do_t, u_s)
    d_1, d_m, do_t = lax.optimization_barrier((d_1, d_m, do_t))
    d_s, d_k = first([d_m, d_1])
    d_2 = flip(d_s, 2)
    do_t = tie(do_t, d_s)
    gpa, gba = backward(1, 2, do_t)
    u_2, d_2, gpa, do_t = lax.optimization_barrier((u_2, d_2, gpa, do_t))
    u_s, u_k = first(u_k + [u_2])
    u_3 = flip(u_s, 2)
    d_s, d_k = first(d_k + [d_2])
    d_3 = flip(d_s, 4)
    gpa_ = tie(gpa, (u_s, d_s))
    qa_t, qa_m = grad_q((gpa_,), gba)
    qa_1 = flip(qa_t, 1)
    do_t = tie(do_t, qa_t)
    gpb, gbb = backward(0, 1, do_t)
    u_3, d_3, qa_1, gpb, do_t = lax.optimization_barrier((u_3, d_3, qa_1, gpb, do_t))
    du_s = [jnp.concatenate([total([t[j] for t in d_k + [d_3]]), jnp.pad(total([t[j] for t in u_k + [u_3]]), ((0, EXTRA), (0, 0)))], axis=1)
            for j in range(J)]
    du_3 = [give(du_s[s], s) for s in (1, 3)]
    qa_s, qa_k = first([qa_m, qa_1])
    qa_2 = flip(qa_s, 2)
    do_t = tie(do_t, (du_s, qa_s))
    gpc, gbc = backward(3, 1, do_t)
    du_3, qa_2, gpb, gpc = lax.optimization_barrier((du_3, qa_2, gpb, gpc))
    qa_s, qa_k = first(qa_k + [qa_2])
    qa_3 = flip(qa_s, 4)
    gpc_ = tie(gpc, qa_s)
    du_2 = give(tie(du_s[2], qa_s), 2)
    qb_t, qb_m = grad_q((gpb, gpc_), jnp.concatenate([gbb, gbc], axis=0))
    qb_1 = flip(qb_t, 1)
    qa_3, du_2, qb_t, qb_m = lax.optimization_barrier((qa_3, du_2, qb_t, qb_m))
    du = rest(total([du_s[0], du_2] + du_3))
    du_x, du_y = flip(du, 2), flip(du, 4)
    qa_s = [total([t[j] for t in qa_k + [qa_3]]) for j in range(2)]
    q_3 = [give(qa_s[0], 1), give(qa_s[1], 2)]
    g1 = tie(g1, (qb_t, qa_s, du))
    x_grad = input_grad([gpb, gpa, gpc], wt0, wt1, g1, 0, C // 768)
    qb_1, qb_m, q_3, x_grad = lax.optimization_barrier((qb_1, qb_m, q_3, x_grad))
    qb_s = [total([t[i // 2, i % 2] for t in (qb_m, qb_1)]) for i in range(1, 4)]
    qb_k = [t[0, 0] for t in (qb_m, qb_1)]
    qb_2 = [flip(x, rel) for x, rel in zip(qb_s, SWAP[1:])]
    g1, x_grad = tie((g1, x_grad), qb_s)
    x_grad = input_grad([gpb, gpa, gpc], wt0, wt1, g1, C // 768, C // 256 - C // 768, x_grad)
    qb_2, du_x, du_y, x_grad = lax.optimization_barrier((qb_2, du_x, du_y, x_grad))
    cut_at = du.shape[0] // 16 * 8
    du_d = [flip(du_y[:cut_at], 2), flip(du_x[cut_at:], 4)]
    qb = total(qb_k + qb_2)
    q_3.append(give(qb[1], J - 1))
    q_3, du_d = lax.optimization_barrier((q_3, du_d))
    q = rest(total([qb[0]] + q_3))
    q_4 = [flip(q, rel) for rel in NEAR[1:]]
    du = jnp.stack([du, du_x, du_y, jnp.concatenate(du_d, axis=0)])
    du_5 = flip(du, 1)
    q_4, du_5 = lax.optimization_barrier((q_4, du_5))
    q = jnp.stack([q] + q_4)
    q_5 = flip(q, 1)
    du = tie(du, q)
    down_g, up_g, ow_g, small = final(
        final_du_kernel, meta, (du, du_5), [(F, D), (D, F), (G * HD, D), (8, D)], [(SPLIT, rows, F), (SPLIT, rows, G * HD)], "final_du")
    q_5, down_g = lax.optimization_barrier((q_5, down_g))
    qkv_g, gb = final(final_q_kernel, meta, (q, q_5), [(N, D), (1, N)], [(SPLIT, rows, N)], "final_q")
    return (
        out[None], x_grad[None], qkv_g.reshape(3, G * HD, D).transpose(2, 0, 1), gb.reshape(3, G * HD), ow_g, small[5], small[3], small[4],
        up_g, small[6], down_g, small[2], small[0], small[1],
    )


def solution(mesh):
    rows = P(("wide", "narrow"), None, None)
    weights = (P(None, None, "narrow"), P(None, "narrow"), P("narrow", None), P(), P(), P(),
               P(None, "narrow"), P("narrow"), P("narrow", None), P(), P(), P())
    return jax.shard_map(
        shards, mesh=mesh, in_specs=(rows, P("wide", None)) + weights + (rows,),
        out_specs=(rows, rows) + weights, check_vma=False,
    )
```

```python
import functools

import jax
import jax.numpy as jnp
from jax import lax
from jax.experimental import pallas as pl
from jax.experimental.pallas import tpu as pltpu
from jax.sharding import PartitionSpec as P

bf = jnp.bfloat16
f32 = jnp.float32
LOG2E = 1.4426950408889634
HEADS = 12
HD = 64
SPLIT = 8
EXTRA = 8
MIB = 1 << 20


def dg(a, b, ca, cb):
    return lax.dot_general(a, b, (((ca,), (cb,)), ((), ())), preferred_element_type=f32)


def mean(x):
    return jnp.mean(x, axis=-1, keepdims=True)


def shape(s, d):
    return jax.ShapeDtypeStruct(s, d)


SMEM = pl.BlockSpec(memory_space=pltpu.SMEM)
ANY = pl.BlockSpec(memory_space=pl.ANY)


def length_of(lengths):
    return lengths[0, lax.axis_index("narrow")]


def low_bits():
    return jnp.bitwise_and(lax.axis_index("wide"), SPLIT - 1)


def params(mib):
    return pltpu.CompilerParams(vmem_limit_bytes=mib * MIB)


def cost(flops, nbytes):
    return pl.CostEstimate(flops=1, bytes_accessed=1, transcendentals=0)


def put_piece(meta, src, g, lanes, place, dst, sem):
    rel, half, whole = place
    rows = src.shape[1]
    at = 0 if rel is None else (low_bits() ^ rel) * whole + half
    return pltpu.make_async_copy(src.at[g, :, lanes], dst.at[pl.ds(pl.multiple_of(at, 16), rows), :], sem)


def attn_fwd_kernel(meta, *refs, C, KC, G, layout, own):
    pieces, refs = refs[:len(layout)], refs[len(layout):]
    x, b, cos, sin, q_t, k_t, v_d, e, ctx, exact, linv, w_t, *rest = refs
    if own:
        x_t, Q2, KD, VA, S, W, flag, sem = rest
    else:
        x_t, (Q2, KD, VA, S, W, flag, sem) = x, rest
    h = pl.program_id(0)
    length = length_of(meta)

    if own:
        @pl.when(h == 0)
        def _():
            x_t[...] = x[...].T
            n = pieces[0].shape[0]
            w_t[:n, :] = pieces[0][...]
            w_t[n:, :] = pieces[1][...]
    else:
        groups = pieces[0].shape[0]

        def copies(g):
            return [put_piece(meta, pieces[t], g, slice(None), layout[t], W.at[g], sem.at[g, t]) for t in range(len(pieces))]

        @pl.when(h == 0)
        def _():
            for g in range(groups):
                for c in copies(g):
                    c.start()

        @pl.when(lax.rem(h, G) == 0)
        def _():
            g = lax.div(h, G)
            for c in copies(g):
                c.wait()
            w_t[...] = W[g].T

    at = lax.rem(h, G)
    w = jnp.concatenate([w_t[pl.ds(pl.multiple_of((p * G + at) * HD, HD), HD), :] for p in range(3)], axis=0)
    bias = [jnp.broadcast_to(b[i:i + 1, :], (2 * HD, HD)).T[:, :1] for i in range(3)]
    p = dg(w, x_t[...], 1, 0) + jnp.concatenate(bias, axis=0)
    c, d = cos[...], sin[...]

    def rot(v):
        u, z = v[:HD // 2], v[HD // 2:]
        return jnp.concatenate([u * c - z * d, z * c + u * d], axis=0)

    live = lax.broadcasted_iota(jnp.int32, (HD, C), 1) < length
    q = rot(p[:HD]).astype(bf).astype(f32)
    k = jnp.where(live, rot(p[HD:2 * HD]), 0.0).astype(bf)
    v = jnp.where(live, p[2 * HD:], 0.0).astype(bf)
    q_t[...] = (q * 0.125).astype(bf)
    q = q * (0.125 * LOG2E)
    hi = q.astype(bf)
    Q2[:HD, :] = hi
    Q2[HD:, :] = (q - hi.astype(f32)).astype(bf)
    k_t[...] = k
    KD[...] = jnp.concatenate([k, k], axis=0).T
    v_d[...] = jnp.concatenate([v, v], axis=0).T
    VA[:HD, :] = v
    VA[HD:, :] = jnp.where(live[:16], 1.0, 0.0).astype(bf)
    kf = k.astype(f32)
    qn = jnp.max(jnp.sum(q * q, axis=0, keepdims=True))
    kn = jnp.max(jnp.sum(kf * kf, axis=0, keepdims=True))
    flag[0] = (qn * kn <= 1e4).astype(jnp.int32)

    @pl.when(flag[0] == 1)
    def _():
        for j in range(C // KC):
            r = slice(j * KC, (j + 1) * KC)
            e[r, :] = jnp.exp2(dg(KD[r, :], Q2[...], 1, 0)).astype(bf)

    @pl.when(flag[0] == 0)
    def _():
        BQ = S.shape[1]

        def block(i, carry):
            cols = pl.ds(pl.multiple_of(i * BQ, BQ), BQ)

            def score(j, m):
                r = pl.ds(pl.multiple_of(j * KC, KC), KC)
                keys = lax.broadcasted_iota(jnp.int32, (KC, BQ), 0) + j * KC
                x = jnp.where(keys < length, dg(KD[r, :], Q2[:, cols], 1, 0), -1e30)
                S[r, :] = x
                return jnp.maximum(m, jnp.max(x, axis=0, keepdims=True))

            m = lax.fori_loop(0, C // KC, score, jnp.full((1, BQ), -1e30, f32))

            def power(j, carry):
                r = pl.ds(pl.multiple_of(j * KC, KC), KC)
                e[r, cols] = jnp.exp2(S[r, :] - m).astype(bf)
                return carry

            return lax.fori_loop(0, C // KC, power, carry)

        lax.fori_loop(0, C // BQ, block, 0)

    o = dg(VA[...], e[...], 1, 0)
    inv = 1.0 / o[HD:HD + 1]
    linv[...] = inv
    o = o[:HD] * inv
    exact[...] = o
    ctx[...] = o.astype(bf)


def attn_fwd(meta, pieces, layout, x, b, cos, sin, own):
    groups, _, D = pieces[0].shape if not own else (1,) + pieces[0].shape
    C = x.shape[0] if own else x.shape[1]
    G = b.shape[1]
    H = groups * G
    at = lambda h: (h, 0, 0)
    fix = lambda a: pl.BlockSpec(a.shape, lambda h: (0,) * a.ndim, pipeline_mode=pl.Buffered(1))
    hb = pl.BlockSpec((None, HD, C), at)
    out_specs = [hb, hb, pl.BlockSpec((None, C, 2 * HD), at), pl.BlockSpec((None, C, C), at), hb, hb,
                 pl.BlockSpec((None, 1, C), at), pl.BlockSpec((None, D, D), lambda h: (h // G, 0, 0))]
    out_shape = [shape((H, HD, C), bf), shape((H, HD, C), bf), shape((H, C, 2 * HD), bf), shape((H, C, C), bf),
                 shape((H, HD, C), bf), shape((H, HD, C), f32), shape((H, 1, C), f32), shape((groups, D, D), bf)]
    if own:
        out_specs.append(pl.BlockSpec((D, C), lambda h: (0, 0)))
        out_shape.append(shape((D, C), bf))
    return pl.pallas_call(
        functools.partial(attn_fwd_kernel, C=C, KC=min(128, C), G=G, layout=layout, own=own), grid=(H,),
        in_specs=[SMEM] + ([fix(p) for p in pieces] if own else [ANY] * len(pieces))
        + [fix(x), pl.BlockSpec((None, None, 3, HD), lambda h: (h // G, h % G, 0, 0)), fix(cos), fix(sin)],
        out_specs=out_specs, out_shape=out_shape,
        scratch_shapes=[pltpu.VMEM((2 * HD, C), bf), pltpu.VMEM((C, 2 * HD), bf), pltpu.VMEM((HD + 16, C), bf),
                        pltpu.VMEM((C, C // 3 if C % 384 == 0 else C), f32), pltpu.VMEM((8, 128) if own else (groups, D, D), bf),
                        pltpu.SMEM((1,), jnp.int32), pltpu.SemaphoreType.DMA((groups, len(pieces)))],
        compiler_params=params(60), cost_estimate=cost(H * (4 * C * C * 256 + 2 * C * D * 3 * HD), H * C * C * 2 + 8 * MIB),
        name="attn_fwd_own" if own else "attn_fwd",
    )(meta, *pieces, x, b, cos, sin)


def ffn_kernel(meta, u_own, d_own, *refs, R, layout):
    pieces, refs = refs[:len(layout)], refs[len(layout):]
    tok, cot, *refs = refs
    J = pieces[0].shape[0] + 1
    ctxs, ows, refs = refs[:2], refs[2:4], refs[4:]
    (vec, ub, out, act, gu, hid_t, gl_t, g1_o, gol_t, do_t, small, ubg, G, U, Dn, sem) = refs
    i = pl.program_id(0)
    groups = J - 1

    def copies():
        cs = [pltpu.make_async_copy(u_own, U.at[0], sem.at[0, 0, 0]), pltpu.make_async_copy(d_own, Dn.at[0], sem.at[1, 0, 0])]
        for g in range(groups):
            for t, (piece, (parts, place)) in enumerate(zip(pieces, layout)):
                for k, s in enumerate(parts):
                    lanes = slice(k * U.shape[2], (k + 1) * U.shape[2])
                    cs.append(put_piece(meta, piece, g, lanes, place, (U, Dn)[s].at[g + 1], sem.at[s, g + 1, t]))
        return cs

    @pl.when(i == 0)
    def _():
        for c in copies():
            c.start()
        small[...] = jnp.zeros_like(small)
        ubg[...] = jnp.zeros_like(ubg)

    ob, g1, s1, db, g2, s2 = [vec[k:k + 1, :] for k in range(6)]
    D = tok.shape[1]
    F = U.shape[2]

    def csum(k, x):
        small[k:k + 1, :] += jnp.sum(x, axis=0, keepdims=True)

    ow = jnp.concatenate([w[g] for w in ows for g in range(w.shape[0])], axis=0)
    ctx = jnp.concatenate([c[...].reshape(-1, R) for c in ctxs], axis=0)
    pre = tok[...].astype(f32) + dg(ctx.T, ow, 1, 0) + ob
    cen = pre - mean(pre)
    r1 = lax.rsqrt(mean(cen * cen) + 1e-6)
    n1 = cen * r1
    hid = n1 * g1 + s1
    hl = hid.astype(bf)
    hid_t[...] = hl.T
    acc = hid + db

    @pl.when(i == 0)
    def _():
        for c in copies():
            c.wait()

    for j in range(J):
        u = dg(hl, U[j], 1, 0) + ub[j:j + 1, :]
        phi = 0.5 * lax.erf(u * 0.7071067811865476) + 0.5
        a = (u * phi).astype(bf)
        act[:, j * F:(j + 1) * F] = a
        G[:, j * F:(j + 1) * F] = phi + u * (jnp.exp2(u * u * -0.7213475204444817) * 0.3989422804014327)
        acc = acc + dg(a, Dn[j], 1, 0)
    cen = acc - mean(acc)
    r2 = lax.rsqrt(mean(cen * cen) + 1e-6)
    n2 = cen * r2
    out[...] = (n2 * g2 + s2).astype(bf)
    c = cot[...].astype(f32)
    csum(0, c * n2)
    csum(1, c)
    sg = c * g2
    gt = r2 * (sg - mean(sg) - n2 * mean(sg * n2))
    csum(2, gt)
    gl = gt.astype(bf)
    gl_t[...] = gl.T
    dh = gt
    for j in range(J):
        g = dg(gl, Dn[j], 1, 1) * G[:, j * F:(j + 1) * F]
        ubg[j:j + 1, :] += jnp.sum(g, axis=0, keepdims=True)
        gb = g.astype(bf)
        gu[:, j * F:(j + 1) * F] = gb
        dh = dh + dg(gb, U[j], 1, 1)
    csum(3, dh * n1)
    csum(4, dh)
    sg = dh * g1
    go = r1 * (sg - mean(sg) - n1 * mean(sg * n1))
    csum(5, go)
    g1_o[...] = go
    gol = go.astype(bf)
    gol_t[...] = gol.T
    do_t[...] = dg(ow, gol, 1, 1).astype(bf).reshape(do_t.shape)


def ffn(meta, u_own, d_own, pieces, layout, tok, cot, ctxs, wts, vec, ub, R=512):
    C, D = tok.shape
    J, F = ub.shape
    H = HEADS
    row = lambda w: pl.BlockSpec((R, w), lambda i: (i, 0))
    col = pl.BlockSpec((D, R), lambda i: (0, i))
    fix = lambda a: pl.BlockSpec(a.shape, lambda i: (0,) * a.ndim, pipeline_mode=pl.Buffered(1))
    hb = lambda n: pl.BlockSpec((n, HD, R), lambda i: (0, 0, i))
    acc = lambda s: pl.BlockSpec(s, lambda i: (0, 0))
    share = H // J * HD
    at = 3
    owb = lambda w: pl.BlockSpec((w.shape[0], share, D), lambda i: (0, at, 0), pipeline_mode=pl.Buffered(1))
    return pl.pallas_call(
        functools.partial(ffn_kernel, R=R, layout=layout), grid=(C // R,),
        in_specs=[SMEM, ANY, ANY] + [ANY] * len(pieces) + [row(D), row(D)] + [hb(c.shape[0]) for c in ctxs] + [owb(w) for w in wts] + [fix(vec), fix(ub)],
        out_specs=[row(D), row(J * F), row(J * F), col, col, row(D), col, hb(H), acc((8, D)), acc((J, F))],
        out_shape=[shape((C, D), bf), shape((C, J * F), bf), shape((C, J * F), bf), shape((D, C), bf), shape((D, C), bf), shape((C, D), f32),
                   shape((D, C), bf), shape((H, HD, C), bf), shape((8, D), f32), shape((J, F), f32)],
        scratch_shapes=[pltpu.VMEM((R, J * F), f32), pltpu.VMEM((J, D, F), bf), pltpu.VMEM((J, F, D), bf),
                        pltpu.SemaphoreType.DMA((2, J, len(pieces)))],
        compiler_params=params(60), cost_estimate=cost(2 * C * D * (2 * D + 4 * J * F), 60 * MIB), name="ffn",
    )(meta, u_own, d_own, *pieces, tok, cot, *ctxs, *wts, vec, ub)


def attn_bwd_kernel(meta, e, v_d, do_t, ctx, linv, q_t, k_t, cos, sin, gp, gb, D2, DI, DS, DST, ET, *, C, KC):
    length = length_of(meta)
    g = do_t[...].astype(f32)
    inv = linv[...]
    DI[...] = jnp.sum(g * ctx[...], axis=0, keepdims=True) * inv
    g = g * inv
    hi = g.astype(bf)
    D2[:HD, :] = hi
    D2[HD:, :] = (g - hi.astype(f32)).astype(bf)
    for j in range(C // KC):
        r = slice(j * KC, (j + 1) * KC)
        dp = dg(v_d[r, :], D2[...], 1, 0)
        ej = e[r, :]
        ds = (ej.astype(f32) * (dp - DI[...])).astype(bf)
        DS[r, :] = ds
        DST[:, r] = ds.T
        ET[:, r] = ej.T
    dq = dg(k_t[...], DS[...], 1, 0)
    dk = dg(q_t[...], DST[...], 1, 0)
    dv = dg(D2[:HD, :], ET[...], 1, 0)
    live = lax.broadcasted_iota(jnp.int32, (HD, C), 1) < length
    c, s = cos[...], sin[...]

    def unrot(x):
        u, w = x[:HD // 2], x[HD // 2:]
        return jnp.concatenate([u * c + w * s, w * c - u * s], axis=0)

    def put(k, x):
        gp[k] = x.astype(bf)
        total = jnp.sum(x, axis=1, keepdims=True)
        gb[k:k + 1, :] = jnp.broadcast_to(total, (HD, 2 * HD)).T[:1]

    put(0, unrot(dq * 0.125))
    put(1, unrot(jnp.where(live, dk, 0.0)))
    put(2, jnp.where(live, dv, 0.0))


def attn_bwd(meta, saved, do_t, cos, sin, G, first, shift, H):
    e, v_d, ctx, linv, q_t, k_t = saved
    C = e.shape[1]
    sp = lambda s: pl.BlockSpec((None,) + s, lambda h: (h + first, 0, 0))
    tab = pl.BlockSpec((HD // 2, C), lambda h: (0, 0))
    return pl.pallas_call(
        functools.partial(attn_bwd_kernel, C=C, KC=min(256, C)), grid=(H,),
        in_specs=[SMEM, sp((C, C)), sp((C, 2 * HD)), pl.BlockSpec((None, HD, C), lambda h: (h + first + shift, 0, 0)), sp((HD, C)), sp((1, C)),
                  sp((HD, C)), sp((HD, C)), tab, tab],
        out_specs=[pl.BlockSpec((None, 3, None, HD, C), lambda h: (h // G, 0, h % G, 0, 0)), pl.BlockSpec((None, 3, HD), lambda h: (h, 0, 0))],
        out_shape=[shape((H // G, 3, G, HD, C), bf), shape((H, 3, HD), f32)],
        scratch_shapes=[pltpu.VMEM((2 * HD, C), bf), pltpu.VMEM((1, C), f32)] + [pltpu.VMEM((C, C), bf)] * 3,
        compiler_params=params(60), cost_estimate=cost(H * 8 * C * C * 256, H * C * C * 2 + 16 * MIB), name="attn_bwd",
    )(meta, e, v_d, do_t, ctx, linv, q_t, k_t, cos, sin)


NEAR = (0, 2, 4, 6)
SWAP = (0, 4, 2, 6)


def lay(meta, S, theirs, mine, rows, lanes, order):
    for i, rel in enumerate(order):
        for ref, low in ((mine, 0), (theirs, 1)):
            ref[i // 2, i % 2, 0, rows, lanes] = S[low_bits() ^ (rel | low)].astype(bf)


def wgrad_d_kernel(meta, gl_t, act, vecs, theirs, mine, S):
    rows = S.shape[1]
    S[...] = dg(gl_t[...], act[...], 1, 0).reshape(S.shape)
    lay(meta, S, theirs, mine, slice(0, rows), slice(None), SWAP)
    for i, rel in enumerate(SWAP):
        for ref, low in ((mine, 0), (theirs, 1)):
            line = vecs[pl.ds(low_bits() ^ (rel | low), 1), :]
            ref[i // 2, i % 2, 0, rows:, :] = jnp.broadcast_to(line, (EXTRA, line.shape[1])).astype(bf)


def wgrad_u_kernel(meta, hid_t, gu, gol_t, *refs):
    c0, c1, theirs, mine, S, SO = refs
    F = gu.shape[1]
    S[...] = dg(hid_t[...], gu[...], 1, 0).reshape(S.shape)
    lay(meta, S, theirs, mine, slice(None), slice(0, F), NEAR)

    def out(ctx):
        SO[...] = dg(gol_t[...], ctx[...].reshape(-1, ctx.shape[-1]), 1, 1).reshape(SO.shape)

    pl.when(pl.program_id(0) == 0)(lambda: out(c0))
    pl.when(pl.program_id(0) > 0)(lambda: out(c1))
    lay(meta, SO, theirs, mine, slice(None), slice(F, F + SO.shape[2]), NEAR)


def wgrad_q_kernel(meta, tok_t, *refs):
    gps, (gb, theirs, mine, S) = refs[:-4], refs[-4:]
    rows = S.shape[1]
    if len(gps) == 1:
        S[...] = dg(tok_t[...], gps[0][...], 1, 1).reshape(S.shape)
    for j, gp in enumerate(gps if len(gps) > 1 else ()):
        @pl.when(pl.program_id(0) == j)
        def _(gp=gp):
            S[...] = dg(tok_t[...], gp[...], 1, 1).reshape(S.shape)

    lay(meta, S, theirs, mine, slice(0, rows), slice(None), SWAP)
    line = jnp.broadcast_to(gb[...], (EXTRA, gb.shape[1])).astype(bf)
    for i in range(4):
        for ref in (mine, theirs):
            ref[i // 2, i % 2, 0, rows:, :] = line


def wgrad(kernel, meta, args, specs, J, rows, lanes, scratch, name, flops):
    spec = pl.BlockSpec((2, 2, 1, rows, lanes), lambda j: (0, 0, j, 0, 0))
    return pl.pallas_call(
        kernel, grid=(J,), in_specs=[SMEM] + specs, out_specs=[spec] * 2, out_shape=[shape((2, 2, J, rows, lanes), bf)] * 2,
        scratch_shapes=[pltpu.VMEM(s, f32) for s in scratch],
        compiler_params=params(28), cost_estimate=cost(flops, 20 * MIB), name=name,
    )(meta, *[pltpu.with_memory_space_constraint(x, pltpu.HBM) for x in args])


def final_du_kernel(meta, x, y, down, up, ow, small, S, SO):
    rows = S.shape[1]
    F = up.shape[1]
    for low, ref in enumerate((x, y)):
        for t, rel in enumerate(NEAR):
            at = low_bits() ^ (rel | low)
            S[at] = ref[t, :rows, :F].astype(f32)
            small[pl.ds(at, 1), :] = ref[t, rows:rows + 1, :F].astype(f32)
            up[pl.ds(pl.multiple_of(at * rows, rows), rows), :] = ref[t, :rows, F:2 * F].astype(f32)
            SO[at] = ref[t, :rows, 2 * F:].astype(f32)
    down[...] = S[...].reshape(down.shape).T
    ow[...] = SO[...].reshape(-1, SO.shape[2]).T


def final_q_kernel(meta, x, y, qkv, gb, S):
    rows = x.shape[1] - EXTRA
    for low, ref in enumerate((x, y)):
        for t, rel in enumerate(NEAR):
            S[low_bits() ^ (rel | low)] = ref[t, :rows, :].astype(f32)
    qkv[...] = S[...].reshape(-1, S.shape[2]).T
    gb[...] = x[0, rows:rows + 1, :].astype(f32)


def final(kernel, meta, xs, outs, scratch, name):
    return pl.pallas_call(
        kernel, in_specs=[SMEM] + [pl.BlockSpec(memory_space=pltpu.VMEM)] * 2,
        out_shape=[shape(s, f32) for s in outs], scratch_shapes=[pltpu.VMEM(s, f32) for s in scratch],
        compiler_params=params(60), cost_estimate=cost(0, 8 * MIB), name=name,
    )(meta, *xs)


def input_grad_kernel(*refs, N, n):
    gps, (w0, w1, g1, *_, out) = refs[:n], refs[n:]
    acc = g1[...]
    j = 0
    for gp in gps:
        for i in range(gp.shape[0]):
            w = w0[0, :N, :] if j == 0 else w1[j - 1, :N, :]
            acc = acc + dg(gp[i], w, 0, 0)
            j += 1
    out[...] = acc


def input_grad(gps, w0, w1, g1, first, count, before=None, R=256):
    _, N, C = gps[0].shape
    D = g1.shape[1]
    fix = lambda a: pl.BlockSpec(a.shape, lambda i: (0,) * a.ndim, pipeline_mode=pl.Buffered(1))
    row = pl.BlockSpec((R, D), lambda i: (i + first, 0))
    more = [] if before is None else [before]
    return pl.pallas_call(
        functools.partial(input_grad_kernel, N=N, n=len(gps)), grid=(count,),
        in_specs=[pl.BlockSpec((g.shape[0], N, R), lambda i: (0, 0, i + first)) for g in gps] + [fix(w0), fix(w1), row] + [ANY] * len(more),
        out_specs=row, out_shape=shape((C, D), f32), input_output_aliases={len(gps) + 3: 0} if more else {},
        compiler_params=params(28), cost_estimate=cost(2 * C * D * D * 3, 24 * MIB), name="input_grad",
    )(*gps, w0, w1, g1, *more)


def fetch(x, s):
    n = lax.axis_size("narrow")
    return lax.ppermute(x, "narrow", [((i + s) % n, i) for i in range(n)])


def give(x, s):
    n = lax.axis_size("narrow")
    return lax.ppermute(x, "narrow", [(i, (i + s) % n) for i in range(n)])


def flip(x, bit):
    return lax.ppermute(x, "wide", [(i, i ^ bit) for i in range(lax.axis_size("wide"))])


def total(terms):
    x = terms[0].astype(f32)
    for y in terms[1:]:
        x = x + y.astype(f32)
    return x.astype(bf)


def rest(x):
    bit = SPLIT
    while bit < lax.axis_size("wide"):
        x = add(x, flip(x, bit))
        bit *= 2
    return x


def tie(xs, deps):
    return lax.optimization_barrier((xs, deps))[0]


def add(a, b):
    return (a.astype(f32) + b.astype(f32)).astype(bf)


def rotary_tables(capacity):
    positions = jnp.arange(capacity).astype(f32)
    frequencies = 10000.0 ** (-2.0 * jnp.arange(HD // 2).astype(f32) / HD)
    angles = frequencies[:, None] * positions[None, :]
    return jnp.cos(angles), jnp.sin(angles)


def shards(
    tokens, lengths, qkv_weight, qkv_bias, out_weight, out_bias, norm1_gain, norm1_shift,
    up_weight, up_bias, down_weight, down_bias, norm2_gain, norm2_shift, cotangent,
):
    J = lax.axis_size("narrow")
    tok, cot = tokens[0], cotangent[0]
    C, D = tok.shape
    G = HEADS // J
    N = 3 * G * HD
    F = up_weight.shape[1]
    rows = D // SPLIT
    low = jnp.bitwise_and(lax.axis_index("wide"), SPLIT - 1).astype(jnp.int32)
    meta = lengths
    cos, sin = rotary_tables(C)

    qkv_t = qkv_weight.transpose(1, 2, 0).reshape(N, D)
    qo = jnp.concatenate([qkv_weight.reshape(D, N), out_weight.T], axis=1)
    bias = jnp.concatenate([qkv_bias.reshape(-1), up_bias])
    bias = jnp.pad(bias, (0, 2 * D - bias.size)).reshape(2, D)
    cut = lambda x: lax.dynamic_slice_in_dim(x, low * rows, rows, 0)
    q_piece = jnp.concatenate([cut(qo), jnp.pad(bias, ((0, EXTRA - 2), (0, 0)))], axis=0)
    got = [fetch(q_piece, s) for s in range(1, J)]
    vec = jnp.stack([out_bias, norm1_gain, norm1_shift, down_bias, norm2_gain, norm2_shift]).astype(f32)
    b_own = qkv_bias.astype(f32).reshape(1, 3, G, HD).transpose(0, 2, 1, 3)
    ud_piece = jnp.concatenate([cut(up_weight), cut(down_weight)], axis=1)
    ud_got = [fetch(tie(ud_piece, q_piece), 1)]
    q0, k0, v0, e0, c0, o0, l0, wt0, tok_t = attn_fwd(meta, [qkv_t, out_weight], (0, 1), tok, b_own, cos, sin, True)
    got, ud_got, tok_t = lax.optimization_barrier((got, ud_got, tok_t))
    biases = jnp.stack([bias] + [x[rows:rows + 2] for x in got]).reshape(J, 2 * D).astype(f32)
    bq, ub = biases[1:, :N].reshape(J - 1, 3, G, HD).transpose(0, 2, 1, 3), biases[:, N:N + F]
    q = jnp.stack([x[:rows] for x in got])
    q_near = [flip(q, rel) for rel in NEAR[1:]]
    ud_2, ud_3 = [fetch(tie(ud_piece, got), n) for n in (2, 3)]
    q_near, ud_2, ud_3, bq, ub, vec = lax.optimization_barrier((q_near, ud_2, ud_3, bq, ub, vec))
    q_near = [q] + q_near
    q_far = [flip(x, 1) for x in q_near]
    q_places = tuple((rel | low, 0, rows) for low in (0, 1) for rel in NEAR)
    q_far, ud_2, ud_3 = lax.optimization_barrier((q_far, ud_2, ud_3))
    ud = jnp.stack(ud_got + [ud_2, ud_3])
    q_pieces = q_near + q_far
    ud_near = [flip(ud, rel) for rel in NEAR[1:]]
    ud_far = [flip(ud, 1)]
    tok_t = tie(tok_t, ud)
    q1, k1, v1, e1, c1, o1, l1, wt1 = attn_fwd(meta, q_pieces, q_places, tok_t, bq, cos, sin, False)
    ud_near, ud_far, c1 = lax.optimization_barrier((ud_near, ud_far, c1))
    ud_pieces = [ud] + ud_near + ud_far + [flip(x, 1) for x in ud_near]
    ud_places = [(rel | low, 0, rows) for low in (0, 1) for rel in NEAR]
    ud_layout = tuple(((0, 1), place) for place in ud_places)
    out, act, gu, hid_t, gl_t, g1, gol_t, do_t, small, ubg = ffn(
        meta, up_weight, down_weight, ud_pieces, ud_layout, tok, cot, (c0, c1), (wt0, wt1), vec, ub)

    whole = lambda a: pl.BlockSpec(a.shape, lambda j: (0,) * a.ndim, pipeline_mode=pl.Buffered(1))
    vecs = jnp.concatenate([jnp.broadcast_to(small[None, :6], (J, 6, D)), ubg[:, None], jnp.zeros((J, 1, D), f32)], axis=1)
    u_t, u_m = wgrad(
        wgrad_u_kernel, meta, (hid_t, gu, gol_t, c0, c1),
        [whole(hid_t), pl.BlockSpec((C, F), lambda j: (0, j)), whole(gol_t), pl.BlockSpec((G, HD, C), lambda j: (0, 0, 0)),
         pl.BlockSpec((G, HD, C), lambda j: (jnp.maximum(j - 1, 0), 0, 0))],
        J, rows, F + G * HD, [(SPLIT, rows, F), (SPLIT, rows, G * HD)], "wgrad_u", 2 * C * D * (J * F + D))
    u_1 = flip(u_t, 1)
    gl_t = tie(gl_t, u_t)
    d_t, d_m = wgrad(
        wgrad_d_kernel, meta, (gl_t, act, vecs),
        [whole(gl_t), pl.BlockSpec((C, F), lambda j: (0, j)), pl.BlockSpec((None, 8, D), lambda j: (j, 0, 0))],
        J, rows + EXTRA, F, [(SPLIT, rows, F)], "wgrad_d", 2 * C * D * J * F)

    def grad_q(gps, gb):
        n = gb.shape[0]
        one = pl.BlockSpec((None, N, C), lambda j: (j, 0, 0)) if len(gps) == 1 else pl.BlockSpec((None, N, C), lambda j: (0, 0, 0))
        return wgrad(
            wgrad_q_kernel, meta, (tok_t, *gps, gb), [whole(tok_t)] + [one] * len(gps) + [pl.BlockSpec((None, 1, N), lambda j: (j, 0, 0))],
            n, rows + EXTRA, N, [(SPLIT, rows, N)], "wgrad_q", 2 * C * D * n * N)

    def backward(group, count, do_t):
        saved, shift = ((e0, v0, o0, l0, q0, k0), 0) if group == 0 else ((e1, v1, o1, l1, q1, k1), G)
        gp, gb = attn_bwd(meta, saved, do_t, cos, sin, G, group * G - shift, shift, count * G)
        return gp.reshape(count, N, C), gb.reshape(count, G, 3, HD).transpose(0, 2, 1, 3).reshape(count, 1, N)

    def first(terms):
        return total([t[1] for t in terms]), [t[0] for t in terms]

    u_1, u_m, d_t = lax.optimization_barrier((u_1, u_m, d_t))
    d_1 = flip(d_t, 1)
    u_s, u_k = first([u_m, u_1])
    u_2 = flip(u_s, 4)
    do_t = tie(do_t, u_s)
    d_1, d_m, do_t = lax.optimization_barrier((d_1, d_m, do_t))
    d_s, d_k = first([d_m, d_1])
    d_2 = flip(d_s, 2)
    do_t = tie(do_t, d_s)
    gpa, gba = backward(1, 2, do_t)
    u_2, d_2, gpa, do_t = lax.optimization_barrier((u_2, d_2, gpa, do_t))
    u_s, u_k = first(u_k + [u_2])
    u_3 = flip(u_s, 2)
    d_s, d_k = first(d_k + [d_2])
    d_3 = flip(d_s, 4)
    gpa_ = tie(gpa, (u_s, d_s))
    qa_t, qa_m = grad_q((gpa_,), gba)
    qa_1 = flip(qa_t, 1)
    do_t = tie(do_t, qa_t)
    gpb, gbb = backward(0, 1, do_t)
    u_3, d_3, qa_1, gpb, do_t = lax.optimization_barrier((u_3, d_3, qa_1, gpb, do_t))
    du_s = [jnp.concatenate([total([t[j] for t in d_k + [d_3]]), jnp.pad(total([t[j] for t in u_k + [u_3]]), ((0, EXTRA), (0, 0)))], axis=1)
            for j in range(J)]
    du_3 = [give(du_s[s], s) for s in (1, 3)]
    qa_s, qa_k = first([qa_m, qa_1])
    qa_2 = flip(qa_s, 2)
    do_t = tie(do_t, (du_s, qa_s))
    gpc, gbc = backward(3, 1, do_t)
    du_3, qa_2, gpb, gpc = lax.optimization_barrier((du_3, qa_2, gpb, gpc))
    qa_s, qa_k = first(qa_k + [qa_2])
    qa_3 = flip(qa_s, 4)
    gpc_ = tie(gpc, qa_s)
    du_2 = give(tie(du_s[2], qa_s), 2)
    qb_t, qb_m = grad_q((gpb, gpc_), jnp.concatenate([gbb, gbc], axis=0))
    qb_1 = flip(qb_t, 1)
    qa_3, du_2, qb_t, qb_m = lax.optimization_barrier((qa_3, du_2, qb_t, qb_m))
    du = rest(total([du_s[0], du_2] + du_3))
    du_x, du_y = flip(du, 2), flip(du, 4)
    qa_s = [total([t[j] for t in qa_k + [qa_3]]) for j in range(2)]
    q_3 = [give(qa_s[0], 1), give(qa_s[1], 2)]
    g1 = tie(g1, (qb_t, qa_s, du))
    x_grad = input_grad([gpb, gpa, gpc], wt0, wt1, g1, 0, C // 768)
    qb_1, qb_m, q_3, x_grad = lax.optimization_barrier((qb_1, qb_m, q_3, x_grad))
    qb_s = [total([t[i // 2, i % 2] for t in (qb_m, qb_1)]) for i in range(1, 4)]
    qb_k = [t[0, 0] for t in (qb_m, qb_1)]
    qb_2 = [flip(x, rel) for x, rel in zip(qb_s, SWAP[1:])]
    g1, x_grad = tie((g1, x_grad), qb_s)
    x_grad = input_grad([gpb, gpa, gpc], wt0, wt1, g1, C // 768, C // 256 - C // 768, x_grad)
    qb_2, du_x, du_y, x_grad = lax.optimization_barrier((qb_2, du_x, du_y, x_grad))
    cut_at = du.shape[0] // 16 * 8
    du_d = [flip(du_y[:cut_at], 2), flip(du_x[cut_at:], 4)]
    qb = total(qb_k + qb_2)
    q_3.append(give(qb[1], J - 1))
    q_3, du_d = lax.optimization_barrier((q_3, du_d))
    q = rest(total([qb[0]] + q_3))
    q_4 = [flip(q, rel) for rel in NEAR[1:]]
    du = jnp.stack([du, du_x, du_y, jnp.concatenate(du_d, axis=0)])
    du_5 = flip(du, 1)
    q_4, du_5 = lax.optimization_barrier((q_4, du_5))
    q = jnp.stack([q] + q_4)
    q_5 = flip(q, 1)
    du = tie(du, q)
    down_g, up_g, ow_g, small = final(
        final_du_kernel, meta, (du, du_5), [(F, D), (D, F), (G * HD, D), (8, D)], [(SPLIT, rows, F), (SPLIT, rows, G * HD)], "final_du")
    q_5, down_g = lax.optimization_barrier((q_5, down_g))
    qkv_g, gb = final(final_q_kernel, meta, (q, q_5), [(N, D), (1, N)], [(SPLIT, rows, N)], "final_q")
    return (
        out[None], x_grad[None], qkv_g.reshape(3, G * HD, D).transpose(2, 0, 1), gb.reshape(3, G * HD), ow_g, small[5], small[3], small[4],
        up_g, small[6], down_g, small[2], small[0], small[1],
    )


def solution(mesh):
    rows = P(("wide", "narrow"), None, None)
    weights = (P(None, None, "narrow"), P(None, "narrow"), P("narrow", None), P(), P(), P(),
               P(None, "narrow"), P("narrow"), P("narrow", None), P(), P(), P())
    return jax.shard_map(
        shards, mesh=mesh, in_specs=(rows, P("wide", None)) + weights + (rows,),
        out_specs=(rows, rows) + weights, check_vma=False,
    )
```

```python
import functools

import jax
import jax.numpy as jnp
from jax import lax
from jax.experimental import pallas as pl
from jax.experimental.pallas import tpu as pltpu
from jax.sharding import PartitionSpec as P

bf = jnp.bfloat16
f32 = jnp.float32
LOG2E = 1.4426950408889634
HEADS = 12
HD = 64
SPLIT = 8
EXTRA = 8
MIB = 1 << 20


def dg(a, b, ca, cb):
    return lax.dot_general(a, b, (((ca,), (cb,)), ((), ())), preferred_element_type=f32)


def mean(x):
    return jnp.mean(x, axis=-1, keepdims=True)


def shape(s, d):
    return jax.ShapeDtypeStruct(s, d)


SMEM = pl.BlockSpec(memory_space=pltpu.SMEM)
ANY = pl.BlockSpec(memory_space=pl.ANY)


def length_of(lengths):
    return lengths[0, lax.axis_index("narrow")]


def low_bits():
    return jnp.bitwise_and(lax.axis_index("wide"), SPLIT - 1)


def params(mib):
    return pltpu.CompilerParams(vmem_limit_bytes=mib * MIB)


def cost(flops, nbytes):
    return pl.CostEstimate(flops=1, bytes_accessed=1, transcendentals=0)


def put_piece(meta, src, g, lanes, place, dst, sem):
    rel, half, whole = place
    rows = src.shape[1]
    at = 0 if rel is None else (low_bits() ^ rel) * whole + half
    return pltpu.make_async_copy(src.at[g, :, lanes], dst.at[pl.ds(pl.multiple_of(at, 16), rows), :], sem)


def attn_fwd_kernel(meta, *refs, C, KC, G, layout, own):
    pieces, refs = refs[:len(layout)], refs[len(layout):]
    x, b, cos, sin, q_t, k_t, v_d, e, ctx, exact, linv, w_t, *rest = refs
    if own:
        x_t, Q2, KD, VA, S, W, flag, sem = rest
    else:
        x_t, (Q2, KD, VA, S, W, flag, sem) = x, rest
    h = pl.program_id(0)
    length = length_of(meta)

    if own:
        @pl.when(h == 0)
        def _():
            x_t[...] = x[...].T
            n = pieces[0].shape[0]
            w_t[:n, :] = pieces[0][...]
            w_t[n:, :] = pieces[1][...]
    else:
        groups = pieces[0].shape[0]

        def copies(g):
            return [put_piece(meta, pieces[t], g, slice(None), layout[t], W.at[g], sem.at[g, t]) for t in range(len(pieces))]

        @pl.when(h == 0)
        def _():
            for g in range(groups):
                for c in copies(g):
                    c.start()

        @pl.when(lax.rem(h, G) == 0)
        def _():
            g = lax.div(h, G)
            for c in copies(g):
                c.wait()
            w_t[...] = W[g].T

    at = lax.rem(h, G)
    w = jnp.concatenate([w_t[pl.ds(pl.multiple_of((p * G + at) * HD, HD), HD), :] for p in range(3)], axis=0)
    bias = [jnp.broadcast_to(b[i:i + 1, :], (2 * HD, HD)).T[:, :1] for i in range(3)]
    p = dg(w, x_t[...], 1, 0) + jnp.concatenate(bias, axis=0)
    c, d = cos[...], sin[...]

    def rot(v):
        u, z = v[:HD // 2], v[HD // 2:]
        return jnp.concatenate([u * c - z * d, z * c + u * d], axis=0)

    live = lax.broadcasted_iota(jnp.int32, (HD, C), 1) < length
    q = rot(p[:HD]).astype(bf).astype(f32)
    k = jnp.where(live, rot(p[HD:2 * HD]), 0.0).astype(bf)
    v = jnp.where(live, p[2 * HD:], 0.0).astype(bf)
    q_t[...] = (q * 0.125).astype(bf)
    q = q * (0.125 * LOG2E)
    hi = q.astype(bf)
    Q2[:HD, :] = hi
    Q2[HD:, :] = (q - hi.astype(f32)).astype(bf)
    k_t[...] = k
    KD[...] = jnp.concatenate([k, k], axis=0).T
    v_d[...] = jnp.concatenate([v, v], axis=0).T
    VA[:HD, :] = v
    VA[HD:, :] = jnp.where(live[:16], 1.0, 0.0).astype(bf)
    kf = k.astype(f32)
    qn = jnp.max(jnp.sum(q * q, axis=0, keepdims=True))
    kn = jnp.max(jnp.sum(kf * kf, axis=0, keepdims=True))
    flag[0] = (qn * kn <= 1e4).astype(jnp.int32)

    @pl.when(flag[0] == 1)
    def _():
        for j in range(C // KC):
            r = slice(j * KC, (j + 1) * KC)
            e[r, :] = jnp.exp2(dg(KD[r, :], Q2[...], 1, 0)).astype(bf)

    @pl.when(flag[0] == 0)
    def _():
        BQ = S.shape[1]

        def block(i, carry):
            cols = pl.ds(pl.multiple_of(i * BQ, BQ), BQ)

            def score(j, m):
                r = pl.ds(pl.multiple_of(j * KC, KC), KC)
                keys = lax.broadcasted_iota(jnp.int32, (KC, BQ), 0) + j * KC
                x = jnp.where(keys < length, dg(KD[r, :], Q2[:, cols], 1, 0), -1e30)
                S[r, :] = x
                return jnp.maximum(m, jnp.max(x, axis=0, keepdims=True))

            m = lax.fori_loop(0, C // KC, score, jnp.full((1, BQ), -1e30, f32))

            def power(j, carry):
                r = pl.ds(pl.multiple_of(j * KC, KC), KC)
                e[r, cols] = jnp.exp2(S[r, :] - m).astype(bf)
                return carry

            return lax.fori_loop(0, C // KC, power, carry)

        lax.fori_loop(0, C // BQ, block, 0)

    o = dg(VA[...], e[...], 1, 0)
    inv = 1.0 / o[HD:HD + 1]
    linv[...] = inv
    o = o[:HD] * inv
    exact[...] = o
    ctx[...] = o.astype(bf)


def attn_fwd(meta, pieces, layout, x, b, cos, sin, own):
    groups, _, D = pieces[0].shape if not own else (1,) + pieces[0].shape
    C = x.shape[0] if own else x.shape[1]
    G = b.shape[1]
    H = groups * G
    at = lambda h: (h, 0, 0)
    fix = lambda a: pl.BlockSpec(a.shape, lambda h: (0,) * a.ndim, pipeline_mode=pl.Buffered(1))
    hb = pl.BlockSpec((None, HD, C), at)
    out_specs = [hb, hb, pl.BlockSpec((None, C, 2 * HD), at), pl.BlockSpec((None, C, C), at), hb, hb,
                 pl.BlockSpec((None, 1, C), at), pl.BlockSpec((None, D, D), lambda h: (h // G, 0, 0))]
    out_shape = [shape((H, HD, C), bf), shape((H, HD, C), bf), shape((H, C, 2 * HD), bf), shape((H, C, C), bf),
                 shape((H, HD, C), bf), shape((H, HD, C), f32), shape((H, 1, C), f32), shape((groups, D, D), bf)]
    if own:
        out_specs.append(pl.BlockSpec((D, C), lambda h: (0, 0)))
        out_shape.append(shape((D, C), bf))
    return pl.pallas_call(
        functools.partial(attn_fwd_kernel, C=C, KC=min(128, C), G=G, layout=layout, own=own), grid=(H,),
        in_specs=[SMEM] + ([fix(p) for p in pieces] if own else [ANY] * len(pieces))
        + [fix(x), pl.BlockSpec((None, None, 3, HD), lambda h: (h // G, h % G, 0, 0)), fix(cos), fix(sin)],
        out_specs=out_specs, out_shape=out_shape,
        scratch_shapes=[pltpu.VMEM((2 * HD, C), bf), pltpu.VMEM((C, 2 * HD), bf), pltpu.VMEM((HD + 16, C), bf),
                        pltpu.VMEM((C, C // 3 if C % 384 == 0 else C), f32), pltpu.VMEM((8, 128) if own else (groups, D, D), bf),
                        pltpu.SMEM((1,), jnp.int32), pltpu.SemaphoreType.DMA((groups, len(pieces)))],
        compiler_params=params(60), cost_estimate=cost(H * (4 * C * C * 256 + 2 * C * D * 3 * HD), H * C * C * 2 + 8 * MIB),
        name="attn_fwd_own" if own else "attn_fwd",
    )(meta, *pieces, x, b, cos, sin)


def ffn_kernel(meta, u_own, d_own, *refs, R, layout):
    pieces, refs = refs[:len(layout)], refs[len(layout):]
    tok, cot, *refs = refs
    J = pieces[0].shape[0] + 1
    ctxs, ows, refs = refs[:2], refs[2:4], refs[4:]
    (vec, ub, out, act, gu, hid_t, gl_t, g1_o, gol_t, do_t, small, ubg, G, U, Dn, sem) = refs
    i = pl.program_id(0)
    groups = J - 1

    def copies():
        cs = [pltpu.make_async_copy(u_own, U.at[0], sem.at[0, 0, 0]), pltpu.make_async_copy(d_own, Dn.at[0], sem.at[1, 0, 0])]
        for g in range(groups):
            for t, (piece, (parts, place)) in enumerate(zip(pieces, layout)):
                for k, s in enumerate(parts):
                    lanes = slice(k * U.shape[2], (k + 1) * U.shape[2])
                    cs.append(put_piece(meta, piece, g, lanes, place, (U, Dn)[s].at[g + 1], sem.at[s, g + 1, t]))
        return cs

    @pl.when(i == 0)
    def _():
        for c in copies():
            c.start()
        small[...] = jnp.zeros_like(small)
        ubg[...] = jnp.zeros_like(ubg)

    ob, g1, s1, db, g2, s2 = [vec[k:k + 1, :] for k in range(6)]
    D = tok.shape[1]
    F = U.shape[2]

    def csum(k, x):
        small[k:k + 1, :] += jnp.sum(x, axis=0, keepdims=True)

    ow = jnp.concatenate([w[g] for w in ows for g in range(w.shape[0])], axis=0)
    ctx = jnp.concatenate([c[...].reshape(-1, R) for c in ctxs], axis=0)
    pre = tok[...].astype(f32) + dg(ctx.T, ow, 1, 0) + ob
    cen = pre - mean(pre)
    r1 = lax.rsqrt(mean(cen * cen) + 1e-6)
    n1 = cen * r1
    hid = n1 * g1 + s1
    hl = hid.astype(bf)
    hid_t[...] = hl.T
    acc = hid + db

    @pl.when(i == 0)
    def _():
        for c in copies():
            c.wait()

    for j in range(J):
        u = dg(hl, U[j], 1, 0) + ub[j:j + 1, :]
        phi = 0.5 * lax.erf(u * 0.7071067811865476) + 0.5
        a = (u * phi).astype(bf)
        act[:, j * F:(j + 1) * F] = a
        G[:, j * F:(j + 1) * F] = phi + u * (jnp.exp2(u * u * -0.7213475204444817) * 0.3989422804014327)
        acc = acc + dg(a, Dn[j], 1, 0)
    cen = acc - mean(acc)
    r2 = lax.rsqrt(mean(cen * cen) + 1e-6)
    n2 = cen * r2
    out[...] = (n2 * g2 + s2).astype(bf)
    c = cot[...].astype(f32)
    csum(0, c * n2)
    csum(1, c)
    sg = c * g2
    gt = r2 * (sg - mean(sg) - n2 * mean(sg * n2))
    csum(2, gt)
    gl = gt.astype(bf)
    gl_t[...] = gl.T
    dh = gt
    for j in range(J):
        g = dg(gl, Dn[j], 1, 1) * G[:, j * F:(j + 1) * F]
        ubg[j:j + 1, :] += jnp.sum(g, axis=0, keepdims=True)
        gb = g.astype(bf)
        gu[:, j * F:(j + 1) * F] = gb
        dh = dh + dg(gb, U[j], 1, 1)
    csum(3, dh * n1)
    csum(4, dh)
    sg = dh * g1
    go = r1 * (sg - mean(sg) - n1 * mean(sg * n1))
    csum(5, go)
    g1_o[...] = go
    gol = go.astype(bf)
    gol_t[...] = gol.T
    do_t[...] = dg(ow, gol, 1, 1).astype(bf).reshape(do_t.shape)


def ffn(meta, u_own, d_own, pieces, layout, tok, cot, ctxs, wts, vec, ub, R=512):
    C, D = tok.shape
    J, F = ub.shape
    H = HEADS
    row = lambda w: pl.BlockSpec((R, w), lambda i: (i, 0))
    col = pl.BlockSpec((D, R), lambda i: (0, i))
    fix = lambda a: pl.BlockSpec(a.shape, lambda i: (0,) * a.ndim, pipeline_mode=pl.Buffered(1))
    hb = lambda n: pl.BlockSpec((n, HD, R), lambda i: (0, 0, i))
    acc = lambda s: pl.BlockSpec(s, lambda i: (0, 0))
    share = H // J * HD
    at = 3
    owb = lambda w: pl.BlockSpec((w.shape[0], share, D), lambda i: (0, at, 0), pipeline_mode=pl.Buffered(1))
    return pl.pallas_call(
        functools.partial(ffn_kernel, R=R, layout=layout), grid=(C // R,),
        in_specs=[SMEM, ANY, ANY] + [ANY] * len(pieces) + [row(D), row(D)] + [hb(c.shape[0]) for c in ctxs] + [owb(w) for w in wts] + [fix(vec), fix(ub)],
        out_specs=[row(D), row(J * F), row(J * F), col, col, row(D), col, hb(H), acc((8, D)), acc((J, F))],
        out_shape=[shape((C, D), bf), shape((C, J * F), bf), shape((C, J * F), bf), shape((D, C), bf), shape((D, C), bf), shape((C, D), f32),
                   shape((D, C), bf), shape((H, HD, C), bf), shape((8, D), f32), shape((J, F), f32)],
        scratch_shapes=[pltpu.VMEM((R, J * F), f32), pltpu.VMEM((J, D, F), bf), pltpu.VMEM((J, F, D), bf),
                        pltpu.SemaphoreType.DMA((2, J, len(pieces)))],
        compiler_params=params(60), cost_estimate=cost(2 * C * D * (2 * D + 4 * J * F), 60 * MIB), name="ffn",
    )(meta, u_own, d_own, *pieces, tok, cot, *ctxs, *wts, vec, ub)


def attn_bwd_kernel(meta, e, v_d, do_t, ctx, linv, q_t, k_t, cos, sin, gp, gb, D2, DI, DS, DST, ET, *, C, KC):
    length = length_of(meta)
    g = do_t[...].astype(f32)
    inv = linv[...]
    DI[...] = jnp.sum(g * ctx[...], axis=0, keepdims=True) * inv
    g = g * inv
    hi = g.astype(bf)
    D2[:HD, :] = hi
    D2[HD:, :] = (g - hi.astype(f32)).astype(bf)
    for j in range(C // KC):
        r = slice(j * KC, (j + 1) * KC)
        dp = dg(v_d[r, :], D2[...], 1, 0)
        ej = e[r, :]
        ds = (ej.astype(f32) * (dp - DI[...])).astype(bf)
        DS[r, :] = ds
        DST[:, r] = ds.T
        ET[:, r] = ej.T
    dq = dg(k_t[...], DS[...], 1, 0)
    dk = dg(q_t[...], DST[...], 1, 0)
    dv = dg(D2[:HD, :], ET[...], 1, 0)
    live = lax.broadcasted_iota(jnp.int32, (HD, C), 1) < length
    c, s = cos[...], sin[...]

    def unrot(x):
        u, w = x[:HD // 2], x[HD // 2:]
        return jnp.concatenate([u * c + w * s, w * c - u * s], axis=0)

    def put(k, x):
        gp[k] = x.astype(bf)
        total = jnp.sum(x, axis=1, keepdims=True)
        gb[k:k + 1, :] = jnp.broadcast_to(total, (HD, 2 * HD)).T[:1]

    put(0, unrot(dq * 0.125))
    put(1, unrot(jnp.where(live, dk, 0.0)))
    put(2, jnp.where(live, dv, 0.0))


def attn_bwd(meta, saved, do_t, cos, sin, G, first, shift, H):
    e, v_d, ctx, linv, q_t, k_t = saved
    C = e.shape[1]
    sp = lambda s: pl.BlockSpec((None,) + s, lambda h: (h + first, 0, 0))
    tab = pl.BlockSpec((HD // 2, C), lambda h: (0, 0))
    return pl.pallas_call(
        functools.partial(attn_bwd_kernel, C=C, KC=min(256, C)), grid=(H,),
        in_specs=[SMEM, sp((C, C)), sp((C, 2 * HD)), pl.BlockSpec((None, HD, C), lambda h: (h + first + shift, 0, 0)), sp((HD, C)), sp((1, C)),
                  sp((HD, C)), sp((HD, C)), tab, tab],
        out_specs=[pl.BlockSpec((None, 3, None, HD, C), lambda h: (h // G, 0, h % G, 0, 0)), pl.BlockSpec((None, 3, HD), lambda h: (h, 0, 0))],
        out_shape=[shape((H // G, 3, G, HD, C), bf), shape((H, 3, HD), f32)],
        scratch_shapes=[pltpu.VMEM((2 * HD, C), bf), pltpu.VMEM((1, C), f32)] + [pltpu.VMEM((C, C), bf)] * 3,
        compiler_params=params(60), cost_estimate=cost(H * 8 * C * C * 256, H * C * C * 2 + 16 * MIB), name="attn_bwd",
    )(meta, e, v_d, do_t, ctx, linv, q_t, k_t, cos, sin)


NEAR = (0, 2, 4, 6)
SWAP = (0, 4, 2, 6)


def lay(meta, S, theirs, mine, rows, lanes, order):
    for i, rel in enumerate(order):
        for ref, low in ((mine, 0), (theirs, 1)):
            ref[i // 2, i % 2, 0, rows, lanes] = S[low_bits() ^ (rel | low)].astype(bf)


def wgrad_d_kernel(meta, gl_t, act, vecs, theirs, mine, S):
    rows = S.shape[1]
    S[...] = dg(gl_t[...], act[...], 1, 0).reshape(S.shape)
    lay(meta, S, theirs, mine, slice(0, rows), slice(None), SWAP)
    for i, rel in enumerate(SWAP):
        for ref, low in ((mine, 0), (theirs, 1)):
            line = vecs[pl.ds(low_bits() ^ (rel | low), 1), :]
            ref[i // 2, i % 2, 0, rows:, :] = jnp.broadcast_to(line, (EXTRA, line.shape[1])).astype(bf)


def wgrad_u_kernel(meta, hid_t, gu, gol_t, *refs):
    c0, c1, theirs, mine, S, SO = refs
    F = gu.shape[1]
    S[...] = dg(hid_t[...], gu[...], 1, 0).reshape(S.shape)
    lay(meta, S, theirs, mine, slice(None), slice(0, F), NEAR)

    def out(ctx):
        SO[...] = dg(gol_t[...], ctx[...].reshape(-1, ctx.shape[-1]), 1, 1).reshape(SO.shape)

    pl.when(pl.program_id(0) == 0)(lambda: out(c0))
    pl.when(pl.program_id(0) > 0)(lambda: out(c1))
    lay(meta, SO, theirs, mine, slice(None), slice(F, F + SO.shape[2]), NEAR)


def wgrad_q_kernel(meta, tok_t, *refs):
    gps, (gb, theirs, mine, S) = refs[:-4], refs[-4:]
    rows = S.shape[1]
    if len(gps) == 1:
        S[...] = dg(tok_t[...], gps[0][...], 1, 1).reshape(S.shape)
    for j, gp in enumerate(gps if len(gps) > 1 else ()):
        @pl.when(pl.program_id(0) == j)
        def _(gp=gp):
            S[...] = dg(tok_t[...], gp[...], 1, 1).reshape(S.shape)

    lay(meta, S, theirs, mine, slice(0, rows), slice(None), SWAP)
    line = jnp.broadcast_to(gb[...], (EXTRA, gb.shape[1])).astype(bf)
    for i in range(4):
        for ref in (mine, theirs):
            ref[i // 2, i % 2, 0, rows:, :] = line


def wgrad(kernel, meta, args, specs, J, rows, lanes, scratch, name, flops):
    spec = pl.BlockSpec((2, 2, 1, rows, lanes), lambda j: (0, 0, j, 0, 0))
    return pl.pallas_call(
        kernel, grid=(J,), in_specs=[SMEM] + specs, out_specs=[spec] * 2, out_shape=[shape((2, 2, J, rows, lanes), bf)] * 2,
        scratch_shapes=[pltpu.VMEM(s, f32) for s in scratch],
        compiler_params=params(28), cost_estimate=cost(flops, 20 * MIB), name=name,
    )(meta, *[pltpu.with_memory_space_constraint(x, pltpu.HBM) for x in args])


def final_du_kernel(meta, x, y, down, up, ow, small, S, SO):
    rows = S.shape[1]
    F = up.shape[1]
    for low, ref in enumerate((x, y)):
        for t, rel in enumerate(NEAR):
            at = low_bits() ^ (rel | low)
            S[at] = ref[t, :rows, :F].astype(f32)
            small[pl.ds(at, 1), :] = ref[t, rows:rows + 1, :F].astype(f32)
            up[pl.ds(pl.multiple_of(at * rows, rows), rows), :] = ref[t, :rows, F:2 * F].astype(f32)
            SO[at] = ref[t, :rows, 2 * F:].astype(f32)
    down[...] = S[...].reshape(down.shape).T
    ow[...] = SO[...].reshape(-1, SO.shape[2]).T


def final_q_kernel(meta, x, y, qkv, gb, S):
    rows = x.shape[1] - EXTRA
    for low, ref in enumerate((x, y)):
        for t, rel in enumerate(NEAR):
            S[low_bits() ^ (rel | low)] = ref[t, :rows, :].astype(f32)
    qkv[...] = S[...].reshape(-1, S.shape[2]).T
    gb[...] = x[0, rows:rows + 1, :].astype(f32)


def final(kernel, meta, xs, outs, scratch, name):
    return pl.pallas_call(
        kernel, in_specs=[SMEM] + [pl.BlockSpec(memory_space=pltpu.VMEM)] * 2,
        out_shape=[shape(s, f32) for s in outs], scratch_shapes=[pltpu.VMEM(s, f32) for s in scratch],
        compiler_params=params(60), cost_estimate=cost(0, 8 * MIB), name=name,
    )(meta, *xs)


def input_grad_kernel(*refs, N, n):
    gps, (w0, w1, g1, *_, out) = refs[:n], refs[n:]
    acc = g1[...]
    j = 0
    for gp in gps:
        for i in range(gp.shape[0]):
            w = w0[0, :N, :] if j == 0 else w1[j - 1, :N, :]
            acc = acc + dg(gp[i], w, 0, 0)
            j += 1
    out[...] = acc


def input_grad(gps, w0, w1, g1, first, count, before=None, R=256):
    _, N, C = gps[0].shape
    D = g1.shape[1]
    fix = lambda a: pl.BlockSpec(a.shape, lambda i: (0,) * a.ndim, pipeline_mode=pl.Buffered(1))
    row = pl.BlockSpec((R, D), lambda i: (i + first, 0))
    more = [] if before is None else [before]
    return pl.pallas_call(
        functools.partial(input_grad_kernel, N=N, n=len(gps)), grid=(count,),
        in_specs=[pl.BlockSpec((g.shape[0], N, R), lambda i: (0, 0, i + first)) for g in gps] + [fix(w0), fix(w1), row] + [ANY] * len(more),
        out_specs=row, out_shape=shape((C, D), f32), input_output_aliases={len(gps) + 3: 0} if more else {},
        compiler_params=params(28), cost_estimate=cost(2 * C * D * D * 3, 24 * MIB), name="input_grad",
    )(*gps, w0, w1, g1, *more)


def fetch(x, s):
    n = lax.axis_size("narrow")
    return lax.ppermute(x, "narrow", [((i + s) % n, i) for i in range(n)])


def give(x, s):
    n = lax.axis_size("narrow")
    return lax.ppermute(x, "narrow", [(i, (i + s) % n) for i in range(n)])


def flip(x, bit):
    return lax.ppermute(x, "wide", [(i, i ^ bit) for i in range(lax.axis_size("wide"))])


def total(terms):
    x = terms[0].astype(f32)
    for y in terms[1:]:
        x = x + y.astype(f32)
    return x.astype(bf)


def rest(x):
    bit = SPLIT
    while bit < lax.axis_size("wide"):
        x = add(x, flip(x, bit))
        bit *= 2
    return x


def tie(xs, deps):
    return lax.optimization_barrier((xs, deps))[0]


def add(a, b):
    return (a.astype(f32) + b.astype(f32)).astype(bf)


def rotary_tables(capacity):
    positions = jnp.arange(capacity).astype(f32)
    frequencies = 10000.0 ** (-2.0 * jnp.arange(HD // 2).astype(f32) / HD)
    angles = frequencies[:, None] * positions[None, :]
    return jnp.cos(angles), jnp.sin(angles)


def shards(
    tokens, lengths, qkv_weight, qkv_bias, out_weight, out_bias, norm1_gain, norm1_shift,
    up_weight, up_bias, down_weight, down_bias, norm2_gain, norm2_shift, cotangent,
):
    J = lax.axis_size("narrow")
    tok, cot = tokens[0], cotangent[0]
    C, D = tok.shape
    G = HEADS // J
    N = 3 * G * HD
    F = up_weight.shape[1]
    rows = D // SPLIT
    low = jnp.bitwise_and(lax.axis_index("wide"), SPLIT - 1).astype(jnp.int32)
    meta = lengths
    cos, sin = rotary_tables(C)

    qkv_t = qkv_weight.transpose(1, 2, 0).reshape(N, D)
    qo = jnp.concatenate([qkv_weight.reshape(D, N), out_weight.T], axis=1)
    bias = jnp.concatenate([qkv_bias.reshape(-1), up_bias])
    bias = jnp.pad(bias, (0, 2 * D - bias.size)).reshape(2, D)
    cut = lambda x: lax.dynamic_slice_in_dim(x, low * rows, rows, 0)
    q_piece = jnp.concatenate([cut(qo), jnp.pad(bias, ((0, EXTRA - 2), (0, 0)))], axis=0)
    got = [fetch(q_piece, s) for s in range(1, J)]
    vec = jnp.stack([out_bias, norm1_gain, norm1_shift, down_bias, norm2_gain, norm2_shift]).astype(f32)
    b_own = qkv_bias.astype(f32).reshape(1, 3, G, HD).transpose(0, 2, 1, 3)
    ud_piece = jnp.concatenate([cut(up_weight), cut(down_weight)], axis=1)
    ud_got = [fetch(tie(ud_piece, q_piece), 1)]
    q0, k0, v0, e0, c0, o0, l0, wt0, tok_t = attn_fwd(meta, [qkv_t, out_weight], (0, 1), tok, b_own, cos, sin, True)
    got, ud_got, tok_t = lax.optimization_barrier((got, ud_got, tok_t))
    biases = jnp.stack([bias] + [x[rows:rows + 2] for x in got]).reshape(J, 2 * D).astype(f32)
    bq, ub = biases[1:, :N].reshape(J - 1, 3, G, HD).transpose(0, 2, 1, 3), biases[:, N:N + F]
    q = jnp.stack([x[:rows] for x in got])
    q_near = [flip(q, rel) for rel in NEAR[1:]]
    ud_2, ud_3 = [fetch(tie(ud_piece, got), n) for n in (2, 3)]
    q_near, ud_2, ud_3, bq, ub, vec = lax.optimization_barrier((q_near, ud_2, ud_3, bq, ub, vec))
    q_near = [q] + q_near
    q_far = [flip(x, 1) for x in q_near]
    q_places = tuple((rel | low, 0, rows) for low in (0, 1) for rel in NEAR)
    q_far, ud_2, ud_3 = lax.optimization_barrier((q_far, ud_2, ud_3))
    ud = jnp.stack(ud_got + [ud_2, ud_3])
    q_pieces = q_near + q_far
    ud_near = [flip(ud, rel) for rel in NEAR[1:]]
    ud_far = [flip(ud, 1)]
    tok_t = tie(tok_t, ud)
    q1, k1, v1, e1, c1, o1, l1, wt1 = attn_fwd(meta, q_pieces, q_places, tok_t, bq, cos, sin, False)
    ud_near, ud_far, c1 = lax.optimization_barrier((ud_near, ud_far, c1))
    ud_pieces = [ud] + ud_near + ud_far + [flip(x, 1) for x in ud_near]
    ud_places = [(rel | low, 0, rows) for low in (0, 1) for rel in NEAR]
    ud_layout = tuple(((0, 1), place) for place in ud_places)
    out, act, gu, hid_t, gl_t, g1, gol_t, do_t, small, ubg = ffn(
        meta, up_weight, down_weight, ud_pieces, ud_layout, tok, cot, (c0, c1), (wt0, wt1), vec, ub)

    whole = lambda a: pl.BlockSpec(a.shape, lambda j: (0,) * a.ndim, pipeline_mode=pl.Buffered(1))
    vecs = jnp.concatenate([jnp.broadcast_to(small[None, :6], (J, 6, D)), ubg[:, None], jnp.zeros((J, 1, D), f32)], axis=1)
    u_t, u_m = wgrad(
        wgrad_u_kernel, meta, (hid_t, gu, gol_t, c0, c1),
        [whole(hid_t), pl.BlockSpec((C, F), lambda j: (0, j)), whole(gol_t), pl.BlockSpec((G, HD, C), lambda j: (0, 0, 0)),
         pl.BlockSpec((G, HD, C), lambda j: (jnp.maximum(j - 1, 0), 0, 0))],
        J, rows, F + G * HD, [(SPLIT, rows, F), (SPLIT, rows, G * HD)], "wgrad_u", 2 * C * D * (J * F + D))
    u_1 = flip(u_t, 1)
    gl_t = tie(gl_t, u_t)
    d_t, d_m = wgrad(
        wgrad_d_kernel, meta, (gl_t, act, vecs),
        [whole(gl_t), pl.BlockSpec((C, F), lambda j: (0, j)), pl.BlockSpec((None, 8, D), lambda j: (j, 0, 0))],
        J, rows + EXTRA, F, [(SPLIT, rows, F)], "wgrad_d", 2 * C * D * J * F)

    def grad_q(gps, gb):
        n = gb.shape[0]
        one = pl.BlockSpec((None, N, C), lambda j: (j, 0, 0)) if len(gps) == 1 else pl.BlockSpec((None, N, C), lambda j: (0, 0, 0))
        return wgrad(
            wgrad_q_kernel, meta, (tok_t, *gps, gb), [whole(tok_t)] + [one] * len(gps) + [pl.BlockSpec((None, 1, N), lambda j: (j, 0, 0))],
            n, rows + EXTRA, N, [(SPLIT, rows, N)], "wgrad_q", 2 * C * D * n * N)

    def backward(group, count, do_t):
        saved, shift = ((e0, v0, o0, l0, q0, k0), 0) if group == 0 else ((e1, v1, o1, l1, q1, k1), G)
        gp, gb = attn_bwd(meta, saved, do_t, cos, sin, G, group * G - shift, shift, count * G)
        return gp.reshape(count, N, C), gb.reshape(count, G, 3, HD).transpose(0, 2, 1, 3).reshape(count, 1, N)

    def first(terms):
        return total([t[1] for t in terms]), [t[0] for t in terms]

    u_1, u_m, d_t = lax.optimization_barrier((u_1, u_m, d_t))
    d_1 = flip(d_t, 1)
    u_s, u_k = first([u_m, u_1])
    u_2 = flip(u_s, 4)
    do_t = tie(do_t, u_s)
    d_1, d_m, do_t = lax.optimization_barrier((d_1, d_m, do_t))
    d_s, d_k = first([d_m, d_1])
    d_2 = flip(d_s, 2)
    do_t = tie(do_t, d_s)
    gpa, gba = backward(1, 2, do_t)
    u_2, d_2, gpa, do_t = lax.optimization_barrier((u_2, d_2, gpa, do_t))
    u_s, u_k = first(u_k + [u_2])
    u_3 = flip(u_s, 2)
    d_s, d_k = first(d_k + [d_2])
    d_3 = flip(d_s, 4)
    gpa_ = tie(gpa, (u_s, d_s))
    qa_t, qa_m = grad_q((gpa_,), gba)
    qa_1 = flip(qa_t, 1)
    do_t = tie(do_t, qa_t)
    gpb, gbb = backward(0, 1, do_t)
    u_3, d_3, qa_1, gpb, do_t = lax.optimization_barrier((u_3, d_3, qa_1, gpb, do_t))
    du_s = [jnp.concatenate([total([t[j] for t in d_k + [d_3]]), jnp.pad(total([t[j] for t in u_k + [u_3]]), ((0, EXTRA), (0, 0)))], axis=1)
            for j in range(J)]
    du_3 = [give(du_s[s], s) for s in (1, 3)]
    qa_s, qa_k = first([qa_m, qa_1])
    qa_2 = flip(qa_s, 2)
    do_t = tie(do_t, (du_s, qa_s))
    gpc, gbc = backward(3, 1, do_t)
    du_3, qa_2, gpb, gpc = lax.optimization_barrier((du_3, qa_2, gpb, gpc))
    qa_s, qa_k = first(qa_k + [qa_2])
    qa_3 = flip(qa_s, 4)
    gpc_ = tie(gpc, qa_s)
    du_2 = give(tie(du_s[2], qa_s), 2)
    qb_t, qb_m = grad_q((gpb, gpc_), jnp.concatenate([gbb, gbc], axis=0))
    qb_1 = flip(qb_t, 1)
    qa_3, du_2, qb_t, qb_m = lax.optimization_barrier((qa_3, du_2, qb_t, qb_m))
    du = rest(total([du_s[0], du_2] + du_3))
    du_x, du_y = flip(du, 2), flip(du, 4)
    qa_s = [total([t[j] for t in qa_k + [qa_3]]) for j in range(2)]
    q_3 = [give(qa_s[0], 1), give(qa_s[1], 2)]
    g1 = tie(g1, (qb_t, qa_s, du))
    x_grad = input_grad([gpb, gpa, gpc], wt0, wt1, g1, 0, C // 768)
    qb_1, qb_m, q_3, x_grad = lax.optimization_barrier((qb_1, qb_m, q_3, x_grad))
    qb_s = [total([t[i // 2, i % 2] for t in (qb_m, qb_1)]) for i in range(1, 4)]
    qb_k = [t[0, 0] for t in (qb_m, qb_1)]
    qb_2 = [flip(x, rel) for x, rel in zip(qb_s, SWAP[1:])]
    g1, x_grad = tie((g1, x_grad), qb_s)
    x_grad = input_grad([gpb, gpa, gpc], wt0, wt1, g1, C // 768, C // 256 - C // 768, x_grad)
    qb_2, du_x, du_y, x_grad = lax.optimization_barrier((qb_2, du_x, du_y, x_grad))
    cut_at = du.shape[0] // 16 * 8
    du_d = [flip(du_y[:cut_at], 2), flip(du_x[cut_at:], 4)]
    qb = total(qb_k + qb_2)
    q_3.append(give(qb[1], J - 1))
    q_3, du_d = lax.optimization_barrier((q_3, du_d))
    du = jnp.stack([du, du_x, du_y, jnp.concatenate(du_d, axis=0)])
    du_5 = flip(du, 1)
    q = rest(total([qb[0]] + q_3))
    q_4 = [flip(q, rel) for rel in NEAR[1:]]
    du_5, du, q = lax.optimization_barrier((du_5, du, q))
    down_g, up_g, ow_g, small = final(
        final_du_kernel, meta, (du, du_5), [(F, D), (D, F), (G * HD, D), (8, D)], [(SPLIT, rows, F), (SPLIT, rows, G * HD)], "final_du")
    q_4, q, down_g = lax.optimization_barrier((q_4, q, down_g))
    q = jnp.stack([q] + q_4)
    q_5 = flip(q, 1)
    qkv_g, gb = final(final_q_kernel, meta, (q, q_5), [(N, D), (1, N)], [(SPLIT, rows, N)], "final_q")
    return (
        out[None], x_grad[None], qkv_g.reshape(3, G * HD, D).transpose(2, 0, 1), gb.reshape(3, G * HD), ow_g, small[5], small[3], small[4],
        up_g, small[6], down_g, small[2], small[0], small[1],
    )


def solution(mesh):
    rows = P(("wide", "narrow"), None, None)
    weights = (P(None, None, "narrow"), P(None, "narrow"), P("narrow", None), P(), P(), P(),
               P(None, "narrow"), P("narrow"), P("narrow", None), P(), P(), P())
    return jax.shard_map(
        shards, mesh=mesh, in_specs=(rows, P("wide", None)) + weights + (rows,),
        out_specs=(rows, rows) + weights, check_vma=False,
    )
```

```python
import functools

import jax
import jax.numpy as jnp
from jax import lax
from jax.experimental import pallas as pl
from jax.experimental.pallas import tpu as pltpu
from jax.sharding import PartitionSpec as P

bf = jnp.bfloat16
f32 = jnp.float32
LOG2E = 1.4426950408889634
HEADS = 12
HD = 64
SPLIT = 8
EXTRA = 8
MIB = 1 << 20


def dg(a, b, ca, cb):
    return lax.dot_general(a, b, (((ca,), (cb,)), ((), ())), preferred_element_type=f32)


def mean(x):
    return jnp.mean(x, axis=-1, keepdims=True)


def shape(s, d):
    return jax.ShapeDtypeStruct(s, d)


SMEM = pl.BlockSpec(memory_space=pltpu.SMEM)
ANY = pl.BlockSpec(memory_space=pl.ANY)


def length_of(lengths):
    return lengths[0, lax.axis_index("narrow")]


def low_bits():
    return jnp.bitwise_and(lax.axis_index("wide"), SPLIT - 1)


def params(mib):
    return pltpu.CompilerParams(vmem_limit_bytes=mib * MIB)


def cost(flops, nbytes):
    return pl.CostEstimate(flops=1, bytes_accessed=1, transcendentals=0)


def put_piece(meta, src, g, lanes, place, dst, sem):
    rel, half, whole = place
    rows = src.shape[1]
    at = 0 if rel is None else (low_bits() ^ rel) * whole + half
    return pltpu.make_async_copy(src.at[g, :, lanes], dst.at[pl.ds(pl.multiple_of(at, 16), rows), :], sem)


def attn_fwd_kernel(meta, *refs, C, KC, G, layout, own):
    pieces, refs = refs[:len(layout)], refs[len(layout):]
    x, b, cos, sin, q_t, k_t, v_d, e, ctx, exact, linv, w_t, *rest = refs
    if own:
        x_t, Q2, KD, VA, S, W, flag, sem = rest
    else:
        x_t, (Q2, KD, VA, S, W, flag, sem) = x, rest
    h = pl.program_id(0)
    length = length_of(meta)

    if own:
        @pl.when(h == 0)
        def _():
            x_t[...] = x[...].T
            n = pieces[0].shape[0]
            w_t[:n, :] = pieces[0][...]
            w_t[n:, :] = pieces[1][...]
    else:
        groups = pieces[0].shape[0]

        def copies(g):
            return [put_piece(meta, pieces[t], g, slice(None), layout[t], W.at[g], sem.at[g, t]) for t in range(len(pieces))]

        @pl.when(h == 0)
        def _():
            for g in range(groups):
                for c in copies(g):
                    c.start()

        @pl.when(lax.rem(h, G) == 0)
        def _():
            g = lax.div(h, G)
            for c in copies(g):
                c.wait()
            w_t[...] = W[g].T

    at = lax.rem(h, G)
    w = jnp.concatenate([w_t[pl.ds(pl.multiple_of((p * G + at) * HD, HD), HD), :] for p in range(3)], axis=0)
    bias = [jnp.broadcast_to(b[i:i + 1, :], (2 * HD, HD)).T[:, :1] for i in range(3)]
    p = dg(w, x_t[...], 1, 0) + jnp.concatenate(bias, axis=0)
    c, d = cos[...], sin[...]

    def rot(v):
        u, z = v[:HD // 2], v[HD // 2:]
        return jnp.concatenate([u * c - z * d, z * c + u * d], axis=0)

    live = lax.broadcasted_iota(jnp.int32, (HD, C), 1) < length
    q = rot(p[:HD]).astype(bf).astype(f32)
    k = jnp.where(live, rot(p[HD:2 * HD]), 0.0).astype(bf)
    v = jnp.where(live, p[2 * HD:], 0.0).astype(bf)
    q_t[...] = (q * 0.125).astype(bf)
    q = q * (0.125 * LOG2E)
    hi = q.astype(bf)
    Q2[:HD, :] = hi
    Q2[HD:, :] = (q - hi.astype(f32)).astype(bf)
    k_t[...] = k
    KD[...] = jnp.concatenate([k, k], axis=0).T
    v_d[...] = jnp.concatenate([v, v], axis=0).T
    VA[:HD, :] = v
    VA[HD:, :] = jnp.where(live[:16], 1.0, 0.0).astype(bf)
    kf = k.astype(f32)
    qn = jnp.max(jnp.sum(q * q, axis=0, keepdims=True))
    kn = jnp.max(jnp.sum(kf * kf, axis=0, keepdims=True))
    flag[0] = (qn * kn <= 1e4).astype(jnp.int32)

    @pl.when(flag[0] == 1)
    def _():
        for j in range(C // KC):
            r = slice(j * KC, (j + 1) * KC)
            e[r, :] = jnp.exp2(dg(KD[r, :], Q2[...], 1, 0)).astype(bf)

    @pl.when(flag[0] == 0)
    def _():
        BQ = S.shape[1]

        def block(i, carry):
            cols = pl.ds(pl.multiple_of(i * BQ, BQ), BQ)

            def score(j, m):
                r = pl.ds(pl.multiple_of(j * KC, KC), KC)
                keys = lax.broadcasted_iota(jnp.int32, (KC, BQ), 0) + j * KC
                x = jnp.where(keys < length, dg(KD[r, :], Q2[:, cols], 1, 0), -1e30)
                S[r, :] = x
                return jnp.maximum(m, jnp.max(x, axis=0, keepdims=True))

            m = lax.fori_loop(0, C // KC, score, jnp.full((1, BQ), -1e30, f32))

            def power(j, carry):
                r = pl.ds(pl.multiple_of(j * KC, KC), KC)
                e[r, cols] = jnp.exp2(S[r, :] - m).astype(bf)
                return carry

            return lax.fori_loop(0, C // KC, power, carry)

        lax.fori_loop(0, C // BQ, block, 0)

    o = dg(VA[...], e[...], 1, 0)
    inv = 1.0 / o[HD:HD + 1]
    linv[...] = inv
    o = o[:HD] * inv
    exact[...] = o
    ctx[...] = o.astype(bf)


def attn_fwd(meta, pieces, layout, x, b, cos, sin, own):
    groups, _, D = pieces[0].shape if not own else (1,) + pieces[0].shape
    C = x.shape[0] if own else x.shape[1]
    G = b.shape[1]
    H = groups * G
    at = lambda h: (h, 0, 0)
    fix = lambda a: pl.BlockSpec(a.shape, lambda h: (0,) * a.ndim, pipeline_mode=pl.Buffered(1))
    hb = pl.BlockSpec((None, HD, C), at)
    out_specs = [hb, hb, pl.BlockSpec((None, C, 2 * HD), at), pl.BlockSpec((None, C, C), at), hb, hb,
                 pl.BlockSpec((None, 1, C), at), pl.BlockSpec((None, D, D), lambda h: (h // G, 0, 0))]
    out_shape = [shape((H, HD, C), bf), shape((H, HD, C), bf), shape((H, C, 2 * HD), bf), shape((H, C, C), bf),
                 shape((H, HD, C), bf), shape((H, HD, C), f32), shape((H, 1, C), f32), shape((groups, D, D), bf)]
    if own:
        out_specs.append(pl.BlockSpec((D, C), lambda h: (0, 0)))
        out_shape.append(shape((D, C), bf))
    return pl.pallas_call(
        functools.partial(attn_fwd_kernel, C=C, KC=min(128, C), G=G, layout=layout, own=own), grid=(H,),
        in_specs=[SMEM] + ([fix(p) for p in pieces] if own else [ANY] * len(pieces))
        + [fix(x), pl.BlockSpec((None, None, 3, HD), lambda h: (h // G, h % G, 0, 0)), fix(cos), fix(sin)],
        out_specs=out_specs, out_shape=out_shape,
        scratch_shapes=[pltpu.VMEM((2 * HD, C), bf), pltpu.VMEM((C, 2 * HD), bf), pltpu.VMEM((HD + 16, C), bf),
                        pltpu.VMEM((C, C // 3 if C % 384 == 0 else C), f32), pltpu.VMEM((8, 128) if own else (groups, D, D), bf),
                        pltpu.SMEM((1,), jnp.int32), pltpu.SemaphoreType.DMA((groups, len(pieces)))],
        compiler_params=params(60), cost_estimate=cost(H * (4 * C * C * 256 + 2 * C * D * 3 * HD), H * C * C * 2 + 8 * MIB),
        name="attn_fwd_own" if own else "attn_fwd",
    )(meta, *pieces, x, b, cos, sin)


def ffn_kernel(meta, u_own, d_own, *refs, R, layout):
    pieces, refs = refs[:len(layout)], refs[len(layout):]
    tok, cot, *refs = refs
    J = pieces[0].shape[0] + 1
    ctxs, ows, refs = refs[:2], refs[2:4], refs[4:]
    (vec, ub, out, act, gu, hid_t, gl_t, g1_o, gol_t, do_t, small, ubg, G, U, Dn, sem) = refs
    i = pl.program_id(0)
    groups = J - 1

    def copies():
        cs = [pltpu.make_async_copy(u_own, U.at[0], sem.at[0, 0, 0]), pltpu.make_async_copy(d_own, Dn.at[0], sem.at[1, 0, 0])]
        for g in range(groups):
            for t, (piece, (parts, place)) in enumerate(zip(pieces, layout)):
                for k, s in enumerate(parts):
                    lanes = slice(k * U.shape[2], (k + 1) * U.shape[2])
                    cs.append(put_piece(meta, piece, g, lanes, place, (U, Dn)[s].at[g + 1], sem.at[s, g + 1, t]))
        return cs

    @pl.when(i == 0)
    def _():
        for c in copies():
            c.start()
        small[...] = jnp.zeros_like(small)
        ubg[...] = jnp.zeros_like(ubg)

    ob, g1, s1, db, g2, s2 = [vec[k:k + 1, :] for k in range(6)]
    D = tok.shape[1]
    F = U.shape[2]

    def csum(k, x):
        small[k:k + 1, :] += jnp.sum(x, axis=0, keepdims=True)

    ow = jnp.concatenate([w[g] for w in ows for g in range(w.shape[0])], axis=0)
    ctx = jnp.concatenate([c[...].reshape(-1, R) for c in ctxs], axis=0)
    pre = tok[...].astype(f32) + dg(ctx.T, ow, 1, 0) + ob
    cen = pre - mean(pre)
    r1 = lax.rsqrt(mean(cen * cen) + 1e-6)
    n1 = cen * r1
    hid = n1 * g1 + s1
    hl = hid.astype(bf)
    hid_t[...] = hl.T
    acc = hid + db

    @pl.when(i == 0)
    def _():
        for c in copies():
            c.wait()

    for j in range(J):
        u = dg(hl, U[j], 1, 0) + ub[j:j + 1, :]
        phi = 0.5 * lax.erf(u * 0.7071067811865476) + 0.5
        a = (u * phi).astype(bf)
        act[:, j * F:(j + 1) * F] = a
        G[:, j * F:(j + 1) * F] = phi + u * (jnp.exp2(u * u * -0.7213475204444817) * 0.3989422804014327)
        acc = acc + dg(a, Dn[j], 1, 0)
    cen = acc - mean(acc)
    r2 = lax.rsqrt(mean(cen * cen) + 1e-6)
    n2 = cen * r2
    out[...] = (n2 * g2 + s2).astype(bf)
    c = cot[...].astype(f32)
    csum(0, c * n2)
    csum(1, c)
    sg = c * g2
    gt = r2 * (sg - mean(sg) - n2 * mean(sg * n2))
    csum(2, gt)
    gl = gt.astype(bf)
    gl_t[...] = gl.T
    dh = gt
    for j in range(J):
        g = dg(gl, Dn[j], 1, 1) * G[:, j * F:(j + 1) * F]
        ubg[j:j + 1, :] += jnp.sum(g, axis=0, keepdims=True)
        gb = g.astype(bf)
        gu[:, j * F:(j + 1) * F] = gb
        dh = dh + dg(gb, U[j], 1, 1)
    csum(3, dh * n1)
    csum(4, dh)
    sg = dh * g1
    go = r1 * (sg - mean(sg) - n1 * mean(sg * n1))
    csum(5, go)
    g1_o[...] = go
    gol = go.astype(bf)
    gol_t[...] = gol.T
    do_t[...] = dg(ow, gol, 1, 1).astype(bf).reshape(do_t.shape)


def ffn(meta, u_own, d_own, pieces, layout, tok, cot, ctxs, wts, vec, ub, R=512):
    C, D = tok.shape
    J, F = ub.shape
    H = HEADS
    row = lambda w: pl.BlockSpec((R, w), lambda i: (i, 0))
    col = pl.BlockSpec((D, R), lambda i: (0, i))
    fix = lambda a: pl.BlockSpec(a.shape, lambda i: (0,) * a.ndim, pipeline_mode=pl.Buffered(1))
    hb = lambda n: pl.BlockSpec((n, HD, R), lambda i: (0, 0, i))
    acc = lambda s: pl.BlockSpec(s, lambda i: (0, 0))
    share = H // J * HD
    at = 3
    owb = lambda w: pl.BlockSpec((w.shape[0], share, D), lambda i: (0, at, 0), pipeline_mode=pl.Buffered(1))
    return pl.pallas_call(
        functools.partial(ffn_kernel, R=R, layout=layout), grid=(C // R,),
        in_specs=[SMEM, ANY, ANY] + [ANY] * len(pieces) + [row(D), row(D)] + [hb(c.shape[0]) for c in ctxs] + [owb(w) for w in wts] + [fix(vec), fix(ub)],
        out_specs=[row(D), row(J * F), row(J * F), col, col, row(D), col, hb(H), acc((8, D)), acc((J, F))],
        out_shape=[shape((C, D), bf), shape((C, J * F), bf), shape((C, J * F), bf), shape((D, C), bf), shape((D, C), bf), shape((C, D), f32),
                   shape((D, C), bf), shape((H, HD, C), bf), shape((8, D), f32), shape((J, F), f32)],
        scratch_shapes=[pltpu.VMEM((R, J * F), f32), pltpu.VMEM((J, D, F), bf), pltpu.VMEM((J, F, D), bf),
                        pltpu.SemaphoreType.DMA((2, J, len(pieces)))],
        compiler_params=params(60), cost_estimate=cost(2 * C * D * (2 * D + 4 * J * F), 60 * MIB), name="ffn",
    )(meta, u_own, d_own, *pieces, tok, cot, *ctxs, *wts, vec, ub)


def attn_bwd_kernel(meta, e, v_d, do_t, ctx, linv, q_t, k_t, cos, sin, gp, gb, D2, DI, DS, DST, ET, *, C, KC):
    length = length_of(meta)
    g = do_t[...].astype(f32)
    inv = linv[...]
    DI[...] = jnp.sum(g * ctx[...], axis=0, keepdims=True) * inv
    g = g * inv
    hi = g.astype(bf)
    D2[:HD, :] = hi
    D2[HD:, :] = (g - hi.astype(f32)).astype(bf)
    for j in range(C // KC):
        r = slice(j * KC, (j + 1) * KC)
        dp = dg(v_d[r, :], D2[...], 1, 0)
        ej = e[r, :]
        ds = (ej.astype(f32) * (dp - DI[...])).astype(bf)
        DS[r, :] = ds
        DST[:, r] = ds.T
        ET[:, r] = ej.T
    dq = dg(k_t[...], DS[...], 1, 0)
    dk = dg(q_t[...], DST[...], 1, 0)
    dv = dg(D2[:HD, :], ET[...], 1, 0)
    live = lax.broadcasted_iota(jnp.int32, (HD, C), 1) < length
    c, s = cos[...], sin[...]

    def unrot(x):
        u, w = x[:HD // 2], x[HD // 2:]
        return jnp.concatenate([u * c + w * s, w * c - u * s], axis=0)

    def put(k, x):
        gp[k] = x.astype(bf)
        total = jnp.sum(x, axis=1, keepdims=True)
        gb[k:k + 1, :] = jnp.broadcast_to(total, (HD, 2 * HD)).T[:1]

    put(0, unrot(dq * 0.125))
    put(1, unrot(jnp.where(live, dk, 0.0)))
    put(2, jnp.where(live, dv, 0.0))


def attn_bwd(meta, saved, do_t, cos, sin, G, first, shift, H):
    e, v_d, ctx, linv, q_t, k_t = saved
    C = e.shape[1]
    sp = lambda s: pl.BlockSpec((None,) + s, lambda h: (h + first, 0, 0))
    tab = pl.BlockSpec((HD // 2, C), lambda h: (0, 0))
    return pl.pallas_call(
        functools.partial(attn_bwd_kernel, C=C, KC=min(256, C)), grid=(H,),
        in_specs=[SMEM, sp((C, C)), sp((C, 2 * HD)), pl.BlockSpec((None, HD, C), lambda h: (h + first + shift, 0, 0)), sp((HD, C)), sp((1, C)),
                  sp((HD, C)), sp((HD, C)), tab, tab],
        out_specs=[pl.BlockSpec((None, 3, None, HD, C), lambda h: (h // G, 0, h % G, 0, 0)), pl.BlockSpec((None, 3, HD), lambda h: (h, 0, 0))],
        out_shape=[shape((H // G, 3, G, HD, C), bf), shape((H, 3, HD), f32)],
        scratch_shapes=[pltpu.VMEM((2 * HD, C), bf), pltpu.VMEM((1, C), f32)] + [pltpu.VMEM((C, C), bf)] * 3,
        compiler_params=params(60), cost_estimate=cost(H * 8 * C * C * 256, H * C * C * 2 + 16 * MIB), name="attn_bwd",
    )(meta, e, v_d, do_t, ctx, linv, q_t, k_t, cos, sin)


NEAR = (0, 2, 4, 6)
SWAP = (0, 4, 2, 6)


def lay(meta, S, theirs, mine, rows, lanes, order):
    for i, rel in enumerate(order):
        for ref, low in ((mine, 0), (theirs, 1)):
            ref[i // 2, i % 2, 0, rows, lanes] = S[low_bits() ^ (rel | low)].astype(bf)


def wgrad_d_kernel(meta, gl_t, act, vecs, theirs, mine, S):
    rows = S.shape[1]
    S[...] = dg(gl_t[...], act[...], 1, 0).reshape(S.shape)
    lay(meta, S, theirs, mine, slice(0, rows), slice(None), SWAP)
    for i, rel in enumerate(SWAP):
        for ref, low in ((mine, 0), (theirs, 1)):
            line = vecs[pl.ds(low_bits() ^ (rel | low), 1), :]
            ref[i // 2, i % 2, 0, rows:, :] = jnp.broadcast_to(line, (EXTRA, line.shape[1])).astype(bf)


def wgrad_u_kernel(meta, hid_t, gu, gol_t, *refs):
    c0, c1, theirs, mine, S, SO = refs
    F = gu.shape[1]
    S[...] = dg(hid_t[...], gu[...], 1, 0).reshape(S.shape)
    lay(meta, S, theirs, mine, slice(None), slice(0, F), NEAR)

    def out(ctx):
        SO[...] = dg(gol_t[...], ctx[...].reshape(-1, ctx.shape[-1]), 1, 1).reshape(SO.shape)

    pl.when(pl.program_id(0) == 0)(lambda: out(c0))
    pl.when(pl.program_id(0) > 0)(lambda: out(c1))
    lay(meta, SO, theirs, mine, slice(None), slice(F, F + SO.shape[2]), NEAR)


def wgrad_q_kernel(meta, tok_t, *refs):
    gps, (gb, theirs, mine, S) = refs[:-4], refs[-4:]
    rows = S.shape[1]
    if len(gps) == 1:
        S[...] = dg(tok_t[...], gps[0][...], 1, 1).reshape(S.shape)
    for j, gp in enumerate(gps if len(gps) > 1 else ()):
        @pl.when(pl.program_id(0) == j)
        def _(gp=gp):
            S[...] = dg(tok_t[...], gp[...], 1, 1).reshape(S.shape)

    lay(meta, S, theirs, mine, slice(0, rows), slice(None), SWAP)
    line = jnp.broadcast_to(gb[...], (EXTRA, gb.shape[1])).astype(bf)
    for i in range(4):
        for ref in (mine, theirs):
            ref[i // 2, i % 2, 0, rows:, :] = line


def wgrad(kernel, meta, args, specs, J, rows, lanes, scratch, name, flops):
    spec = pl.BlockSpec((2, 2, 1, rows, lanes), lambda j: (0, 0, j, 0, 0))
    return pl.pallas_call(
        kernel, grid=(J,), in_specs=[SMEM] + specs, out_specs=[spec] * 2, out_shape=[shape((2, 2, J, rows, lanes), bf)] * 2,
        scratch_shapes=[pltpu.VMEM(s, f32) for s in scratch],
        compiler_params=params(28), cost_estimate=cost(flops, 20 * MIB), name=name,
    )(meta, *[pltpu.with_memory_space_constraint(x, pltpu.HBM) for x in args])


def final_du_kernel(meta, x, y, down, up, ow, small, S, SO):
    rows = S.shape[1]
    F = up.shape[1]
    for low, ref in enumerate((x, y)):
        for t, rel in enumerate(NEAR):
            at = low_bits() ^ (rel | low)
            S[at] = ref[t, :rows, :F].astype(f32)
            small[pl.ds(at, 1), :] = ref[t, rows:rows + 1, :F].astype(f32)
            up[pl.ds(pl.multiple_of(at * rows, rows), rows), :] = ref[t, :rows, F:2 * F].astype(f32)
            SO[at] = ref[t, :rows, 2 * F:].astype(f32)
    down[...] = S[...].reshape(down.shape).T
    ow[...] = SO[...].reshape(-1, SO.shape[2]).T


def final_q_kernel(meta, x, y, qkv, gb, S):
    rows = x.shape[1] - EXTRA
    for low, ref in enumerate((x, y)):
        for t, rel in enumerate(NEAR):
            S[low_bits() ^ (rel | low)] = ref[t, :rows, :].astype(f32)
    qkv[...] = S[...].reshape(-1, S.shape[2]).T
    gb[...] = x[0, rows:rows + 1, :].astype(f32)


def final(kernel, meta, xs, outs, scratch, name):
    return pl.pallas_call(
        kernel, in_specs=[SMEM] + [pl.BlockSpec(memory_space=pltpu.VMEM)] * 2,
        out_shape=[shape(s, f32) for s in outs], scratch_shapes=[pltpu.VMEM(s, f32) for s in scratch],
        compiler_params=params(60), cost_estimate=cost(0, 8 * MIB), name=name,
    )(meta, *xs)


def input_grad_kernel(*refs, N, n):
    gps, (w0, w1, g1, *_, out) = refs[:n], refs[n:]
    acc = g1[...]
    j = 0
    for gp in gps:
        for i in range(gp.shape[0]):
            w = w0[0, :N, :] if j == 0 else w1[j - 1, :N, :]
            acc = acc + dg(gp[i], w, 0, 0)
            j += 1
    out[...] = acc


def input_grad(gps, w0, w1, g1, first, count, before=None, R=256):
    _, N, C = gps[0].shape
    D = g1.shape[1]
    fix = lambda a: pl.BlockSpec(a.shape, lambda i: (0,) * a.ndim, pipeline_mode=pl.Buffered(1))
    row = pl.BlockSpec((R, D), lambda i: (i + first, 0))
    more = [] if before is None else [before]
    return pl.pallas_call(
        functools.partial(input_grad_kernel, N=N, n=len(gps)), grid=(count,),
        in_specs=[pl.BlockSpec((g.shape[0], N, R), lambda i: (0, 0, i + first)) for g in gps] + [fix(w0), fix(w1), row] + [ANY] * len(more),
        out_specs=row, out_shape=shape((C, D), f32), input_output_aliases={len(gps) + 3: 0} if more else {},
        compiler_params=params(28), cost_estimate=cost(2 * C * D * D * 3, 24 * MIB), name="input_grad",
    )(*gps, w0, w1, g1, *more)


def fetch(x, s):
    n = lax.axis_size("narrow")
    return lax.ppermute(x, "narrow", [((i + s) % n, i) for i in range(n)])


def give(x, s):
    n = lax.axis_size("narrow")
    return lax.ppermute(x, "narrow", [(i, (i + s) % n) for i in range(n)])


def flip(x, bit):
    return lax.ppermute(x, "wide", [(i, i ^ bit) for i in range(lax.axis_size("wide"))])


def total(terms):
    x = terms[0].astype(f32)
    for y in terms[1:]:
        x = x + y.astype(f32)
    return x.astype(bf)


def rest(x):
    bit = SPLIT
    while bit < lax.axis_size("wide"):
        x = add(x, flip(x, bit))
        bit *= 2
    return x


def tie(xs, deps):
    return lax.optimization_barrier((xs, deps))[0]


def add(a, b):
    return (a.astype(f32) + b.astype(f32)).astype(bf)


def rotary_tables(capacity):
    positions = jnp.arange(capacity).astype(f32)
    frequencies = 10000.0 ** (-2.0 * jnp.arange(HD // 2).astype(f32) / HD)
    angles = frequencies[:, None] * positions[None, :]
    return jnp.cos(angles), jnp.sin(angles)


def shards(
    tokens, lengths, qkv_weight, qkv_bias, out_weight, out_bias, norm1_gain, norm1_shift,
    up_weight, up_bias, down_weight, down_bias, norm2_gain, norm2_shift, cotangent,
):
    J = lax.axis_size("narrow")
    tok, cot = tokens[0], cotangent[0]
    C, D = tok.shape
    G = HEADS // J
    N = 3 * G * HD
    F = up_weight.shape[1]
    rows = D // SPLIT
    low = jnp.bitwise_and(lax.axis_index("wide"), SPLIT - 1).astype(jnp.int32)
    meta = lengths
    cos, sin = rotary_tables(C)

    qkv_t = qkv_weight.transpose(1, 2, 0).reshape(N, D)
    qo = jnp.concatenate([qkv_weight.reshape(D, N), out_weight.T], axis=1)
    bias = jnp.concatenate([qkv_bias.reshape(-1), up_bias])
    bias = jnp.pad(bias, (0, 2 * D - bias.size)).reshape(2, D)
    cut = lambda x: lax.dynamic_slice_in_dim(x, low * rows, rows, 0)
    q_piece = jnp.concatenate([cut(qo), jnp.pad(bias, ((0, EXTRA - 2), (0, 0)))], axis=0)
    got = [fetch(q_piece, s) for s in range(1, J)]
    vec = jnp.stack([out_bias, norm1_gain, norm1_shift, down_bias, norm2_gain, norm2_shift]).astype(f32)
    b_own = qkv_bias.astype(f32).reshape(1, 3, G, HD).transpose(0, 2, 1, 3)
    ud_piece = jnp.concatenate([cut(up_weight), cut(down_weight)], axis=1)
    ud_got = [fetch(tie(ud_piece, q_piece), 1)]
    q0, k0, v0, e0, c0, o0, l0, wt0, tok_t = attn_fwd(meta, [qkv_t, out_weight], (0, 1), tok, b_own, cos, sin, True)
    got, ud_got, tok_t = lax.optimization_barrier((got, ud_got, tok_t))
    biases = jnp.stack([bias] + [x[rows:rows + 2] for x in got]).reshape(J, 2 * D).astype(f32)
    bq, ub = biases[1:, :N].reshape(J - 1, 3, G, HD).transpose(0, 2, 1, 3), biases[:, N:N + F]
    q = jnp.stack([x[:rows] for x in got])
    q_near = [flip(q, rel) for rel in NEAR[1:]]
    ud_2, ud_3 = [fetch(tie(ud_piece, got), n) for n in (2, 3)]
    q_near, ud_2, ud_3, bq, ub, vec = lax.optimization_barrier((q_near, ud_2, ud_3, bq, ub, vec))
    q_near = [q] + q_near
    q_far = [flip(x, 1) for x in q_near]
    q_places = tuple((rel | low, 0, rows) for low in (0, 1) for rel in NEAR)
    q_far, ud_2, ud_3 = lax.optimization_barrier((q_far, ud_2, ud_3))
    ud = jnp.stack(ud_got + [ud_2, ud_3])
    q_pieces = q_near + q_far
    ud_near = [flip(ud, rel) for rel in NEAR[1:]]
    ud_far = [flip(ud, 1)]
    tok_t = tie(tok_t, ud)
    q1, k1, v1, e1, c1, o1, l1, wt1 = attn_fwd(meta, q_pieces, q_places, tok_t, bq, cos, sin, False)
    ud_near, ud_far, c1 = lax.optimization_barrier((ud_near, ud_far, c1))
    ud_pieces = [ud] + ud_near + ud_far + [flip(x, 1) for x in ud_near]
    ud_places = [(rel | low, 0, rows) for low in (0, 1) for rel in NEAR]
    ud_layout = tuple(((0, 1), place) for place in ud_places)
    out, act, gu, hid_t, gl_t, g1, gol_t, do_t, small, ubg = ffn(
        meta, up_weight, down_weight, ud_pieces, ud_layout, tok, cot, (c0, c1), (wt0, wt1), vec, ub)

    whole = lambda a: pl.BlockSpec(a.shape, lambda j: (0,) * a.ndim, pipeline_mode=pl.Buffered(1))
    vecs = jnp.concatenate([jnp.broadcast_to(small[None, :6], (J, 6, D)), ubg[:, None], jnp.zeros((J, 1, D), f32)], axis=1)
    u_t, u_m = wgrad(
        wgrad_u_kernel, meta, (hid_t, gu, gol_t, c0, c1),
        [whole(hid_t), pl.BlockSpec((C, F), lambda j: (0, j)), whole(gol_t), pl.BlockSpec((G, HD, C), lambda j: (0, 0, 0)),
         pl.BlockSpec((G, HD, C), lambda j: (jnp.maximum(j - 1, 0), 0, 0))],
        J, rows, F + G * HD, [(SPLIT, rows, F), (SPLIT, rows, G * HD)], "wgrad_u", 2 * C * D * (J * F + D))
    u_1 = flip(u_t, 1)
    gl_t = tie(gl_t, u_t)
    d_t, d_m = wgrad(
        wgrad_d_kernel, meta, (gl_t, act, vecs),
        [whole(gl_t), pl.BlockSpec((C, F), lambda j: (0, j)), pl.BlockSpec((None, 8, D), lambda j: (j, 0, 0))],
        J, rows + EXTRA, F, [(SPLIT, rows, F)], "wgrad_d", 2 * C * D * J * F)

    def grad_q(gps, gb):
        n = gb.shape[0]
        one = pl.BlockSpec((None, N, C), lambda j: (j, 0, 0)) if len(gps) == 1 else pl.BlockSpec((None, N, C), lambda j: (0, 0, 0))
        return wgrad(
            wgrad_q_kernel, meta, (tok_t, *gps, gb), [whole(tok_t)] + [one] * len(gps) + [pl.BlockSpec((None, 1, N), lambda j: (j, 0, 0))],
            n, rows + EXTRA, N, [(SPLIT, rows, N)], "wgrad_q", 2 * C * D * n * N)

    def backward(group, count, do_t):
        saved, shift = ((e0, v0, o0, l0, q0, k0), 0) if group == 0 else ((e1, v1, o1, l1, q1, k1), G)
        gp, gb = attn_bwd(meta, saved, do_t, cos, sin, G, group * G - shift, shift, count * G)
        return gp.reshape(count, N, C), gb.reshape(count, G, 3, HD).transpose(0, 2, 1, 3).reshape(count, 1, N)

    def first(terms):
        return total([t[1] for t in terms]), [t[0] for t in terms]

    u_1, u_m, d_t = lax.optimization_barrier((u_1, u_m, d_t))
    d_1 = flip(d_t, 1)
    u_s, u_k = first([u_m, u_1])
    u_2 = flip(u_s, 4)
    do_t = tie(do_t, u_s)
    d_1, d_m, do_t = lax.optimization_barrier((d_1, d_m, do_t))
    d_s, d_k = first([d_m, d_1])
    d_2 = flip(d_s, 2)
    do_t = tie(do_t, d_s)
    gpa, gba = backward(1, 2, do_t)
    u_2, d_2, gpa, do_t = lax.optimization_barrier((u_2, d_2, gpa, do_t))
    u_s, u_k = first(u_k + [u_2])
    u_3 = flip(u_s, 2)
    d_s, d_k = first(d_k + [d_2])
    d_3 = flip(d_s, 4)
    gpa_ = tie(gpa, (u_s, d_s))
    qa_t, qa_m = grad_q((gpa_,), gba)
    qa_1 = flip(qa_t, 1)
    do_t = tie(do_t, qa_t)
    gpb, gbb = backward(0, 1, do_t)
    u_3, d_3, qa_1, gpb, do_t = lax.optimization_barrier((u_3, d_3, qa_1, gpb, do_t))
    du_s = [jnp.concatenate([total([t[j] for t in d_k + [d_3]]), jnp.pad(total([t[j] for t in u_k + [u_3]]), ((0, EXTRA), (0, 0)))], axis=1)
            for j in range(J)]
    du_3 = [give(du_s[2], 1), give(du_s[3], 3)]
    qa_s, qa_k = first([qa_m, qa_1])
    qa_2 = flip(qa_s, 2)
    do_t = tie(do_t, (du_s, qa_s))
    gpc, gbc = backward(3, 1, do_t)
    du_3, qa_2, gpb, gpc = lax.optimization_barrier((du_3, qa_2, gpb, gpc))
    qa_s, qa_k = first(qa_k + [qa_2])
    qa_3 = flip(qa_s, 4)
    gpc_ = tie(gpc, qa_s)
    du_2 = give(total([du_s[1], du_3[0]]), 1)
    qb_t, qb_m = grad_q((gpb, gpc_), jnp.concatenate([gbb, gbc], axis=0))
    qb_1 = flip(qb_t, 1)
    qa_3, du_2, qb_t, qb_m = lax.optimization_barrier((qa_3, du_2, qb_t, qb_m))
    du = rest(total([du_s[0], du_2, du_3[1]]))
    du_x, du_y = flip(du, 2), flip(du, 4)
    qa_s = [total([t[j] for t in qa_k + [qa_3]]) for j in range(2)]
    q_3 = [give(qa_s[0], 1), give(qa_s[1], 2)]
    g1 = tie(g1, (qb_t, qa_s, du))
    x_grad = input_grad([gpb, gpa, gpc], wt0, wt1, g1, 0, C // 768)
    qb_1, qb_m, q_3, x_grad = lax.optimization_barrier((qb_1, qb_m, q_3, x_grad))
    qb_s = [total([t[i // 2, i % 2] for t in (qb_m, qb_1)]) for i in range(1, 4)]
    qb_k = [t[0, 0] for t in (qb_m, qb_1)]
    qb_2 = [flip(x, rel) for x, rel in zip(qb_s, SWAP[1:])]
    g1, x_grad = tie((g1, x_grad), qb_s)
    x_grad = input_grad([gpb, gpa, gpc], wt0, wt1, g1, C // 768, C // 256 - C // 768, x_grad)
    qb_2, du_x, du_y, x_grad = lax.optimization_barrier((qb_2, du_x, du_y, x_grad))
    cut_at = du.shape[0] // 16 * 8
    du_d = [flip(du_y[:cut_at], 2), flip(du_x[cut_at:], 4)]
    qb = total(qb_k + qb_2)
    q_3.append(give(qb[1], J - 1))
    q_3, du_d = lax.optimization_barrier((q_3, du_d))
    du = jnp.stack([du, du_x, du_y, jnp.concatenate(du_d, axis=0)])
    du_5 = flip(du, 1)
    q = rest(total([qb[0]] + q_3))
    q_4 = [flip(q, rel) for rel in NEAR[1:]]
    du_5, du, q = lax.optimization_barrier((du_5, du, q))
    down_g, up_g, ow_g, small = final(
        final_du_kernel, meta, (du, du_5), [(F, D), (D, F), (G * HD, D), (8, D)], [(SPLIT, rows, F), (SPLIT, rows, G * HD)], "final_du")
    q_4, q, down_g = lax.optimization_barrier((q_4, q, down_g))
    q = jnp.stack([q] + q_4)
    q_5 = flip(q, 1)
    qkv_g, gb = final(final_q_kernel, meta, (q, q_5), [(N, D), (1, N)], [(SPLIT, rows, N)], "final_q")
    return (
        out[None], x_grad[None], qkv_g.reshape(3, G * HD, D).transpose(2, 0, 1), gb.reshape(3, G * HD), ow_g, small[5], small[3], small[4],
        up_g, small[6], down_g, small[2], small[0], small[1],
    )


def solution(mesh):
    rows = P(("wide", "narrow"), None, None)
    weights = (P(None, None, "narrow"), P(None, "narrow"), P("narrow", None), P(), P(), P(),
               P(None, "narrow"), P("narrow"), P("narrow", None), P(), P(), P())
    return jax.shard_map(
        shards, mesh=mesh, in_specs=(rows, P("wide", None)) + weights + (rows,),
        out_specs=(rows, rows) + weights, check_vma=False,
    )
```

```python
import functools

import jax
import jax.numpy as jnp
from jax import lax
from jax.experimental import pallas as pl
from jax.experimental.pallas import tpu as pltpu
from jax.sharding import PartitionSpec as P

bf = jnp.bfloat16
f32 = jnp.float32
LOG2E = 1.4426950408889634
HEADS = 12
HD = 64
SPLIT = 8
EXTRA = 8
MIB = 1 << 20


def dg(a, b, ca, cb):
    return lax.dot_general(a, b, (((ca,), (cb,)), ((), ())), preferred_element_type=f32)


def mean(x):
    return jnp.mean(x, axis=-1, keepdims=True)


def shape(s, d):
    return jax.ShapeDtypeStruct(s, d)


SMEM = pl.BlockSpec(memory_space=pltpu.SMEM)
ANY = pl.BlockSpec(memory_space=pl.ANY)


def length_of(lengths):
    return lengths[0, lax.axis_index("narrow")]


def low_bits():
    return jnp.bitwise_and(lax.axis_index("wide"), SPLIT - 1)


def params(mib):
    return pltpu.CompilerParams(vmem_limit_bytes=mib * MIB)


def cost(flops, nbytes):
    return pl.CostEstimate(flops=1, bytes_accessed=1, transcendentals=0)


def put_piece(meta, src, g, lanes, place, dst, sem):
    rel, half, whole = place
    rows = src.shape[1]
    at = 0 if rel is None else (low_bits() ^ rel) * whole + half
    return pltpu.make_async_copy(src.at[g, :, lanes], dst.at[pl.ds(pl.multiple_of(at, 16), rows), :], sem)


def attn_fwd_kernel(meta, *refs, C, KC, G, layout, own):
    pieces, refs = refs[:len(layout)], refs[len(layout):]
    x, b, cos, sin, q_t, k_t, v_d, e, ctx, exact, linv, w_t, *rest = refs
    if own:
        x_t, Q2, KD, VA, S, W, flag, sem = rest
    else:
        x_t, (Q2, KD, VA, S, W, flag, sem) = x, rest
    h = pl.program_id(0)
    length = length_of(meta)

    if own:
        @pl.when(h == 0)
        def _():
            x_t[...] = x[...].T
            n = pieces[0].shape[0]
            w_t[:n, :] = pieces[0][...]
            w_t[n:, :] = pieces[1][...]
    else:
        groups = pieces[0].shape[0]

        def copies(g):
            return [put_piece(meta, pieces[t], g, slice(None), layout[t], W.at[g], sem.at[g, t]) for t in range(len(pieces))]

        @pl.when(h == 0)
        def _():
            for g in range(groups):
                for c in copies(g):
                    c.start()

        @pl.when(lax.rem(h, G) == 0)
        def _():
            g = lax.div(h, G)
            for c in copies(g):
                c.wait()
            w_t[...] = W[g].T

    at = lax.rem(h, G)
    w = jnp.concatenate([w_t[pl.ds(pl.multiple_of((p * G + at) * HD, HD), HD), :] for p in range(3)], axis=0)
    bias = [jnp.broadcast_to(b[i:i + 1, :], (2 * HD, HD)).T[:, :1] for i in range(3)]
    p = dg(w, x_t[...], 1, 0) + jnp.concatenate(bias, axis=0)
    c, d = cos[...], sin[...]

    def rot(v):
        u, z = v[:HD // 2], v[HD // 2:]
        return jnp.concatenate([u * c - z * d, z * c + u * d], axis=0)

    live = lax.broadcasted_iota(jnp.int32, (HD, C), 1) < length
    q = rot(p[:HD]).astype(bf).astype(f32)
    k = jnp.where(live, rot(p[HD:2 * HD]), 0.0).astype(bf)
    v = jnp.where(live, p[2 * HD:], 0.0).astype(bf)
    q_t[...] = (q * 0.125).astype(bf)
    q = q * (0.125 * LOG2E)
    hi = q.astype(bf)
    Q2[:HD, :] = hi
    Q2[HD:, :] = (q - hi.astype(f32)).astype(bf)
    k_t[...] = k
    KD[...] = jnp.concatenate([k, k], axis=0).T
    v_d[...] = jnp.concatenate([v, v], axis=0).T
    VA[:HD, :] = v
    VA[HD:, :] = jnp.where(live[:16], 1.0, 0.0).astype(bf)
    kf = k.astype(f32)
    qn = jnp.max(jnp.sum(q * q, axis=0, keepdims=True))
    kn = jnp.max(jnp.sum(kf * kf, axis=0, keepdims=True))
    flag[0] = (qn * kn <= 1e4).astype(jnp.int32)

    @pl.when(flag[0] == 1)
    def _():
        for j in range(C // KC):
            r = slice(j * KC, (j + 1) * KC)
            e[r, :] = jnp.exp2(dg(KD[r, :], Q2[...], 1, 0)).astype(bf)

    @pl.when(flag[0] == 0)
    def _():
        BQ = S.shape[1]

        def block(i, carry):
            cols = pl.ds(pl.multiple_of(i * BQ, BQ), BQ)

            def score(j, m):
                r = pl.ds(pl.multiple_of(j * KC, KC), KC)
                keys = lax.broadcasted_iota(jnp.int32, (KC, BQ), 0) + j * KC
                x = jnp.where(keys < length, dg(KD[r, :], Q2[:, cols], 1, 0), -1e30)
                S[r, :] = x
                return jnp.maximum(m, jnp.max(x, axis=0, keepdims=True))

            m = lax.fori_loop(0, C // KC, score, jnp.full((1, BQ), -1e30, f32))

            def power(j, carry):
                r = pl.ds(pl.multiple_of(j * KC, KC), KC)
                e[r, cols] = jnp.exp2(S[r, :] - m).astype(bf)
                return carry

            return lax.fori_loop(0, C // KC, power, carry)

        lax.fori_loop(0, C // BQ, block, 0)

    o = dg(VA[...], e[...], 1, 0)
    inv = 1.0 / o[HD:HD + 1]
    linv[...] = inv
    o = o[:HD] * inv
    exact[...] = o
    ctx[...] = o.astype(bf)


def attn_fwd(meta, pieces, layout, x, b, cos, sin, own):
    groups, _, D = pieces[0].shape if not own else (1,) + pieces[0].shape
    C = x.shape[0] if own else x.shape[1]
    G = b.shape[1]
    H = groups * G
    at = lambda h: (h, 0, 0)
    fix = lambda a: pl.BlockSpec(a.shape, lambda h: (0,) * a.ndim, pipeline_mode=pl.Buffered(1))
    hb = pl.BlockSpec((None, HD, C), at)
    out_specs = [hb, hb, pl.BlockSpec((None, C, 2 * HD), at), pl.BlockSpec((None, C, C), at), hb, hb,
                 pl.BlockSpec((None, 1, C), at), pl.BlockSpec((None, D, D), lambda h: (h // G, 0, 0))]
    out_shape = [shape((H, HD, C), bf), shape((H, HD, C), bf), shape((H, C, 2 * HD), bf), shape((H, C, C), bf),
                 shape((H, HD, C), bf), shape((H, HD, C), f32), shape((H, 1, C), f32), shape((groups, D, D), bf)]
    if own:
        out_specs.append(pl.BlockSpec((D, C), lambda h: (0, 0)))
        out_shape.append(shape((D, C), bf))
    return pl.pallas_call(
        functools.partial(attn_fwd_kernel, C=C, KC=min(128, C), G=G, layout=layout, own=own), grid=(H,),
        in_specs=[SMEM] + ([fix(p) for p in pieces] if own else [ANY] * len(pieces))
        + [fix(x), pl.BlockSpec((None, None, 3, HD), lambda h: (h // G, h % G, 0, 0)), fix(cos), fix(sin)],
        out_specs=out_specs, out_shape=out_shape,
        scratch_shapes=[pltpu.VMEM((2 * HD, C), bf), pltpu.VMEM((C, 2 * HD), bf), pltpu.VMEM((HD + 16, C), bf),
                        pltpu.VMEM((C, C // 3 if C % 384 == 0 else C), f32), pltpu.VMEM((8, 128) if own else (groups, D, D), bf),
                        pltpu.SMEM((1,), jnp.int32), pltpu.SemaphoreType.DMA((groups, len(pieces)))],
        compiler_params=params(60), cost_estimate=cost(H * (4 * C * C * 256 + 2 * C * D * 3 * HD), H * C * C * 2 + 8 * MIB),
        name="attn_fwd_own" if own else "attn_fwd",
    )(meta, *pieces, x, b, cos, sin)


def ffn_kernel(meta, u_own, d_own, *refs, R, layout):
    pieces, refs = refs[:len(layout)], refs[len(layout):]
    tok, cot, *refs = refs
    J = pieces[0].shape[0] + 1
    ctxs, ows, refs = refs[:2], refs[2:4], refs[4:]
    (vec, ub, out, act, gu, hid_t, gl_t, g1_o, gol_t, do_t, small, ubg, G, U, Dn, sem) = refs
    i = pl.program_id(0)
    groups = J - 1

    def copies():
        cs = [pltpu.make_async_copy(u_own, U.at[0], sem.at[0, 0, 0]), pltpu.make_async_copy(d_own, Dn.at[0], sem.at[1, 0, 0])]
        for g in range(groups):
            for t, (piece, (parts, place)) in enumerate(zip(pieces, layout)):
                for k, s in enumerate(parts):
                    lanes = slice(k * U.shape[2], (k + 1) * U.shape[2])
                    cs.append(put_piece(meta, piece, g, lanes, place, (U, Dn)[s].at[g + 1], sem.at[s, g + 1, t]))
        return cs

    @pl.when(i == 0)
    def _():
        for c in copies():
            c.start()
        small[...] = jnp.zeros_like(small)
        ubg[...] = jnp.zeros_like(ubg)

    ob, g1, s1, db, g2, s2 = [vec[k:k + 1, :] for k in range(6)]
    D = tok.shape[1]
    F = U.shape[2]

    def csum(k, x):
        small[k:k + 1, :] += jnp.sum(x, axis=0, keepdims=True)

    ow = jnp.concatenate([w[g] for w in ows for g in range(w.shape[0])], axis=0)
    ctx = jnp.concatenate([c[...].reshape(-1, R) for c in ctxs], axis=0)
    pre = tok[...].astype(f32) + dg(ctx.T, ow, 1, 0) + ob
    cen = pre - mean(pre)
    r1 = lax.rsqrt(mean(cen * cen) + 1e-6)
    n1 = cen * r1
    hid = n1 * g1 + s1
    hl = hid.astype(bf)
    hid_t[...] = hl.T
    acc = hid + db

    @pl.when(i == 0)
    def _():
        for c in copies():
            c.wait()

    for j in range(J):
        u = dg(hl, U[j], 1, 0) + ub[j:j + 1, :]
        phi = 0.5 * lax.erf(u * 0.7071067811865476) + 0.5
        a = (u * phi).astype(bf)
        act[:, j * F:(j + 1) * F] = a
        G[:, j * F:(j + 1) * F] = phi + u * (jnp.exp2(u * u * -0.7213475204444817) * 0.3989422804014327)
        acc = acc + dg(a, Dn[j], 1, 0)
    cen = acc - mean(acc)
    r2 = lax.rsqrt(mean(cen * cen) + 1e-6)
    n2 = cen * r2
    out[...] = (n2 * g2 + s2).astype(bf)
    c = cot[...].astype(f32)
    csum(0, c * n2)
    csum(1, c)
    sg = c * g2
    gt = r2 * (sg - mean(sg) - n2 * mean(sg * n2))
    csum(2, gt)
    gl = gt.astype(bf)
    gl_t[...] = gl.T
    dh = gt
    for j in range(J):
        g = dg(gl, Dn[j], 1, 1) * G[:, j * F:(j + 1) * F]
        ubg[j:j + 1, :] += jnp.sum(g, axis=0, keepdims=True)
        gb = g.astype(bf)
        gu[:, j * F:(j + 1) * F] = gb
        dh = dh + dg(gb, U[j], 1, 1)
    csum(3, dh * n1)
    csum(4, dh)
    sg = dh * g1
    go = r1 * (sg - mean(sg) - n1 * mean(sg * n1))
    csum(5, go)
    g1_o[...] = go
    gol = go.astype(bf)
    gol_t[...] = gol.T
    do_t[...] = dg(ow, gol, 1, 1).astype(bf).reshape(do_t.shape)


def ffn(meta, u_own, d_own, pieces, layout, tok, cot, ctxs, wts, vec, ub, R=512):
    C, D = tok.shape
    J, F = ub.shape
    H = HEADS
    row = lambda w: pl.BlockSpec((R, w), lambda i: (i, 0))
    col = pl.BlockSpec((D, R), lambda i: (0, i))
    fix = lambda a: pl.BlockSpec(a.shape, lambda i: (0,) * a.ndim, pipeline_mode=pl.Buffered(1))
    hb = lambda n: pl.BlockSpec((n, HD, R), lambda i: (0, 0, i))
    acc = lambda s: pl.BlockSpec(s, lambda i: (0, 0))
    share = H // J * HD
    at = 3
    owb = lambda w: pl.BlockSpec((w.shape[0], share, D), lambda i: (0, at, 0), pipeline_mode=pl.Buffered(1))
    return pl.pallas_call(
        functools.partial(ffn_kernel, R=R, layout=layout), grid=(C // R,),
        in_specs=[SMEM, ANY, ANY] + [ANY] * len(pieces) + [row(D), row(D)] + [hb(c.shape[0]) for c in ctxs] + [owb(w) for w in wts] + [fix(vec), fix(ub)],
        out_specs=[row(D), row(J * F), row(J * F), col, col, row(D), col, hb(H), acc((8, D)), acc((J, F))],
        out_shape=[shape((C, D), bf), shape((C, J * F), bf), shape((C, J * F), bf), shape((D, C), bf), shape((D, C), bf), shape((C, D), f32),
                   shape((D, C), bf), shape((H, HD, C), bf), shape((8, D), f32), shape((J, F), f32)],
        scratch_shapes=[pltpu.VMEM((R, J * F), f32), pltpu.VMEM((J, D, F), bf), pltpu.VMEM((J, F, D), bf),
                        pltpu.SemaphoreType.DMA((2, J, len(pieces)))],
        compiler_params=params(60), cost_estimate=cost(2 * C * D * (2 * D + 4 * J * F), 60 * MIB), name="ffn",
    )(meta, u_own, d_own, *pieces, tok, cot, *ctxs, *wts, vec, ub)


def attn_bwd_kernel(meta, e, v_d, do_t, ctx, linv, q_t, k_t, cos, sin, gp, gb, D2, DI, DS, DST, ET, *, C, KC):
    length = length_of(meta)
    g = do_t[...].astype(f32)
    inv = linv[...]
    DI[...] = jnp.sum(g * ctx[...], axis=0, keepdims=True) * inv
    g = g * inv
    hi = g.astype(bf)
    D2[:HD, :] = hi
    D2[HD:, :] = (g - hi.astype(f32)).astype(bf)
    for j in range(C // KC):
        r = slice(j * KC, (j + 1) * KC)
        dp = dg(v_d[r, :], D2[...], 1, 0)
        ej = e[r, :]
        ds = (ej.astype(f32) * (dp - DI[...])).astype(bf)
        DS[r, :] = ds
        DST[:, r] = ds.T
        ET[:, r] = ej.T
    dq = dg(k_t[...], DS[...], 1, 0)
    dk = dg(q_t[...], DST[...], 1, 0)
    dv = dg(D2[:HD, :], ET[...], 1, 0)
    live = lax.broadcasted_iota(jnp.int32, (HD, C), 1) < length
    c, s = cos[...], sin[...]

    def unrot(x):
        u, w = x[:HD // 2], x[HD // 2:]
        return jnp.concatenate([u * c + w * s, w * c - u * s], axis=0)

    def put(k, x):
        gp[k] = x.astype(bf)
        total = jnp.sum(x, axis=1, keepdims=True)
        gb[k:k + 1, :] = jnp.broadcast_to(total, (HD, 2 * HD)).T[:1]

    put(0, unrot(dq * 0.125))
    put(1, unrot(jnp.where(live, dk, 0.0)))
    put(2, jnp.where(live, dv, 0.0))


def attn_bwd(meta, saved, do_t, cos, sin, G, first, shift, H):
    e, v_d, ctx, linv, q_t, k_t = saved
    C = e.shape[1]
    sp = lambda s: pl.BlockSpec((None,) + s, lambda h: (h + first, 0, 0))
    tab = pl.BlockSpec((HD // 2, C), lambda h: (0, 0))
    return pl.pallas_call(
        functools.partial(attn_bwd_kernel, C=C, KC=min(256, C)), grid=(H,),
        in_specs=[SMEM, sp((C, C)), sp((C, 2 * HD)), pl.BlockSpec((None, HD, C), lambda h: (h + first + shift, 0, 0)), sp((HD, C)), sp((1, C)),
                  sp((HD, C)), sp((HD, C)), tab, tab],
        out_specs=[pl.BlockSpec((None, 3, None, HD, C), lambda h: (h // G, 0, h % G, 0, 0)), pl.BlockSpec((None, 3, HD), lambda h: (h, 0, 0))],
        out_shape=[shape((H // G, 3, G, HD, C), bf), shape((H, 3, HD), f32)],
        scratch_shapes=[pltpu.VMEM((2 * HD, C), bf), pltpu.VMEM((1, C), f32)] + [pltpu.VMEM((C, C), bf)] * 3,
        compiler_params=params(60), cost_estimate=cost(H * 8 * C * C * 256, H * C * C * 2 + 16 * MIB), name="attn_bwd",
    )(meta, e, v_d, do_t, ctx, linv, q_t, k_t, cos, sin)


NEAR = (0, 2, 4, 6)
SWAP = (0, 4, 2, 6)


def lay(meta, S, theirs, mine, rows, lanes, order):
    for i, rel in enumerate(order):
        for ref, low in ((mine, 0), (theirs, 1)):
            ref[i // 2, i % 2, 0, rows, lanes] = S[low_bits() ^ (rel | low)].astype(bf)


def wgrad_d_kernel(meta, gl_t, act, vecs, theirs, mine, S):
    rows = S.shape[1]
    S[...] = dg(gl_t[...], act[...], 1, 0).reshape(S.shape)
    lay(meta, S, theirs, mine, slice(0, rows), slice(None), SWAP)
    for i, rel in enumerate(SWAP):
        for ref, low in ((mine, 0), (theirs, 1)):
            line = vecs[pl.ds(low_bits() ^ (rel | low), 1), :]
            ref[i // 2, i % 2, 0, rows:, :] = jnp.broadcast_to(line, (EXTRA, line.shape[1])).astype(bf)


def wgrad_u_kernel(meta, hid_t, gu, gol_t, *refs):
    c0, c1, theirs, mine, S, SO = refs
    F = gu.shape[1]
    S[...] = dg(hid_t[...], gu[...], 1, 0).reshape(S.shape)
    lay(meta, S, theirs, mine, slice(None), slice(0, F), NEAR)

    def out(ctx):
        SO[...] = dg(gol_t[...], ctx[...].reshape(-1, ctx.shape[-1]), 1, 1).reshape(SO.shape)

    pl.when(pl.program_id(0) == 0)(lambda: out(c0))
    pl.when(pl.program_id(0) > 0)(lambda: out(c1))
    lay(meta, SO, theirs, mine, slice(None), slice(F, F + SO.shape[2]), NEAR)


def wgrad_q_kernel(meta, tok_t, *refs):
    gps, (gb, theirs, mine, S) = refs[:-4], refs[-4:]
    rows = S.shape[1]
    if len(gps) == 1:
        S[...] = dg(tok_t[...], gps[0][...], 1, 1).reshape(S.shape)
    for j, gp in enumerate(gps if len(gps) > 1 else ()):
        @pl.when(pl.program_id(0) == j)
        def _(gp=gp):
            S[...] = dg(tok_t[...], gp[...], 1, 1).reshape(S.shape)

    lay(meta, S, theirs, mine, slice(0, rows), slice(None), SWAP)
    line = jnp.broadcast_to(gb[...], (EXTRA, gb.shape[1])).astype(bf)
    for i in range(4):
        for ref in (mine, theirs):
            ref[i // 2, i % 2, 0, rows:, :] = line


def wgrad(kernel, meta, args, specs, J, rows, lanes, scratch, name, flops):
    spec = pl.BlockSpec((2, 2, 1, rows, lanes), lambda j: (0, 0, j, 0, 0))
    return pl.pallas_call(
        kernel, grid=(J,), in_specs=[SMEM] + specs, out_specs=[spec] * 2, out_shape=[shape((2, 2, J, rows, lanes), bf)] * 2,
        scratch_shapes=[pltpu.VMEM(s, f32) for s in scratch],
        compiler_params=params(28), cost_estimate=cost(flops, 20 * MIB), name=name,
    )(meta, *[pltpu.with_memory_space_constraint(x, pltpu.HBM) for x in args])


def final_du_kernel(meta, x, y, down, up, ow, small, S, SO):
    rows = S.shape[1]
    F = up.shape[1]
    for low, ref in enumerate((x, y)):
        for t, rel in enumerate(NEAR):
            at = low_bits() ^ (rel | low)
            S[at] = ref[t, :rows, :F].astype(f32)
            small[pl.ds(at, 1), :] = ref[t, rows:rows + 1, :F].astype(f32)
            up[pl.ds(pl.multiple_of(at * rows, rows), rows), :] = ref[t, :rows, F:2 * F].astype(f32)
            SO[at] = ref[t, :rows, 2 * F:].astype(f32)
    down[...] = S[...].reshape(down.shape).T
    ow[...] = SO[...].reshape(-1, SO.shape[2]).T


def final_q_kernel(meta, x, y, qkv, gb, S):
    rows = x.shape[1] - EXTRA
    for low, ref in enumerate((x, y)):
        for t, rel in enumerate(NEAR):
            S[low_bits() ^ (rel | low)] = ref[t, :rows, :].astype(f32)
    qkv[...] = S[...].reshape(-1, S.shape[2]).T
    gb[...] = x[0, rows:rows + 1, :].astype(f32)


def final(kernel, meta, xs, outs, scratch, name):
    return pl.pallas_call(
        kernel, in_specs=[SMEM] + [pl.BlockSpec(memory_space=pltpu.VMEM)] * 2,
        out_shape=[shape(s, f32) for s in outs], scratch_shapes=[pltpu.VMEM(s, f32) for s in scratch],
        compiler_params=params(60), cost_estimate=cost(0, 8 * MIB), name=name,
    )(meta, *xs)


def input_grad_kernel(*refs, N, n):
    gps, (w0, w1, g1, *_, out) = refs[:n], refs[n:]
    acc = g1[...]
    j = 0
    for gp in gps:
        for i in range(gp.shape[0]):
            w = w0[0, :N, :] if j == 0 else w1[j - 1, :N, :]
            acc = acc + dg(gp[i], w, 0, 0)
            j += 1
    out[...] = acc


def input_grad(gps, w0, w1, g1, first, count, before=None, R=256):
    _, N, C = gps[0].shape
    D = g1.shape[1]
    fix = lambda a: pl.BlockSpec(a.shape, lambda i: (0,) * a.ndim, pipeline_mode=pl.Buffered(1))
    row = pl.BlockSpec((R, D), lambda i: (i + first, 0))
    more = [] if before is None else [before]
    return pl.pallas_call(
        functools.partial(input_grad_kernel, N=N, n=len(gps)), grid=(count,),
        in_specs=[pl.BlockSpec((g.shape[0], N, R), lambda i: (0, 0, i + first)) for g in gps] + [fix(w0), fix(w1), row] + [ANY] * len(more),
        out_specs=row, out_shape=shape((C, D), f32), input_output_aliases={len(gps) + 3: 0} if more else {},
        compiler_params=params(28), cost_estimate=cost(2 * C * D * D * 3, 24 * MIB), name="input_grad",
    )(*gps, w0, w1, g1, *more)


def fetch(x, s):
    n = lax.axis_size("narrow")
    return lax.ppermute(x, "narrow", [((i + s) % n, i) for i in range(n)])


def give(x, s):
    n = lax.axis_size("narrow")
    return lax.ppermute(x, "narrow", [(i, (i + s) % n) for i in range(n)])


def flip(x, bit):
    return lax.ppermute(x, "wide", [(i, i ^ bit) for i in range(lax.axis_size("wide"))])


def total(terms):
    x = terms[0].astype(f32)
    for y in terms[1:]:
        x = x + y.astype(f32)
    return x.astype(bf)


def rest(x):
    bit = SPLIT
    while bit < lax.axis_size("wide"):
        x = add(x, flip(x, bit))
        bit *= 2
    return x


def tie(xs, deps):
    return lax.optimization_barrier((xs, deps))[0]


def add(a, b):
    return (a.astype(f32) + b.astype(f32)).astype(bf)


def rotary_tables(capacity):
    positions = jnp.arange(capacity).astype(f32)
    frequencies = 10000.0 ** (-2.0 * jnp.arange(HD // 2).astype(f32) / HD)
    angles = frequencies[:, None] * positions[None, :]
    return jnp.cos(angles), jnp.sin(angles)


def shards(
    tokens, lengths, qkv_weight, qkv_bias, out_weight, out_bias, norm1_gain, norm1_shift,
    up_weight, up_bias, down_weight, down_bias, norm2_gain, norm2_shift, cotangent,
):
    J = lax.axis_size("narrow")
    tok, cot = tokens[0], cotangent[0]
    C, D = tok.shape
    G = HEADS // J
    N = 3 * G * HD
    F = up_weight.shape[1]
    rows = D // SPLIT
    low = jnp.bitwise_and(lax.axis_index("wide"), SPLIT - 1).astype(jnp.int32)
    meta = lengths
    cos, sin = rotary_tables(C)

    qkv_t = qkv_weight.transpose(1, 2, 0).reshape(N, D)
    qo = jnp.concatenate([qkv_weight.reshape(D, N), out_weight.T], axis=1)
    bias = jnp.concatenate([qkv_bias.reshape(-1), up_bias])
    bias = jnp.pad(bias, (0, 2 * D - bias.size)).reshape(2, D)
    cut = lambda x: lax.dynamic_slice_in_dim(x, low * rows, rows, 0)
    q_piece = jnp.concatenate([cut(qo), jnp.pad(bias, ((0, EXTRA - 2), (0, 0)))], axis=0)
    got = [fetch(q_piece, s) for s in range(1, J)]
    vec = jnp.stack([out_bias, norm1_gain, norm1_shift, down_bias, norm2_gain, norm2_shift]).astype(f32)
    b_own = qkv_bias.astype(f32).reshape(1, 3, G, HD).transpose(0, 2, 1, 3)
    ud_piece = jnp.concatenate([cut(up_weight), cut(down_weight)], axis=1)
    ud_got = [fetch(tie(ud_piece, q_piece), 1)]
    q0, k0, v0, e0, c0, o0, l0, wt0, tok_t = attn_fwd(meta, [qkv_t, out_weight], (0, 1), tok, b_own, cos, sin, True)
    got, ud_got, tok_t = lax.optimization_barrier((got, ud_got, tok_t))
    biases = jnp.stack([bias] + [x[rows:rows + 2] for x in got]).reshape(J, 2 * D).astype(f32)
    bq, ub = biases[1:, :N].reshape(J - 1, 3, G, HD).transpose(0, 2, 1, 3), biases[:, N:N + F]
    q = jnp.stack([x[:rows] for x in got])
    q_near = [flip(q, rel) for rel in NEAR[1:]]
    ud_2, ud_3 = fetch(ud_got[0], 1), fetch(tie(ud_piece, got), 3)
    q_near, ud_2, ud_3, bq, ub, vec = lax.optimization_barrier((q_near, ud_2, ud_3, bq, ub, vec))
    q_near = [q] + q_near
    q_far = [flip(x, 1) for x in q_near]
    q_places = tuple((rel | low, 0, rows) for low in (0, 1) for rel in NEAR)
    q_far, ud_2, ud_3 = lax.optimization_barrier((q_far, ud_2, ud_3))
    ud = jnp.stack(ud_got + [ud_2, ud_3])
    q_pieces = q_near + q_far
    ud_near = [flip(ud, rel) for rel in NEAR[1:]]
    ud_far = [flip(ud, 1)]
    tok_t = tie(tok_t, ud)
    q1, k1, v1, e1, c1, o1, l1, wt1 = attn_fwd(meta, q_pieces, q_places, tok_t, bq, cos, sin, False)
    ud_near, ud_far, c1 = lax.optimization_barrier((ud_near, ud_far, c1))
    ud_pieces = [ud] + ud_near + ud_far + [flip(x, 1) for x in ud_near]
    ud_places = [(rel | low, 0, rows) for low in (0, 1) for rel in NEAR]
    ud_layout = tuple(((0, 1), place) for place in ud_places)
    out, act, gu, hid_t, gl_t, g1, gol_t, do_t, small, ubg = ffn(
        meta, up_weight, down_weight, ud_pieces, ud_layout, tok, cot, (c0, c1), (wt0, wt1), vec, ub)

    whole = lambda a: pl.BlockSpec(a.shape, lambda j: (0,) * a.ndim, pipeline_mode=pl.Buffered(1))
    vecs = jnp.concatenate([jnp.broadcast_to(small[None, :6], (J, 6, D)), ubg[:, None], jnp.zeros((J, 1, D), f32)], axis=1)
    u_t, u_m = wgrad(
        wgrad_u_kernel, meta, (hid_t, gu, gol_t, c0, c1),
        [whole(hid_t), pl.BlockSpec((C, F), lambda j: (0, j)), whole(gol_t), pl.BlockSpec((G, HD, C), lambda j: (0, 0, 0)),
         pl.BlockSpec((G, HD, C), lambda j: (jnp.maximum(j - 1, 0), 0, 0))],
        J, rows, F + G * HD, [(SPLIT, rows, F), (SPLIT, rows, G * HD)], "wgrad_u", 2 * C * D * (J * F + D))
    u_1 = flip(u_t, 1)
    gl_t = tie(gl_t, u_t)
    d_t, d_m = wgrad(
        wgrad_d_kernel, meta, (gl_t, act, vecs),
        [whole(gl_t), pl.BlockSpec((C, F), lambda j: (0, j)), pl.BlockSpec((None, 8, D), lambda j: (j, 0, 0))],
        J, rows + EXTRA, F, [(SPLIT, rows, F)], "wgrad_d", 2 * C * D * J * F)

    def grad_q(gps, gb):
        n = gb.shape[0]
        one = pl.BlockSpec((None, N, C), lambda j: (j, 0, 0)) if len(gps) == 1 else pl.BlockSpec((None, N, C), lambda j: (0, 0, 0))
        return wgrad(
            wgrad_q_kernel, meta, (tok_t, *gps, gb), [whole(tok_t)] + [one] * len(gps) + [pl.BlockSpec((None, 1, N), lambda j: (j, 0, 0))],
            n, rows + EXTRA, N, [(SPLIT, rows, N)], "wgrad_q", 2 * C * D * n * N)

    def backward(group, count, do_t):
        saved, shift = ((e0, v0, o0, l0, q0, k0), 0) if group == 0 else ((e1, v1, o1, l1, q1, k1), G)
        gp, gb = attn_bwd(meta, saved, do_t, cos, sin, G, group * G - shift, shift, count * G)
        return gp.reshape(count, N, C), gb.reshape(count, G, 3, HD).transpose(0, 2, 1, 3).reshape(count, 1, N)

    def first(terms):
        return total([t[1] for t in terms]), [t[0] for t in terms]

    u_1, u_m, d_t = lax.optimization_barrier((u_1, u_m, d_t))
    d_1 = flip(d_t, 1)
    u_s, u_k = first([u_m, u_1])
    u_2 = flip(u_s, 4)
    do_t = tie(do_t, u_s)
    d_1, d_m, do_t = lax.optimization_barrier((d_1, d_m, do_t))
    d_s, d_k = first([d_m, d_1])
    d_2 = flip(d_s, 2)
    do_t = tie(do_t, d_s)
    gpa, gba = backward(1, 2, do_t)
    u_2, d_2, gpa, do_t = lax.optimization_barrier((u_2, d_2, gpa, do_t))
    u_s, u_k = first(u_k + [u_2])
    u_3 = flip(u_s, 2)
    d_s, d_k = first(d_k + [d_2])
    d_3 = flip(d_s, 4)
    gpa_ = tie(gpa, (u_s, d_s))
    qa_t, qa_m = grad_q((gpa_,), gba)
    qa_1 = flip(qa_t, 1)
    do_t = tie(do_t, qa_t)
    gpb, gbb = backward(0, 1, do_t)
    u_3, d_3, qa_1, gpb, do_t = lax.optimization_barrier((u_3, d_3, qa_1, gpb, do_t))
    du_s = [jnp.concatenate([total([t[j] for t in d_k + [d_3]]), jnp.pad(total([t[j] for t in u_k + [u_3]]), ((0, EXTRA), (0, 0)))], axis=1)
            for j in range(J)]
    du_3 = [give(du_s[2], 1), give(du_s[3], 3)]
    qa_s, qa_k = first([qa_m, qa_1])
    qa_2 = flip(qa_s, 2)
    do_t = tie(do_t, (du_s, qa_s))
    gpc, gbc = backward(3, 1, do_t)
    du_3, qa_2, gpb, gpc = lax.optimization_barrier((du_3, qa_2, gpb, gpc))
    qa_s, qa_k = first(qa_k + [qa_2])
    qa_3 = flip(qa_s, 4)
    gpc_ = tie(gpc, qa_s)
    du_2 = give(total([du_s[1], du_3[0]]), 1)
    qb_t, qb_m = grad_q((gpb, gpc_), jnp.concatenate([gbb, gbc], axis=0))
    qb_1 = flip(qb_t, 1)
    qa_3, du_2, qb_t, qb_m = lax.optimization_barrier((qa_3, du_2, qb_t, qb_m))
    du = rest(total([du_s[0], du_2, du_3[1]]))
    du_x, du_y = flip(du, 2), flip(du, 4)
    qa_s = [total([t[j] for t in qa_k + [qa_3]]) for j in range(2)]
    q_3 = [give(qa_s[0], 1), give(qa_s[1], 2)]
    g1 = tie(g1, (qb_t, qa_s, du))
    x_grad = input_grad([gpb, gpa, gpc], wt0, wt1, g1, 0, C // 768)
    qb_1, qb_m, q_3, x_grad = lax.optimization_barrier((qb_1, qb_m, q_3, x_grad))
    qb_s = [total([t[i // 2, i % 2] for t in (qb_m, qb_1)]) for i in range(1, 4)]
    qb_k = [t[0, 0] for t in (qb_m, qb_1)]
    qb_2 = [flip(x, rel) for x, rel in zip(qb_s, SWAP[1:])]
    g1, x_grad = tie((g1, x_grad), qb_s)
    x_grad = input_grad([gpb, gpa, gpc], wt0, wt1, g1, C // 768, C // 256 - C // 768, x_grad)
    qb_2, du_x, du_y, x_grad = lax.optimization_barrier((qb_2, du_x, du_y, x_grad))
    cut_at = du.shape[0] // 16 * 8
    du_d = [flip(du_y[:cut_at], 2), flip(du_x[cut_at:], 4)]
    qb = total(qb_k + qb_2)
    q_3.append(give(qb[1], J - 1))
    q_3, du_d = lax.optimization_barrier((q_3, du_d))
    du = jnp.stack([du, du_x, du_y, jnp.concatenate(du_d, axis=0)])
    du_5 = flip(du, 1)
    q = rest(total([qb[0]] + q_3))
    q_4 = [flip(q, rel) for rel in NEAR[1:]]
    du_5, du, q = lax.optimization_barrier((du_5, du, q))
    down_g, up_g, ow_g, small = final(
        final_du_kernel, meta, (du, du_5), [(F, D), (D, F), (G * HD, D), (8, D)], [(SPLIT, rows, F), (SPLIT, rows, G * HD)], "final_du")
    q_4, q, down_g = lax.optimization_barrier((q_4, q, down_g))
    q = jnp.stack([q] + q_4)
    q_5 = flip(q, 1)
    qkv_g, gb = final(final_q_kernel, meta, (q, q_5), [(N, D), (1, N)], [(SPLIT, rows, N)], "final_q")
    return (
        out[None], x_grad[None], qkv_g.reshape(3, G * HD, D).transpose(2, 0, 1), gb.reshape(3, G * HD), ow_g, small[5], small[3], small[4],
        up_g, small[6], down_g, small[2], small[0], small[1],
    )


def solution(mesh):
    rows = P(("wide", "narrow"), None, None)
    weights = (P(None, None, "narrow"), P(None, "narrow"), P("narrow", None), P(), P(), P(),
               P(None, "narrow"), P("narrow"), P("narrow", None), P(), P(), P())
    return jax.shard_map(
        shards, mesh=mesh, in_specs=(rows, P("wide", None)) + weights + (rows,),
        out_specs=(rows, rows) + weights, check_vma=False,
    )
```
